32 devices in a mesh: dp: 4 (over z), fsdp: 8 (over y, x, core).
Axes of the slice: x: 2, y: 2, z: 4, core: 2. Of those that a mesh axis runs over, the one named last changes fastest.
Arguments:
- hidden_in: float32 [32768, 768], P(('dp', 'fsdp')), may hold values from -6 to 6
- time_embed: float32 [512, 768], P(('dp', 'fsdp')), may hold values from -6 to 6
- seg_ids: int32 [32768], P(('dp', 'fsdp')), may hold values from -1 to 15, as said below
- pre_gain: float32 [768], P(('dp', 'fsdp')), may hold values from 0.5 to 1.5
- pre_shift: float32 [768], P(('dp', 'fsdp')), may hold values from -3 to 3
- qkv_weight: float32 [768, 2304], P(('dp', 'fsdp')), may hold values from -0.21875 to 0.21875
- qv_bias: float32 [1536], P(('dp', 'fsdp')), may hold values from -3 to 3
- out_weight: float32 [768, 768], P(('dp', 'fsdp')), may hold values from -0.625 to 0.625
- out_bias: float32 [768], P(('dp', 'fsdp')), may hold values from -3 to 3
- mid_gain: float32 [768], P(('dp', 'fsdp')), may hold values from 0.5 to 1.5
- mid_shift: float32 [768], P(('dp', 'fsdp')), may hold values from -3 to 3
- in_weight: float32 [768, 3072], P(('dp', 'fsdp')), may hold values from -0.21875 to 0.21875
- in_bias: float32 [3072], P(('dp', 'fsdp')), may hold values from -3 to 3
- down_weight: float32 [3072, 768], P(('dp', 'fsdp')), may hold values from -0.109375 to 0.109375
- down_bias: float32 [768], P(('dp', 'fsdp')), may hold values from -3 to 3
- grad_out: float32 [32768, 768], P(('dp', 'fsdp')), may hold values from -6 to 6
Outputs:
- block_out: float32 [32768, 768], P(('dp', 'fsdp'))
- input_grad: float32 [32768, 768], P(('dp', 'fsdp'))
- time_grad: float32 [512, 768], P(('dp', 'fsdp'))
- grad_pre_gain: float32 [768], P(('dp', 'fsdp'))
- grad_pre_shift: float32 [768], P(('dp', 'fsdp'))
- grad_qkv_weight: float32 [768, 2304], P(('dp', 'fsdp'))
- grad_qv_bias: float32 [1536], P(('dp', 'fsdp'))
- grad_out_weight: float32 [768, 768], P(('dp', 'fsdp'))
- grad_out_bias: float32 [768], P(('dp', 'fsdp'))
- grad_mid_gain: float32 [768], P(('dp', 'fsdp'))
- grad_mid_shift: float32 [768], P(('dp', 'fsdp'))
- grad_in_weight: float32 [768, 3072], P(('dp', 'fsdp'))
- grad_in_bias: float32 [3072], P(('dp', 'fsdp'))
- grad_down_weight: float32 [3072, 768], P(('dp', 'fsdp'))
- grad_down_bias: float32 [768], P(('dp', 'fsdp'))
The draws below stay inside these ranges and needn't reach their ends.
Inputs may be any that keep to these rules, and one draw needn't show every extreme that they name: Within each block of 1024 tokens, either every token has seg_ids 0 (one item of 1024 tokens), or items of 64 tokens numbered 0, 1, 2, ... follow one another from the block's start and the rest of the block is padding with -1. Some block of every draw is one whole item and some other block is filled with short items.
All inputs are finite; a program needn't handle non-finite values.
Results may differ from the reference program's by a relative error of at most 0.011.
Values may be sent and summed in bfloat16 or wider, within the bound.
A program may use at most 256 MiB of HBM per device.

```python
import jax
import jax.numpy as jnp
from jax import lax

D = 768
HEADS = 12
HEAD_DIM = 64
FF = 3072
BLOCK = 1024
SHORT = 64
ITEMS_DEV = 16
TOKENS = 32768
ITEMS = 512


def draw_seg_ids(key, part):
    blocks = TOKENS // BLOCK
    first_key, second_key, third_key, fourth_key = jax.random.split(jax.random.fold_in(key, 11), 4)
    single = jax.random.randint(first_key, (blocks,), 0, 4) == 0
    forced_long = jax.random.randint(second_key, (), 0, blocks)
    forced_full = (forced_long + 1 + jax.random.randint(fourth_key, (), 0, blocks - 1)) % blocks
    index_blocks = jnp.arange(blocks, dtype=jnp.int32)
    single = (single | (index_blocks == forced_long)) & (index_blocks != forced_full)
    counts = jax.random.randint(third_key, (blocks,), ITEMS_DEV * 3 // 4, ITEMS_DEV + 1)
    counts = jnp.where(index_blocks == forced_full, ITEMS_DEV, counts)
    short_ids = jnp.arange(BLOCK, dtype=jnp.int32) // SHORT
    packed = jnp.where(short_ids[None, :] < counts[:, None], short_ids[None, :], -1)
    result = jnp.where(single[:, None], 0, packed)
    return result.reshape(-1).astype(jnp.int32)


def level_of(own_key, dims, cuts, smallest, top_value):
    loudness, own = 1.0, jax.random.fold_in(own_key, 6)
    for axis_at, shards_of in cuts:
        heights = jnp.exp(jax.random.uniform(jax.random.fold_in(own, axis_at), (shards_of,), jnp.float32, smallest / len(cuts), top_value / len(cuts)))
        loudness = loudness * jnp.repeat(heights, dims[axis_at] // shards_of).reshape([-1 if axis == axis_at else 1 for axis in range(len(dims))])
    return loudness


def normal_values(key, dims, scale, reach, cuts=(), kind=jnp.bfloat16):
    array = scale * jax.random.normal(key, dims, jnp.float32)
    if cuts:
        array = array * level_of(key, dims, cuts, -0.22, 0.18)
    return jnp.clip(array, -reach, reach).astype(kind)


def setup_inputs(seed: int = 0) -> dict:
    splits = jax.random.split(jax.random.key(seed), 17)
    hidden_in = normal_values(splits[0], (TOKENS, D), 1.0, 6.0, ((0, 32),), jnp.float32)
    time_embed = normal_values(splits[1], (ITEMS, D), 1.0, 6.0, ((0, 32),), jnp.float32)
    seg_ids = draw_seg_ids(jax.random.fold_in(splits[16], 71), 0)
    pre_gain = jnp.clip(1.0 + 0.1 * jax.random.normal(splits[3], (D,), jnp.float32), 0.5, 1.5)
    pre_shift = normal_values(splits[4], (D,), 0.5, 3.0, ((0, 32),), jnp.float32)
    qkv_weight = normal_values(splits[5], (D, 3 * D), D ** -0.5, 0.21875, ((0, 32),), jnp.float32)
    qv_bias = normal_values(splits[6], (2 * D,), 0.5, 3.0, ((0, 32),), jnp.float32)
    out_weight = normal_values(splits[7], (D, D), (D // 8) ** -0.5, 0.625, ((0, 32),), jnp.float32)
    out_bias = normal_values(splits[8], (D,), 0.5, 3.0, ((0, 32),), jnp.float32)
    mid_gain = jnp.clip(1.0 + 0.1 * jax.random.normal(splits[9], (D,), jnp.float32), 0.5, 1.5)
    mid_shift = normal_values(splits[10], (D,), 0.5, 3.0, ((0, 32),), jnp.float32)
    in_weight = normal_values(splits[11], (D, FF), D ** -0.5, 0.21875, ((0, 32),), jnp.float32)
    in_bias = normal_values(splits[12], (FF,), 0.5, 3.0, ((0, 32),), jnp.float32)
    down_weight = normal_values(splits[13], (FF, D), FF ** -0.5, 0.109375, ((0, 32),), jnp.float32)
    down_bias = normal_values(splits[14], (D,), 0.5, 3.0, ((0, 32),), jnp.float32)
    grad_out = normal_values(splits[15], (TOKENS, D), 1.0, 6.0, ((0, 32),), jnp.float32)
    return {"hidden_in": hidden_in, "time_embed": time_embed, "seg_ids": seg_ids, "pre_gain": pre_gain, "pre_shift": pre_shift, "qkv_weight": qkv_weight, "qv_bias": qv_bias, "out_weight": out_weight, "out_bias": out_bias, "mid_gain": mid_gain, "mid_shift": mid_shift, "in_weight": in_weight, "in_bias": in_bias, "down_weight": down_weight, "down_bias": down_bias, "grad_out": grad_out}


@jax.custom_vjp
def low(v):
    return lax.optimization_barrier(v.astype(jnp.bfloat16)).astype(jnp.float32)

@jax.custom_vjp
def low_back(v):
    return v

def low_keep(v):
    return (low(v), None)

def low_pass(kept, grad):
    return (grad,)

def back_keep(v):
    return (v, None)

def back_low(kept, grad):
    return (low(grad),)
low.defvjp(low_keep, low_pass)
low_back.defvjp(back_keep, back_low)

def layer_norm(v, gain_vec, shift_vec):
    center = v - lax.optimization_barrier(jnp.mean(v, axis=-1, keepdims=True))
    spread = lax.optimization_barrier(jnp.mean(center * center, axis=-1, keepdims=True))
    return center * lax.rsqrt(spread + 1e-05) * gain_vec + shift_vec

def block_forward(params, hidden, time_rows, segment):
    pre_gain, pre_shift, qkv_weight, qv_bias, out_weight, out_bias, mid_gain, mid_shift, in_weight, in_bias, down_weight, down_bias = tuple((low(p) for p in params))
    row_count = hidden.shape[0]
    onehot = (segment[:, None] == jnp.arange(ITEMS_DEV, dtype=jnp.int32)[None, :]).astype(jnp.float32)
    live_mask = (segment >= 0).astype(jnp.float32)[:, None]
    x = (hidden + jnp.dot(onehot, time_rows, precision=lax.Precision.HIGHEST)) * live_mask
    normed = low(layer_norm(x, pre_gain, pre_shift))
    bias_full = jnp.concatenate([qv_bias[:D], jnp.zeros((D,), jnp.float32), qv_bias[D:]])
    projected = low(low_back(jnp.dot(normed, qkv_weight, precision=lax.Precision.HIGHEST) + bias_full))
    q = projected[:, :D].reshape(row_count, HEADS, HEAD_DIM)
    k = projected[:, D:2 * D].reshape(row_count, HEADS, HEAD_DIM)
    v = projected[:, 2 * D:].reshape(row_count, HEADS, HEAD_DIM)
    scores = jnp.einsum('qhd,khd->hqk', q, k, precision=lax.Precision.HIGHEST) * HEAD_DIM ** (-0.5)
    allowed = (segment[:, None] == segment[None, :]) & (segment[None, :] >= 0)
    scores = low_back(jnp.where(allowed[None], scores, -1e+30))
    row_max = lax.optimization_barrier(jnp.max(scores, axis=-1, keepdims=True))
    exp_terms = jnp.exp(scores - row_max)
    p = low(exp_terms / lax.optimization_barrier(jnp.sum(exp_terms, axis=-1, keepdims=True)))
    attended = jnp.einsum('hqk,khd->qhd', p, v, precision=lax.Precision.HIGHEST).reshape(row_count, D)
    attended = low(low_back(attended))
    residual = x + low_back(jnp.dot(attended, out_weight, precision=lax.Precision.HIGHEST) + out_bias)
    normed_mid = low(layer_norm(residual, mid_gain, mid_shift))
    before = low_back(jnp.dot(normed_mid, in_weight, precision=lax.Precision.HIGHEST) + in_bias)
    active = low(jax.nn.gelu(before, approximate=False))
    branch = low_back(jnp.dot(active, down_weight, precision=lax.Precision.HIGHEST) + down_bias)
    return (residual + branch) * live_mask

def reference(hidden_in, time_embed, seg_ids, pre_gain, pre_shift, qkv_weight, qv_bias, out_weight, out_bias, mid_gain, mid_shift, in_weight, in_bias, down_weight, down_bias, grad_out):
    params = (pre_gain, pre_shift, qkv_weight, qv_bias, out_weight, out_bias, mid_gain, mid_shift, in_weight, in_bias, down_weight, down_bias)
    blocks = hidden_in.shape[0] // BLOCK
    stacked = (hidden_in.reshape(blocks, BLOCK, D), time_embed.reshape(blocks, ITEMS_DEV, D), seg_ids.reshape(blocks, BLOCK), grad_out.reshape(blocks, BLOCK, D))
    totals = tuple((jnp.zeros(p.shape, jnp.float32) for p in params))

    def one_block(running, pieces):
        hidden, time_rows, segment, cotangent = pieces

        def forward(weights, hidden_part, time_part):
            return block_forward(weights, hidden_part, time_part, segment)
        result, pullback = jax.vjp(forward, params, hidden, time_rows)
        grad_params, grad_hidden, grad_time = pullback(cotangent)
        running = tuple((a + b for a, b in zip(running, grad_params)))
        return (running, (result, grad_hidden, grad_time))
    totals, (results, grad_hidden, grad_time) = lax.scan(one_block, totals, stacked)
    return (results.reshape(-1, D), grad_hidden.reshape(-1, D), grad_time.reshape(-1, D), totals[0], totals[1], totals[2], totals[3], totals[4], totals[5], totals[6], totals[7], totals[8], totals[9], totals[10], totals[11])
```

```python
import functools

import jax
import jax.numpy as jnp
from jax import lax
from jax.experimental import pallas as pl
from jax.experimental.pallas import tpu as pltpu
from jax.sharding import PartitionSpec as P

D = 768
HEADS = 12
HEAD_DIM = 64
FF = 3072
BLOCK = 1024
SHORT = 64
GROUPS = BLOCK // SHORT
PAIRS = HEADS // 2
TB = 256
NEG = -1e30
F32 = jnp.float32
BF16 = jnp.bfloat16
VMEM_LIMIT = 62 * 1024 * 1024
ANY = pl.BlockSpec(memory_space=pl.ANY)
VMEM = pl.BlockSpec(memory_space=pltpu.VMEM)
SMEM = pl.BlockSpec(memory_space=pltpu.SMEM)
ERFC_SCALE = 0.44
ERFC_POLY = (
    0.24822097621403005,
    0.2488708795734658,
    0.21731516533725015,
    0.21580763970434977,
    -0.020173037922183695,
    0.2966799647080617,
    -0.2779439059726245,
    0.07122249905985603,
)


def rows_at(i, size):
    return pl.ds(pl.multiple_of(i * size, size), size)


def mm(a, b):
    return lax.dot_general(a, b, (((1,), (0,)), ((), ())), preferred_element_type=F32)


def mm_t(a, b):
    return lax.dot_general(a, b, (((1,), (1,)), ((), ())), preferred_element_type=F32)


def normalize(v):
    center = v - jnp.mean(v, axis=-1, keepdims=True)
    spread = jnp.mean(center * center, axis=-1, keepdims=True)
    scale = lax.rsqrt(spread + 1e-05)
    return center * scale, scale


def norm_back(grad, gain, n, scale):
    g = grad * gain
    return scale * (
        g - jnp.mean(g, axis=-1, keepdims=True) - n * jnp.mean(g * n, axis=-1, keepdims=True)
    )


def fold8(v):
    return jnp.sum(v.reshape(v.shape[0] // 8, 8, v.shape[1]), axis=0)


def gelu_parts(u):
    z = jnp.abs(u) * 0.7071067811865476
    t = 1.0 / (1.0 + ERFC_SCALE * z)
    poly = jnp.full_like(t, ERFC_POLY[-1])
    for c in ERFC_POLY[-2::-1]:
        poly = poly * t + c
    e = jnp.exp(-(z * z))
    tail = 0.5 * poly * t * e
    phi = jnp.where(u >= 0, 1.0 - tail, tail)
    return u * phi, phi + u * e * 0.3989422804014327


class Mover:
    def __init__(self, sems):
        self.sems, self.next = sems, 0

    def start(self, src, dst):
        copy = pltpu.make_async_copy(src, dst, self.sems.at[self.next])
        self.next += 1
        copy.start()
        return copy


def stage_norm1(sid, time, vecs, x, a1, a1t):
    gain, shift = vecs[0:1, :], vecs[1:2, :]

    @pl.loop(0, BLOCK // 128)
    def _(i):
        parts = []
        for half in range(2):
            s = sid[2 * i + half]
            live = (s >= 0).astype(F32)
            row = time[pl.ds(jnp.maximum(s, 0), 1), :]
            parts.append((x[rows_at(2 * i + half, SHORT), :] + row) * live)
        block = jnp.concatenate(parts, axis=0)
        at = rows_at(i, 128)
        x[at, :] = block
        n, _ = normalize(block)
        a = n * gain + shift
        a1[at, :] = a.astype(BF16)
        a1t[:, at] = a.T.astype(BF16)


def mask_rows(sid, i, groups):
    lane = lax.rem(lax.broadcasted_iota(jnp.int32, (SHORT, 128), 1), 64)
    mq, mk = [], []
    for g in range(groups):
        s = sid[groups * i + g]
        own = jnp.where(s >= 0, s, 16)
        mk.append((lane == own).astype(F32))
        bad = ((lane < 16) & (lane != s)) | (lane == 16)
        mq.append(jnp.where(bad, NEG, 0.0))
    return jnp.concatenate(mq, axis=0), jnp.concatenate(mk, axis=0)


def low_lanes(shape):
    return lax.broadcasted_iota(jnp.int32, shape, 1) < 64


def low_rows(shape):
    return lax.broadcasted_iota(jnp.int32, shape, 0) < 64


def stage_q(sid, vecs, a1, w, q0, q1):
    @pl.loop(0, BLOCK // TB)
    def _(i):
        at = rows_at(i, TB)
        mq, _ = mask_rows(sid, i, TB // SHORT)
        acc = mm(a1[at, :], w) + vecs[2:3, :]
        acc = acc.astype(BF16).astype(F32) * (HEAD_DIM**-0.5)
        low = low_lanes((TB, 128))
        for p in range(PAIRS):
            part = acc[:, 128 * p : 128 * p + 128]
            q0[at, 128 * p : 128 * p + 128] = jnp.where(low, part, mq).astype(BF16)
            q1[at, 128 * p : 128 * p + 128] = jnp.where(low, mq, part).astype(BF16)


def stage_k(sid, a1, w, k0, k1, kt):
    @pl.loop(0, BLOCK // TB)
    def _(i):
        at = rows_at(i, TB)
        _, mk = mask_rows(sid, i, TB // SHORT)
        acc = mm(a1[at, :], w)
        low = low_lanes((TB, 128))
        for p in range(PAIRS):
            part = acc[:, 128 * p : 128 * p + 128]
            k0[at, 128 * p : 128 * p + 128] = jnp.where(low, part, mk).astype(BF16)
            k1[at, 128 * p : 128 * p + 128] = jnp.where(low, mk, part).astype(BF16)
        kt[:, at] = acc.T.astype(BF16)


def stage_v(vecs, a1, w, v, vt0, vt1):
    @pl.loop(0, BLOCK // TB)
    def _(i):
        at = rows_at(i, TB)
        acc = mm(a1[at, :], w) + vecs[3:4, :]
        v[at, :] = acc.astype(BF16)
        accT = acc.T
        low = low_rows((128, TB))
        for p in range(PAIRS):
            part = accT[128 * p : 128 * p + 128, :]
            vt0[128 * p : 128 * p + 128, at] = jnp.where(low, part, 1.0).astype(BF16)
            vt1[128 * p : 128 * p + 128, at] = jnp.where(low, 1.0, part).astype(BF16)


QB = 256


def attention_step(step, q0, q1, k0, k1, vt0, vt1, o, ot, lse):
    pair, part = step // (BLOCK // QB), step % (BLOCK // QB)
    lanes, at = rows_at(pair, 128), rows_at(part, QB)
    outs, logs = [], []
    for q, k, vt, total_row in ((q0, k0, vt0, 64), (q1, k1, vt1, 0)):
        scores = mm_t(k[:, lanes], q[at, lanes])
        top = jnp.max(scores, axis=0, keepdims=True)
        e = jnp.exp(scores - top).astype(BF16)
        res = mm(vt[lanes, :], e)
        total = res[total_row : total_row + 1, :]
        outs.append(res * (1.0 / total))
        logs.append(top + jnp.log(total))
    both = jnp.where(low_rows((128, QB)), outs[0], outs[1])
    ot[lanes, at] = both.astype(BF16)
    o[at, lanes] = both.T.astype(BF16)
    lse[pl.ds(2 * pair, 1), at] = logs[0]
    lse[pl.ds(2 * pair + 1, 1), at] = logs[1]


def kernel_a(sid, hidden, time, vecs, wqkv, x_h, a1t_h, q0_h, q1_h, k0_h, k1_h, v_h, kt_h, o_h, ot_h, lse,
             x, a1, a1t, q0, q1, k0, k1, v, kt, vt0, vt1, o, ot, w, sems):
    mv = Mover(sems)
    cx = mv.start(hidden, x)
    cw = [mv.start(wqkv.at[:, pl.ds(D * j, D)], w.at[j]) for j in range(3)]
    cx.wait()
    stage_norm1(sid, time, vecs, x, a1, a1t)
    outs = [mv.start(x, x_h), mv.start(a1t, a1t_h)]
    cw[0].wait()
    stage_q(sid, vecs, a1, w[0], q0, q1)
    outs += [mv.start(q0, q0_h), mv.start(q1, q1_h)]
    cw[1].wait()
    stage_k(sid, a1, w[1], k0, k1, kt)
    outs += [mv.start(k0, k0_h), mv.start(k1, k1_h), mv.start(kt, kt_h)]
    cw[2].wait()
    stage_v(vecs, a1, w[2], v, vt0, vt1)
    outs += [mv.start(v, v_h)]

    @pl.loop(0, PAIRS * (BLOCK // QB))
    def _(step):
        attention_step(step, q0, q1, k0, k1, vt0, vt1, o, ot, lse)

    outs += [mv.start(o, o_h), mv.start(ot, ot_h)]
    for c in outs:
        c.wait()


def sds(shape, dtype):
    return jax.ShapeDtypeStruct(shape, dtype)


TOK = (BLOCK, D)
TOKT = (D, BLOCK)


def vm(shape, dtype):
    return pltpu.VMEM(shape, dtype)


def call_a(sid, hidden, time, vecs, wqkv):
    out = [sds(TOK, F32), sds(TOKT, BF16)] + [sds(TOK, BF16)] * 5 + [sds(TOKT, BF16), sds(TOK, BF16), sds(TOKT, BF16), sds((16, BLOCK), F32)]
    return pl.pallas_call(
        kernel_a,
        name="part_a",
        out_shape=out,
        in_specs=[SMEM, ANY, VMEM, VMEM, ANY],
        out_specs=[ANY] * 10 + [VMEM],
        scratch_shapes=[vm(TOK, F32), vm(TOK, BF16), vm(TOKT, BF16)] + [vm(TOK, BF16)] * 5 + [vm(TOKT, BF16)] * 3
        + [vm(TOK, BF16), vm(TOKT, BF16), vm((3, D, D), BF16), pltpu.SemaphoreType.DMA((16,))],
        compiler_params=pltpu.CompilerParams(vmem_limit_bytes=VMEM_LIMIT),
    )(sid, hidden, time, vecs, wqkv)


def kernel_b(sid, x_h, o_h, gout_h, vecs, wout_h, win_h, wdown_h,
             out_h, gx1_h, gb_h, go0_h, go1_h, dots, gdown_h, gin_h, sums,
             x, o, gy, wout, win, wdown, gm, a2t, ht, gu, gb, go0, go1, stage, sems):
    mv = Mover(sems)
    cx, co, cg = mv.start(x_h, x), mv.start(o_h, o), mv.start(gout_h, gy)
    cwo = mv.start(wout_h, wout)
    cwi = [mv.start(win_h.at[:, pl.ds(D * j, D)], win.at[j]) for j in range(4)]
    cwd = [mv.start(wdown_h.at[pl.ds(D * j, D), :], wdown.at[j]) for j in range(4)]
    sums[...] = jnp.zeros_like(sums)
    for c in [cx, co, cg, cwo] + cwi + cwd:
        c.wait()
    lane = lax.broadcasted_iota(jnp.int32, (16, D), 1) // HEAD_DIM
    heads = (lane == lax.broadcasted_iota(jnp.int32, (16, D), 0)).astype(BF16)
    blocks = BLOCK // TB
    outs = []
    so = mv.sems

    def out_copies(i):
        at = rows_at(i, TB)
        return [pltpu.make_async_copy(x.at[at, :], out_h.at[at, :], so.at[16]),
                pltpu.make_async_copy(gy.at[at, :], gx1_h.at[at, :], so.at[17])]

    @pl.loop(0, blocks)
    def _(i):
        at = rows_at(i, TB)
        live = jnp.concatenate(
            [jnp.full((SHORT, 1), (sid[(TB // SHORT) * i + g] >= 0).astype(F32), F32) for g in range(TB // SHORT)], axis=0)
        x1 = x[at, :] + mm(o[at, :], wout[...]) + vecs[4:5, :]
        n2, r2 = normalize(x1)
        a2f = n2 * vecs[5:6, :] + vecs[6:7, :]
        a2 = a2f.astype(BF16)
        a2t[:, at] = a2f.T.astype(BF16)
        gyb = gy[at, :] * live
        gmb = gyb.astype(BF16)
        gm[at, :] = gmb
        acc = x1 + vecs[11:12, :]
        ga2 = jnp.zeros((TB, D), F32)
        for j in range(4):
            u = mm(a2, win[j]) + vecs[7 + j : 8 + j, :]
            hf, slope = gelu_parts(u)
            ht[D * j : D * j + D, at] = hf.T.astype(BF16)
            acc = acc + mm(hf.astype(BF16), wdown[j])
            guf = mm_t(gmb, wdown[j]) * slope
            gub = guf.astype(BF16)
            gu[at, D * j : D * j + D] = gub
            sums[4 + j] += fold8(gub.astype(F32))
            ga2 = ga2 + mm_t(gub, win[j])
        x[at, :] = acc * live
        sums[8] += fold8(gmb.astype(F32))
        sums[2] += fold8(ga2 * n2)
        sums[3] += fold8(ga2)
        gx1 = gyb + norm_back(ga2, vecs[5:6, :], n2, r2)
        gy[at, :] = gx1
        for c in out_copies(i):
            c.start()
        gbb = gx1.astype(BF16)
        gb[at, :] = gbb
        sums[1] += fold8(gbb.astype(F32))
        go = mm_t(gbb, wout[...]).astype(BF16).astype(F32)
        prod = go * o[at, :].astype(F32)
        hi = prod.astype(BF16)
        lo = (prod - hi.astype(F32)).astype(BF16)
        dots[:, at] = mm_t(heads, hi) + mm_t(heads, lo)
        low = lax.rem(lax.broadcasted_iota(jnp.int32, (TB, D), 1), 128) < 64
        go0[at, :] = jnp.where(low, go, 0.0).astype(BF16)
        go1[at, :] = jnp.where(low, 0.0, go).astype(BF16)

    outs += [mv.start(gb, gb_h), mv.start(go0, go0_h), mv.start(go1, go1_h)]

    def tile_out(j, slot):
        return pltpu.make_async_copy(stage.at[slot], gdown_h.at[rows_at(j, D), :], so.at[18 + slot])

    def tile_in(j, slot):
        return pltpu.make_async_copy(stage.at[slot], gin_h.at[:, pl.ds(D * j, D)], so.at[18 + slot])

    pending = [None, None]
    for t in range(8):
        slot, j = t % 2, t % 4
        if pending[slot] is not None:
            pending[slot].wait()

        @pl.loop(0, D // TB)
        def _(r):
            if t < 4:
                stage[slot, rows_at(r, TB), :] = mm(ht[pl.ds(pl.multiple_of(D * j + r * TB, TB), TB), :], gm[...]).astype(BF16)
            else:
                stage[slot, rows_at(r, TB), :] = mm(a2t[rows_at(r, TB), :], gu[:, D * j : D * j + D]).astype(BF16)

        pending[slot] = tile_out(j, slot) if t < 4 else tile_in(j, slot)
        pending[slot].start()
    for c in pending:
        c.wait()
    for c in outs:
        c.wait()
    for i in range(blocks):
        for c in out_copies(i):
            c.wait()


def call_b(sid, x, o, gout, vecs, wout, win, wdown):
    out = [sds(TOK, F32), sds(TOK, F32)] + [sds(TOK, BF16)] * 3 + [sds((16, BLOCK), F32), sds((FF, D), BF16), sds((D, FF), BF16), sds((9, 8, D), F32)]
    return pl.pallas_call(
        kernel_b,
        name="part_b",
        out_shape=out,
        in_specs=[SMEM, ANY, ANY, ANY, VMEM, ANY, ANY, ANY],
        out_specs=[ANY] * 5 + [VMEM, ANY, ANY, VMEM],
        scratch_shapes=[vm(TOK, F32), vm(TOK, BF16), vm(TOK, F32), vm((D, D), BF16), vm((4, D, D), BF16), vm((4, D, D), BF16),
                        vm(TOK, BF16), vm(TOKT, BF16), vm((FF, BLOCK), BF16), vm((BLOCK, FF), BF16),
                        vm(TOK, BF16), vm(TOK, BF16), vm(TOK, BF16), vm((2, D, D), BF16), pltpu.SemaphoreType.DMA((20,))],
        compiler_params=pltpu.CompilerParams(vmem_limit_bytes=VMEM_LIMIT),
    )(sid, x, o, gout, vecs, wout, win, wdown)


def attention_back_step(step, q0, q1, k0, k1, v, kt, go0, go1, lse, dots, gk_acc, gv_acc, gqkv):
    parts = BLOCK // QB
    pair, part = step // parts, step % parts
    lanes, at = rows_at(pair, 128), rows_at(part, QB)
    gk_parts, gq_parts, pbs = [], [], []
    vv = v[:, lanes]
    for h, (q, k, go) in enumerate(((q0, k0, go0), (q1, k1, go1))):
        scores = mm_t(k[:, lanes], q[at, lanes])
        p = jnp.exp(scores - lse[pl.ds(2 * pair + h, 1), at])
        gp = mm_t(vv, go[at, lanes])
        gs = (p * (gp - dots[pl.ds(2 * pair + h, 1), at])).astype(BF16)
        pbs.append(mm(p.astype(BF16), go[at, lanes]))
        gk_parts.append(mm(gs, q[at, lanes]))
        gq_parts.append(mm(kt[lanes, :], gs))
    gk = jnp.where(low_lanes((BLOCK, 128)), gk_parts[0], gk_parts[1])
    gv = pbs[0] + pbs[1]
    gq = jnp.where(low_rows((128, QB)), gq_parts[0], gq_parts[1]) * (HEAD_DIM**-0.5)
    gqkv[0, at, lanes] = gq.T.astype(BF16)
    first = part == 0
    gk_acc[...] = jnp.where(first, gk, gk_acc[...] + gk)
    gv_acc[...] = jnp.where(first, gv, gv_acc[...] + gv)

    @pl.when(part == parts - 1)
    def _():
        gqkv[1, :, lanes] = gk_acc[...].astype(BF16)
        gqkv[2, :, lanes] = gv_acc[...].astype(BF16)


def kernel_c(sid, x_h, a1t_h, q0_h, q1_h, k0_h, k1_h, v_h, kt_h, ot_h, lse, gx1_h, gb_h, go0_h, go1_h, dots, vecs, wqkv_h,
             ig_h, tg, gqkvw_h, goutw_h, sums,
             x, a1t, q0, q1, k0, k1, v, kt, ot, gx1, gb, go0, go1, w, gqkv, gk_acc, gv_acc, gw, gwo, tsum, sems):
    mv = Mover(sems)
    early = [mv.start(s, d) for s, d in ((ot_h, ot), (gb_h, gb), (q0_h, q0), (q1_h, q1), (k0_h, k0), (k1_h, k1), (v_h, v), (kt_h, kt), (go0_h, go0), (go1_h, go1))]
    late = [mv.start(a1t_h, a1t), mv.start(x_h, x), mv.start(gx1_h, gx1)]
    late += [mv.start(wqkv_h.at[:, pl.ds(D * j, D)], w.at[j]) for j in range(3)]
    for c in early[:2]:
        c.wait()
    sums[...] = jnp.zeros_like(sums)

    @pl.loop(0, D // TB)
    def _(r):
        gwo[rows_at(r, TB), :] = mm(ot[rows_at(r, TB), :], gb[...]).astype(BF16)

    outs = [mv.start(gwo, goutw_h)]
    for c in early[2:]:
        c.wait()

    @pl.loop(0, PAIRS * (BLOCK // QB))
    def _(step):
        attention_back_step(step, q0, q1, k0, k1, v, kt, go0, go1, lse, dots, gk_acc, gv_acc, gqkv)

    for c in late:
        c.wait()
    for j in range(3):
        @pl.loop(0, D // TB)
        def _(r):
            gw[j, rows_at(r, TB), :] = mm(a1t[rows_at(r, TB), :], gqkv[j]).astype(BF16)

        outs.append(mv.start(gw.at[j], gqkvw_h.at[:, pl.ds(D * j, D)]))
    gain = vecs[0:1, :]

    @pl.loop(0, BLOCK // TB)
    def _(i):
        at = rows_at(i, TB)
        ga1 = mm_t(gqkv[0, at, :], w[0]) + mm_t(gqkv[1, at, :], w[1]) + mm_t(gqkv[2, at, :], w[2])
        sums[2] += fold8(gqkv[0, at, :].astype(F32))
        sums[3] += fold8(gqkv[2, at, :].astype(F32))
        n1, r1 = normalize(x[at, :])
        sums[0] += fold8(ga1 * n1)
        sums[1] += fold8(ga1)
        total = gx1[at, :] + norm_back(ga1, gain, n1, r1)
        for g in range(TB // SHORT):
            s = sid[(TB // SHORT) * i + g]
            live = (s >= 0).astype(F32)
            part = total[SHORT * g : SHORT * g + SHORT, :] * live
            x[rows_at((TB // SHORT) * i + g, SHORT), :] = part
            tsum[pl.ds((TB // SHORT) * i + g, 1), :] = jnp.sum(part, axis=0, keepdims=True)

    outs.append(mv.start(x, ig_h))
    row = lax.broadcasted_iota(jnp.int32, (GROUPS, D), 0)
    acc = jnp.zeros((GROUPS, D), F32)
    for g in range(GROUPS):
        acc = acc + jnp.where(row == sid[g], tsum[g : g + 1, :], 0.0)
    tg[...] = acc
    for c in outs:
        c.wait()


def call_c(sid, x, a1t, q0, q1, k0, k1, v, kt, ot, lse, gx1, gb, go0, go1, dots, vecs, wqkv):
    out = [sds(TOK, F32), sds((GROUPS, D), F32), sds((D, 3 * D), BF16), sds((D, D), BF16), sds((4, 8, D), F32)]
    return pl.pallas_call(
        kernel_c,
        name="part_c",
        out_shape=out,
        in_specs=[SMEM] + [ANY] * 9 + [VMEM] + [ANY] * 4 + [VMEM, VMEM, ANY],
        out_specs=[ANY, VMEM, ANY, ANY, VMEM],
        scratch_shapes=[vm(TOK, F32), vm(TOKT, BF16)] + [vm(TOK, BF16)] * 5 + [vm(TOKT, BF16)] * 2 + [vm(TOK, F32)] + [vm(TOK, BF16)] * 3
        + [vm((3, D, D), BF16), vm((3, BLOCK, D), BF16), vm((BLOCK, 128), F32), vm((BLOCK, 128), F32), vm((3, D, D), BF16), vm((D, D), BF16),
           vm((GROUPS, D), F32), pltpu.SemaphoreType.DMA((24,))],
        compiler_params=pltpu.CompilerParams(vmem_limit_bytes=VMEM_LIMIT),
    )(sid, x, a1t, q0, q1, k0, k1, v, kt, ot, lse, gx1, gb, go0, go1, dots, vecs, wqkv)


AXES = ("dp", "fsdp")
MESH = pl.DeviceIdType.MESH
SMALL = ((0, 24, 0), (24, 24, 1), (48, 48, 2), (96, 24, 4), (120, 24, 5), (144, 24, 6), (168, 96, 7), (264, 24, 11))
SMALL_LEN = 384


class Peers:
    def __init__(self):
        self.z, self.f = lax.axis_index("dp"), lax.axis_index("fsdp")
        self.c = self.f % 2
        self.yx = self.f // 2
        x, y = self.yx % 2, self.yx // 2
        self.partner = self.f + 1 - 2 * self.c
        self.fx, self.fy = self.f + 2 - 4 * x, self.f + 4 - 8 * y
        self.fd = self.fx + 4 - 8 * y
        self.qx, self.qy, self.qd = self.fx // 2, self.fy // 2, self.fd // 2
        self.dev = self.z * 8 + self.f

    def up(self, d):
        return (self.z + d) % 4

    def at(self, name, d=0):
        if name == "z":
            return (self.up(d), self.f)
        return (self.z, {"x": self.fx, "y": self.fy, "p": self.partner}[name])

    def greet(self):
        barrier = pltpu.get_barrier_semaphore()
        for target in [self.at("p"), self.at("x"), self.at("y")] + [self.at("z", d) for d in (1, 2, 3)]:
            pl.semaphore_signal(barrier, inc=1, device_id=target, device_id_type=MESH)
        pl.semaphore_wait(barrier, 6)


class Links:
    def __init__(self, peers, send, recv):
        self.peers, self.send, self.recv = peers, send, recv
        self.slots, self.sent = {}, []

    def slot(self, key):
        return self.slots.setdefault(key, len(self.slots))

    def start(self, key, src, dst, name, d=0):
        n = self.slot(key)
        copy = pltpu.make_async_remote_copy(
            src_ref=src, dst_ref=dst, send_sem=self.send.at[n], recv_sem=self.recv.at[n],
            device_id=self.peers.at(name, d), device_id_type=MESH)
        copy.start()
        self.sent.append(copy)

    def arrived(self, key, dst):
        n = self.slot(key)
        pltpu.make_async_remote_copy(
            src_ref=dst, dst_ref=dst, send_sem=self.send.at[n], recv_sem=self.recv.at[n],
            device_id=self.peers.at("p"), device_id_type=MESH).wait_recv()

    def finish(self):
        for copy in self.sent:
            copy.wait_send()
        self.sent = []


GATHER_SLOTS = 19


class Gather:
    def __init__(self, name, links, own, full, sem):
        self.name, self.links, self.own, self.full, self.sem = name, links, own, full, sem

    def key(self, *k):
        return (self.name,) + k

    def piece(self, d, f):
        return self.full.at[(self.links.peers.z + 4 - d) % 4, f]

    def begin(self):
        p = self.links.peers
        here = self.full.at[p.z, p.f]
        for d in (1, 3, 2):
            self.links.start(self.key("z", d), self.own, here, "z", d)
        self.local = pltpu.make_async_copy(self.own, here, self.sem)
        self.local.start()

    def first(self):
        p, links = self.links.peers, self.links
        for d in (0, 1, 3, 2):
            piece = self.piece(d, p.f)
            if d:
                links.arrived(self.key("z", d), piece)
            src = piece if d else self.own
            links.start(self.key("x", d), src, piece, "x")
            links.start(self.key("y", d), src, piece, "y")
        self.local.wait()
        mine = self.full.at[:, p.f]
        links.start(self.key("p", 0), mine, mine, "p")

    def second(self):
        p, links = self.links.peers, self.links
        for d in (0, 1, 3, 2):
            px, py = self.piece(d, p.fx), self.piece(d, p.fy)
            links.arrived(self.key("x", d), px)
            links.arrived(self.key("y", d), py)
            if d < 2:
                links.start(self.key("d", d), px, px, "y")
            else:
                links.start(self.key("d", d), py, py, "x")
        for n, f in ((1, p.fx), (2, p.fy)):
            part = self.full.at[:, f]
            links.start(self.key("p", n), part, part, "p")

    def third(self):
        p, links = self.links.peers, self.links
        for d in range(4):
            links.arrived(self.key("d", d), self.piece(d, p.fd))
        part = self.full.at[:, p.fd]
        links.start(self.key("p", 3), part, part, "p")

    def last(self):
        p, links = self.links.peers, self.links
        for n, f in enumerate((p.f, p.fx, p.fy, p.fd)):
            other = f + 1 - 2 * p.c
            links.arrived(self.key("p", n), self.full.at[:, other])


SCATTER_SLOTS = 10


class Scatter:
    def __init__(self, name, links, parts, out, bufs, sem):
        self.name, self.links, self.parts, self.out, self.sem = name, links, parts, out, sem
        self.t, self.p, self.dx, self.dy, self.xr, self.yr, self.zr = bufs

    def key(self, *k):
        return (self.name,) + k

    def begin(self):
        p = self.links.peers
        self.links.start(self.key("p"), self.parts.at[:, :, 1 - p.c], self.p, "p")
        self.local = pltpu.make_async_copy(self.parts.at[:, :, p.c], self.t, self.sem)
        self.local.start()

    def add(self, q, zs, ref, base=0):
        t = self.t

        @pl.loop(zs[0], zs[1])
        def _(i):
            t[i, q] = (t[i, q].astype(F32) + ref(i - base).astype(F32)).astype(BF16)

    def first(self):
        p, links, t = self.links.peers, self.links, self.t
        self.local.wait()
        links.arrived(self.key("p"), self.p)
        self.add(p.qd, (0, 4), lambda i: self.p[i, p.qd])
        links.start(self.key("dx"), t.at[pl.ds(0, 2), p.qd], self.dx, "x")
        links.start(self.key("dy"), t.at[pl.ds(2, 2), p.qd], self.dy, "y")
        self.add(p.qx, (0, 4), lambda i: self.p[i, p.qx])
        links.start(self.key("x", 0), t.at[pl.ds(0, 2), p.qx], self.xr.at[pl.ds(0, 2)], "x")
        self.add(p.qy, (0, 4), lambda i: self.p[i, p.qy])
        links.start(self.key("y", 1), t.at[pl.ds(2, 2), p.qy], self.yr.at[pl.ds(2, 2)], "y")
        self.add(p.yx, (0, 4), lambda i: self.p[i, p.yx])

    def second(self):
        p, links, t = self.links.peers, self.links, self.t
        links.arrived(self.key("dy"), self.dy)
        self.add(p.qx, (2, 4), lambda i: self.dy[i], 2)
        links.start(self.key("x", 1), t.at[pl.ds(2, 2), p.qx], self.xr.at[pl.ds(2, 2)], "x")
        links.arrived(self.key("dx"), self.dx)
        self.add(p.qy, (0, 2), lambda i: self.dx[i])
        links.start(self.key("y", 0), t.at[pl.ds(0, 2), p.qy], self.yr.at[pl.ds(0, 2)], "y")

    def third(self):
        p, links, t = self.links.peers, self.links, self.t
        for n in range(2):
            links.arrived(self.key("x", n), self.xr.at[pl.ds(2 * n, 2)])
            links.arrived(self.key("y", n), self.yr.at[pl.ds(2 * n, 2)])

        @pl.loop(0, 4)
        def _(i):
            t[i, p.yx] = (t[i, p.yx].astype(F32) + self.xr[i].astype(F32) + self.yr[i].astype(F32)).astype(BF16)

        for d in (2, 1, 3):
            links.start(self.key("z", d), t.at[p.up(d), p.yx], self.zr.at[d - 1], "z", d)

    def last(self):
        p, links = self.links.peers, self.links
        for d in (1, 2, 3):
            links.arrived(self.key("z", d), self.zr.at[d - 1])
        total = self.t[p.z, p.yx].astype(F32)
        for n in range(3):
            total = total + self.zr[n].astype(F32)
        self.out[...] = total


def scatter_bufs(rows, cols):
    return [pltpu.VMEM(lead + (rows, cols), BF16) for lead in ((4, 4), (4, 4), (2,), (2,), (4,), (4,), (3,))]


class SmallSum:
    def __init__(self, links, value, bufs):
        self.links, self.value, self.bufs = links, value, bufs

    def send(self, n, name):
        self.links.start(("s", n), self.value.at[n], self.bufs.at[n], name)

    def take(self, n):
        self.links.arrived(("s", n), self.bufs.at[n])
        self.value[n + 1] = self.value[n] + self.bufs[n]

    def spread(self):
        for d in (1, 2, 3):
            self.links.start(("s", 2 + d), self.value.at[3], self.bufs.at[2 + d], "z", d)

    def total(self):
        for d in (1, 2, 3):
            self.links.arrived(("s", 2 + d), self.bufs.at[2 + d])
        return self.value[3] + self.bufs[3] + self.bufs[4] + self.bufs[5]


def small_places(dev):
    i = lax.broadcasted_iota(jnp.int32, (1, SMALL_LEN), 1)
    row, col = jnp.full((1, SMALL_LEN), 15, jnp.int32), jnp.full((1, SMALL_LEN), -1, jnp.int32)
    for start, n, base in SMALL:
        here = (i >= start) & (i < start + n)
        row = jnp.where(here, base + (dev * n) // D, row)
        col = jnp.where(here, (dev * n) % D + i - start, col)
    return row, col


def small_select(col):
    return (lax.broadcasted_iota(jnp.int32, (D, SMALL_LEN), 0) == col).astype(F32)


def kernel_prep(small, wqkv, wout, win, wdown, small_o, qkv_o, out_o, in_o, down_o):
    row, col = small_places(lax.axis_index("dp") * 8 + lax.axis_index("fsdp"))
    at_row = lax.broadcasted_iota(jnp.int32, (16, SMALL_LEN), 0) == row
    values = jnp.where(at_row, small[...].astype(BF16).astype(F32), 0.0).astype(BF16)
    small_o[...] = mm_t(values, small_select(col).astype(BF16)).astype(BF16)
    qkv_o[...] = wqkv[...].astype(BF16)
    out_o[...] = wout[...].astype(BF16)
    in_o[...] = win[...].astype(BF16)
    down_o[...] = wdown[...].astype(BF16)


def call_prep(small, weights):
    return pl.pallas_call(
        kernel_prep, name="prep",
        out_shape=[sds((16, D), BF16)] + [sds(w.shape, BF16) for w in weights],
        in_specs=[VMEM] * 5, out_specs=[VMEM] * 5,
    )(small, *weights)


def sum_small(gathered, staged, sem, vecs):
    copy = pltpu.make_async_copy(gathered, staged, sem)
    copy.start()
    copy.wait()
    total = jnp.zeros((16, D), F32)
    for i in range(4):
        for j in range(8):
            total = total + staged[i, j].astype(F32)
    vecs[...] = total


def kernel_gather(small, wqkv, wout, win, wdown, vecs, small_f, qkv_f, out_f, in_f, down_f, staged, sems, send, recv):
    peers = Peers()
    links = Links(peers, send, recv)
    peers.greet()
    g = [Gather(n, links, own, full, sems.at[n])
         for n, (own, full) in enumerate(((small, small_f), (wqkv, qkv_f), (wout, out_f), (win, in_f), (wdown, down_f)))]
    for a in g:
        a.begin()
    for n, a in enumerate(g):
        a.first()
        if n:
            g[n - 1].second()
        if n > 1:
            g[n - 2].third()
    g[4].second()
    g[3].third()
    g[4].third()
    for a in g:
        a.last()
    links.finish()
    sum_small(small_f, staged, sems.at[5], vecs)


def call_gather(own):
    n = len(own)
    return pl.pallas_call(
        kernel_gather, name="gather",
        out_shape=[sds((16, D), F32)] + [sds((4, 8) + a.shape, BF16) for a in own],
        in_specs=[VMEM] * n, out_specs=[VMEM] + [ANY] * n,
        scratch_shapes=[vm((4, 8, 16, D), BF16), pltpu.SemaphoreType.DMA((n + 1,)),
                        pltpu.SemaphoreType.DMA((GATHER_SLOTS * n,)), pltpu.SemaphoreType.DMA((GATHER_SLOTS * n,))],
        compiler_params=pltpu.CompilerParams(vmem_limit_bytes=VMEM_LIMIT, collective_id=1, has_side_effects=True),
    )(*own)


def kernel_scatter(sums_b, sums_c, down, inn, out, qkv, small_o, down_o, in_o, out_o, qkv_o, value, small_b, *rest):
    bufs, (sems, send, recv) = rest[:28], rest[28:]
    peers = Peers()
    links = Links(peers, send, recv)
    pick = lambda ref, n: jnp.sum(ref[n], axis=0, keepdims=True)
    rows = [pick(sums_c, n) for n in range(4)] + [pick(sums_b, n) for n in range(1, 9)] + [jnp.zeros((4, D), F32)]
    value[0] = jnp.concatenate(rows, axis=0)
    peers.greet()
    small = SmallSum(links, value, small_b)
    s = [Scatter(n, links, parts, o, bufs[7 * n : 7 * n + 7], sems.at[n])
         for n, (parts, o) in enumerate(((down, down_o), (inn, in_o), (out, out_o), (qkv, qkv_o)))]
    for a in s:
        a.begin()
    small.send(0, "p")
    s[0].first()
    small.take(0)
    small.send(1, "x")
    s[1].first()
    small.take(1)
    small.send(2, "y")
    s[0].second()
    s[2].first()
    small.take(2)
    small.spread()
    s[0].third()
    s[1].second()
    s[3].first()
    s[1].third()
    s[2].second()
    s[0].last()
    s[3].second()
    s[2].third()
    total = small.total()
    row, col = small_places(peers.dev)
    picked = lax.dot_general(total, small_select(col), (((1,), (0,)), ((), ())),
                             precision=lax.Precision.HIGHEST, preferred_element_type=F32)
    at_row = lax.broadcasted_iota(jnp.int32, (16, SMALL_LEN), 0) == row
    small_o[...] = jnp.sum(jnp.where(at_row, picked, 0.0), axis=0, keepdims=True)
    s[1].last()
    s[3].third()
    s[2].last()
    s[3].last()
    links.finish()


def call_scatter(sums_b, sums_c, parts):
    shapes = [(p.shape[0] // 32, p.shape[1]) for p in parts]
    parts = [p.reshape(4, 4, 2, r, p.shape[1]) for p, (r, _) in zip(parts, shapes)]
    bufs = [b for s in shapes for b in scatter_bufs(*s)]
    slots = SCATTER_SLOTS * len(parts) + 6
    return pl.pallas_call(
        kernel_scatter, name="scatter",
        out_shape=[sds((1, SMALL_LEN), F32)] + [sds(s, F32) for s in shapes],
        in_specs=[VMEM, VMEM] + [ANY] * 4, out_specs=[VMEM] * 5,
        scratch_shapes=[vm((4, 16, D), F32), vm((6, 16, D), F32)] + bufs
        + [pltpu.SemaphoreType.DMA((4,)), pltpu.SemaphoreType.DMA((slots,)), pltpu.SemaphoreType.DMA((slots,))],
        compiler_params=pltpu.CompilerParams(vmem_limit_bytes=VMEM_LIMIT, collective_id=2, has_side_effects=True),
    )(sums_b, sums_c, *parts)


def gather_all(a):
    return lax.all_gather(a.astype(BF16), AXES, axis=0, tiled=True)


def scatter_sum(a):
    return lax.psum_scatter(a, AXES, scatter_dimension=0, tiled=True)


def split_small(row, small):
    parts, at = [], 0
    for s in small:
        parts.append(row[at : at + s.shape[0]])
        at += s.shape[0]
    return parts


def gather_plain(small, weights):
    every = lax.all_gather(jnp.concatenate([s.astype(BF16) for s in small]), AXES, axis=0, tiled=False)
    vecs, at = [], 0
    for s in small:
        vecs.append(every[:, at : at + s.shape[0]].reshape(-1, D))
        at += s.shape[0]
    vecs = jnp.concatenate(vecs + [jnp.zeros((4, D), BF16)], axis=0).astype(F32)
    return vecs, [gather_all(w) for w in weights]


def scatter_plain(sums_b, sums_c, grads, small):
    sb, sc = jnp.sum(sums_b, axis=1), jnp.sum(sums_c, axis=1)
    vectors = (sc[0], sc[1], sc[2:4].reshape(-1), sb[1], sb[2], sb[3], sb[4:8].reshape(-1), sb[8])
    devices = D // small[0].shape[0]
    packed = jnp.concatenate([g.reshape(devices, -1) for g in vectors], axis=1)
    return scatter_sum(packed).reshape(-1), [scatter_sum(g.astype(F32)) for g in grads]


def local(
    own_links,
    hidden_in, time_embed, seg_ids, pre_gain, pre_shift, qkv_weight, qv_bias, out_weight, out_bias,
    mid_gain, mid_shift, in_weight, in_bias, down_weight, down_bias, grad_out,
):
    sid = seg_ids.reshape(GROUPS, SHORT)[:, 0]
    small = (pre_gain, pre_shift, qv_bias, out_bias, mid_gain, mid_shift, in_bias, down_bias)
    weights = (qkv_weight, out_weight, in_weight, down_weight)
    if own_links:
        row = jnp.concatenate(small + (jnp.zeros((SMALL_LEN - 288,), F32),)).reshape(1, SMALL_LEN)
        vecs, _, *full = call_gather(call_prep(row, weights))
        wqkv, wout, win, wdown = [a.reshape(-1, a.shape[-1]) for a in full]
    else:
        vecs, (wqkv, wout, win, wdown) = gather_plain(small, weights)
    x, a1t, q0, q1, k0, k1, v, kt, o, ot, lse = call_a(sid, hidden_in, time_embed, vecs, wqkv)
    block_out, gx1, gb, go0, go1, dots, gdown, gin, sums_b = call_b(sid, x, o, grad_out, vecs, wout, win, wdown)
    input_grad, time_grad, gqkv, gout, sums_c = call_c(
        sid, x, a1t, q0, q1, k0, k1, v, kt, ot, lse, gx1, gb, go0, go1, dots, vecs, wqkv)
    if own_links:
        mine, gdown, gin, gout, gqkv = call_scatter(sums_b, sums_c, (gdown, gin, gout, gqkv))
        mine = mine.reshape(-1)
    else:
        mine, (gdown, gin, gout, gqkv) = scatter_plain(sums_b, sums_c, (gdown, gin, gout, gqkv), small)
    gpg, gps, gqvb, gob, gmg, gms, gib, gdb = split_small(mine, small)
    return (block_out, input_grad, time_grad, gpg, gps, gqkv, gqvb, gout, gob, gmg, gms, gin, gib, gdown, gdb)


def solution(mesh):
    rows, flat = P(AXES, None), P(AXES)
    own_links = dict(mesh.shape) == {"dp": 4, "fsdp": 8}
    return jax.shard_map(
        functools.partial(local, own_links),
        mesh=mesh,
        in_specs=(rows, rows, flat, flat, flat, rows, flat, rows, flat, flat, flat, rows, flat, rows, flat, rows),
        out_specs=(rows, rows, rows, flat, flat, rows, flat, rows, flat, flat, flat, rows, flat, rows, flat),
        check_vma=False,
    )
```

```python
import functools

import jax
import jax.numpy as jnp
from jax import lax
from jax.experimental import pallas as pl
from jax.experimental.pallas import tpu as pltpu
from jax.sharding import PartitionSpec as P

D = 768
HEADS = 12
HEAD_DIM = 64
FF = 3072
BLOCK = 1024
SHORT = 64
GROUPS = BLOCK // SHORT
PAIRS = HEADS // 2
TB = 256
NEG = -1e30
F32 = jnp.float32
BF16 = jnp.bfloat16
VMEM_LIMIT = 62 * 1024 * 1024
ANY = pl.BlockSpec(memory_space=pl.ANY)
VMEM = pl.BlockSpec(memory_space=pltpu.VMEM)
SMEM = pl.BlockSpec(memory_space=pltpu.SMEM)
ERFC_SCALE = 0.44
ERFC_POLY = (
    0.24822097621403005,
    0.2488708795734658,
    0.21731516533725015,
    0.21580763970434977,
    -0.020173037922183695,
    0.2966799647080617,
    -0.2779439059726245,
    0.07122249905985603,
)


def rows_at(i, size):
    return pl.ds(pl.multiple_of(i * size, size), size)


def mm(a, b):
    return lax.dot_general(a, b, (((1,), (0,)), ((), ())), preferred_element_type=F32)


def mm_t(a, b):
    return lax.dot_general(a, b, (((1,), (1,)), ((), ())), preferred_element_type=F32)


def normalize(v):
    center = v - jnp.mean(v, axis=-1, keepdims=True)
    spread = jnp.mean(center * center, axis=-1, keepdims=True)
    scale = lax.rsqrt(spread + 1e-05)
    return center * scale, scale


def norm_back(grad, gain, n, scale):
    g = grad * gain
    return scale * (
        g - jnp.mean(g, axis=-1, keepdims=True) - n * jnp.mean(g * n, axis=-1, keepdims=True)
    )


def fold8(v):
    return jnp.sum(v.reshape(v.shape[0] // 8, 8, v.shape[1]), axis=0)


def gelu_parts(u):
    z = jnp.abs(u) * 0.7071067811865476
    t = 1.0 / (1.0 + ERFC_SCALE * z)
    poly = jnp.full_like(t, ERFC_POLY[-1])
    for c in ERFC_POLY[-2::-1]:
        poly = poly * t + c
    e = jnp.exp(-(z * z))
    tail = 0.5 * poly * t * e
    phi = jnp.where(u >= 0, 1.0 - tail, tail)
    return u * phi, phi + u * e * 0.3989422804014327


class Mover:
    def __init__(self, sems):
        self.sems, self.next = sems, 0

    def start(self, src, dst):
        copy = pltpu.make_async_copy(src, dst, self.sems.at[self.next])
        self.next += 1
        copy.start()
        return copy


def run_hooks(step, hooks):
    for n, action in hooks.items():
        pl.when(step == n)(action)


def stage_norm1(sid, time, vecs, x, a1, a1t, hooks):
    gain, shift = vecs[0:1, :], vecs[1:2, :]

    @pl.loop(0, BLOCK // 128)
    def _(i):
        parts = []
        for half in range(2):
            s = sid[2 * i + half]
            live = (s >= 0).astype(F32)
            row = time[pl.ds(jnp.maximum(s, 0), 1), :]
            parts.append((x[rows_at(2 * i + half, SHORT), :] + row) * live)
        block = jnp.concatenate(parts, axis=0)
        at = rows_at(i, 128)
        x[at, :] = block
        n, _ = normalize(block)
        a = n * gain + shift
        a1[at, :] = a.astype(BF16)
        a1t[:, at] = a.T.astype(BF16)
        run_hooks(i, hooks)


def mask_rows(sid, i, groups):
    lane = lax.rem(lax.broadcasted_iota(jnp.int32, (SHORT, 128), 1), 64)
    mq, mk = [], []
    for g in range(groups):
        s = sid[groups * i + g]
        own = jnp.where(s >= 0, s, 16)
        mk.append((lane == own).astype(F32))
        bad = ((lane < 16) & (lane != s)) | (lane == 16)
        mq.append(jnp.where(bad, NEG, 0.0))
    return jnp.concatenate(mq, axis=0), jnp.concatenate(mk, axis=0)


def low_lanes(shape):
    return lax.broadcasted_iota(jnp.int32, shape, 1) < 64


def low_rows(shape):
    return lax.broadcasted_iota(jnp.int32, shape, 0) < 64


def stage_q(sid, vecs, a1, w, q0, q1):
    @pl.loop(0, BLOCK // TB)
    def _(i):
        at = rows_at(i, TB)
        mq, _ = mask_rows(sid, i, TB // SHORT)
        acc = mm(a1[at, :], w) + vecs[2:3, :]
        acc = acc.astype(BF16).astype(F32) * (HEAD_DIM**-0.5)
        low = low_lanes((TB, 128))
        for p in range(PAIRS):
            part = acc[:, 128 * p : 128 * p + 128]
            q0[at, 128 * p : 128 * p + 128] = jnp.where(low, part, mq).astype(BF16)
            q1[at, 128 * p : 128 * p + 128] = jnp.where(low, mq, part).astype(BF16)


def stage_k(sid, a1, w, k0, k1, kt):
    @pl.loop(0, BLOCK // TB)
    def _(i):
        at = rows_at(i, TB)
        _, mk = mask_rows(sid, i, TB // SHORT)
        acc = mm(a1[at, :], w)
        low = low_lanes((TB, 128))
        for p in range(PAIRS):
            part = acc[:, 128 * p : 128 * p + 128]
            k0[at, 128 * p : 128 * p + 128] = jnp.where(low, part, mk).astype(BF16)
            k1[at, 128 * p : 128 * p + 128] = jnp.where(low, mk, part).astype(BF16)
        kt[:, at] = acc.T.astype(BF16)


def stage_v(vecs, a1, w, v, vt0, vt1):
    @pl.loop(0, BLOCK // TB)
    def _(i):
        at = rows_at(i, TB)
        acc = mm(a1[at, :], w) + vecs[3:4, :]
        v[at, :] = acc.astype(BF16)
        accT = acc.T
        low = low_rows((128, TB))
        for p in range(PAIRS):
            part = accT[128 * p : 128 * p + 128, :]
            vt0[128 * p : 128 * p + 128, at] = jnp.where(low, part, 1.0).astype(BF16)
            vt1[128 * p : 128 * p + 128, at] = jnp.where(low, 1.0, part).astype(BF16)


QB = 256


def attention_step(step, q0, q1, k0, k1, vt0, vt1, o, ot, lse):
    pair, part = step // (BLOCK // QB), step % (BLOCK // QB)
    lanes, at = rows_at(pair, 128), rows_at(part, QB)
    outs, logs = [], []
    for q, k, vt, total_row in ((q0, k0, vt0, 64), (q1, k1, vt1, 0)):
        scores = mm_t(k[:, lanes], q[at, lanes])
        top = jnp.max(scores, axis=0, keepdims=True)
        e = jnp.exp(scores - top).astype(BF16)
        res = mm(vt[lanes, :], e)
        total = res[total_row : total_row + 1, :]
        outs.append(res * (1.0 / total))
        logs.append(top + jnp.log(total))
    both = jnp.where(low_rows((128, QB)), outs[0], outs[1])
    ot[lanes, at] = both.astype(BF16)
    o[at, lanes] = both.T.astype(BF16)
    lse[pl.ds(2 * pair, 1), at] = logs[0]
    lse[pl.ds(2 * pair + 1, 1), at] = logs[1]


def kernel_a(linked, sid, hidden, time, *refs):
    if linked:
        own, refs = refs[:5], refs[5:]
        vecs, refs = refs[0], refs[1:]
    else:
        (vecs, wqkv), refs = refs[:2], refs[2:]
    (x_h, a1t_h, q0_h, q1_h, k0_h, k1_h, v_h, kt_h, o_h, ot_h, lse), refs = refs[:11], refs[11:]
    if linked:
        full, refs = refs[:5], refs[5:]
        wqkv = full[1]
    (x, a1, a1t, q0, q1, k0, k1, v, kt, vt0, vt1, o, ot, w, sems), refs = refs[:15], refs[15:]
    mv = Mover(sems)
    cx = mv.start(hidden, x)
    norm_hooks, attention_hooks, after = {}, {}, [[], [], [], []]
    if linked:
        staged, local_sems, send, recv = refs
        peers = Peers()
        links = Links(peers, send, recv)
        peers.greet()
        small, qkv, out, inn, down = [Gather(n, links, own[n], full[n], local_sems.at[n]) for n in range(5)]
        for a in (small, qkv, out, inn, down):
            a.begin()
        small.first()
        qkv.first()
        small.second()
        small.third()
        out.first((0,))
        small.last()
        sum_small(full[0], staged, local_sems.at[5], vecs)
        norm_hooks = {1: qkv.second, 3: out.first_rest, 5: qkv.third, 6: inn.first_own}
        after = [[out.second, inn.first_rest], [out.third, down.first_own], [inn.second, down.first_rest], []]
        attention_hooks = {4: inn.third, 9: down.second, 17: down.third}
    cx.wait()
    stage_norm1(sid, time, vecs, x, a1, a1t, norm_hooks)
    outs = [mv.start(x, x_h), mv.start(a1t, a1t_h)]
    if linked:
        qkv.last()
    cw = [mv.start(wqkv.at[:, :, pl.ds(D * j, D)], w.at[j]) for j in range(3)]

    def weight(j):
        cw[j].wait()
        return w[j].reshape(D, D)

    stage_q(sid, vecs, a1, weight(0), q0, q1)
    for action in after[0]:
        action()
    outs += [mv.start(q0, q0_h), mv.start(q1, q1_h)]
    stage_k(sid, a1, weight(1), k0, k1, kt)
    for action in after[1]:
        action()
    outs += [mv.start(k0, k0_h), mv.start(k1, k1_h), mv.start(kt, kt_h)]
    stage_v(vecs, a1, weight(2), v, vt0, vt1)
    for action in after[2]:
        action()
    outs += [mv.start(v, v_h)]

    @pl.loop(0, PAIRS * (BLOCK // QB))
    def _(step):
        attention_step(step, q0, q1, k0, k1, vt0, vt1, o, ot, lse)
        run_hooks(step, attention_hooks)

    outs += [mv.start(o, o_h), mv.start(ot, ot_h)]
    for copy in outs:
        copy.wait()
    if linked:
        for a in (out, inn, down):
            a.last()
        links.finish()


def sds(shape, dtype):
    return jax.ShapeDtypeStruct(shape, dtype)


TOK = (BLOCK, D)
TOKT = (D, BLOCK)


def vm(shape, dtype):
    return pltpu.VMEM(shape, dtype)


OUT_A = [sds(TOK, F32), sds(TOKT, BF16)] + [sds(TOK, BF16)] * 5 + [sds(TOKT, BF16), sds(TOK, BF16), sds(TOKT, BF16), sds((16, BLOCK), F32)]
SCRATCH_A = [vm(TOK, F32), vm(TOK, BF16), vm(TOKT, BF16)] + [vm(TOK, BF16)] * 5 + [vm(TOKT, BF16)] * 3 + [
    vm(TOK, BF16), vm(TOKT, BF16), vm((3, 4, D // 4, D), BF16), pltpu.SemaphoreType.DMA((16,))]


def call_a(sid, hidden, time, vecs, wqkv):
    return pl.pallas_call(
        functools.partial(kernel_a, False),
        name="part_a",
        out_shape=OUT_A,
        in_specs=[SMEM, ANY, VMEM, VMEM, ANY],
        out_specs=[ANY] * 10 + [VMEM],
        scratch_shapes=SCRATCH_A,
        compiler_params=pltpu.CompilerParams(vmem_limit_bytes=VMEM_LIMIT),
    )(sid, hidden, time, vecs, wqkv.reshape(4, D // 4, 3 * D))


def call_a_links(sid, hidden, time, own):
    res = pl.pallas_call(
        functools.partial(kernel_a, True),
        name="part_a",
        out_shape=[sds((16, D), F32)] + OUT_A + [sds((4, 8 * a.shape[0], a.shape[1]), BF16) for a in own],
        in_specs=[SMEM, ANY, VMEM] + [VMEM] * 5,
        out_specs=[VMEM] + [ANY] * 10 + [VMEM] + [ANY] * 5,
        scratch_shapes=SCRATCH_A + [vm((4, 128, D), BF16), pltpu.SemaphoreType.DMA((6,)),
                                    pltpu.SemaphoreType.DMA((GATHER_SLOTS * 5,)), pltpu.SemaphoreType.DMA((GATHER_SLOTS * 5,))],
        compiler_params=pltpu.CompilerParams(vmem_limit_bytes=VMEM_LIMIT, collective_id=1, has_side_effects=True),
    )(sid, hidden, time, *own)
    return res[0], res[1:12], [a.reshape(-1, a.shape[-1]) for a in res[13:]]


def kernel_b(sid, x_h, o_h, gout_h, vecs, wout_h, win_h, wdown_h,
             out_h, gx1_h, gb_h, go0_h, go1_h, dots, gdown_h, gin_h, sums,
             x, o, gy, wout, win, wdown, gm, a2t, ht, gu, gb, go0, go1, stage, sems):
    mv = Mover(sems)
    cx, co, cg = mv.start(x_h, x), mv.start(o_h, o), mv.start(gout_h, gy)
    cwo = mv.start(wout_h, wout)
    cwi = [mv.start(win_h.at[:, pl.ds(D * j, D)], win.at[j]) for j in range(4)]
    cwd = [mv.start(wdown_h.at[pl.ds(D * j, D), :], wdown.at[j]) for j in range(4)]
    sums[...] = jnp.zeros_like(sums)
    for c in [cx, co, cg, cwo] + cwi + cwd:
        c.wait()
    lane = lax.broadcasted_iota(jnp.int32, (16, D), 1) // HEAD_DIM
    heads = (lane == lax.broadcasted_iota(jnp.int32, (16, D), 0)).astype(BF16)
    blocks = BLOCK // TB
    outs = []
    so = mv.sems

    def out_copies(i):
        at = rows_at(i, TB)
        return [pltpu.make_async_copy(x.at[at, :], out_h.at[at, :], so.at[16]),
                pltpu.make_async_copy(gy.at[at, :], gx1_h.at[at, :], so.at[17])]

    @pl.loop(0, blocks)
    def _(i):
        at = rows_at(i, TB)
        live = jnp.concatenate(
            [jnp.full((SHORT, 1), (sid[(TB // SHORT) * i + g] >= 0).astype(F32), F32) for g in range(TB // SHORT)], axis=0)
        x1 = x[at, :] + mm(o[at, :], wout[...]) + vecs[4:5, :]
        n2, r2 = normalize(x1)
        a2f = n2 * vecs[5:6, :] + vecs[6:7, :]
        a2 = a2f.astype(BF16)
        a2t[:, at] = a2f.T.astype(BF16)
        gyb = gy[at, :] * live
        gmb = gyb.astype(BF16)
        gm[at, :] = gmb
        acc = x1 + vecs[11:12, :]
        ga2 = jnp.zeros((TB, D), F32)
        for j in range(4):
            u = mm(a2, win[j]) + vecs[7 + j : 8 + j, :]
            hf, slope = gelu_parts(u)
            ht[D * j : D * j + D, at] = hf.T.astype(BF16)
            acc = acc + mm(hf.astype(BF16), wdown[j])
            guf = mm_t(gmb, wdown[j]) * slope
            gub = guf.astype(BF16)
            gu[at, D * j : D * j + D] = gub
            sums[4 + j] += fold8(gub.astype(F32))
            ga2 = ga2 + mm_t(gub, win[j])
        x[at, :] = acc * live
        sums[8] += fold8(gmb.astype(F32))
        sums[2] += fold8(ga2 * n2)
        sums[3] += fold8(ga2)
        gx1 = gyb + norm_back(ga2, vecs[5:6, :], n2, r2)
        gy[at, :] = gx1
        for c in out_copies(i):
            c.start()
        gbb = gx1.astype(BF16)
        gb[at, :] = gbb
        sums[1] += fold8(gbb.astype(F32))
        go = mm_t(gbb, wout[...]).astype(BF16).astype(F32)
        prod = go * o[at, :].astype(F32)
        hi = prod.astype(BF16)
        lo = (prod - hi.astype(F32)).astype(BF16)
        dots[:, at] = mm_t(heads, hi) + mm_t(heads, lo)
        low = lax.rem(lax.broadcasted_iota(jnp.int32, (TB, D), 1), 128) < 64
        go0[at, :] = jnp.where(low, go, 0.0).astype(BF16)
        go1[at, :] = jnp.where(low, 0.0, go).astype(BF16)

    outs += [mv.start(gb, gb_h), mv.start(go0, go0_h), mv.start(go1, go1_h)]

    def tile_out(j, slot):
        return pltpu.make_async_copy(stage.at[slot], gdown_h.at[rows_at(j, D), :], so.at[18 + slot])

    def tile_in(j, slot):
        return pltpu.make_async_copy(stage.at[slot], gin_h.at[:, pl.ds(D * j, D)], so.at[18 + slot])

    pending = [None, None]
    for t in range(8):
        slot, j = t % 2, t % 4
        if pending[slot] is not None:
            pending[slot].wait()

        @pl.loop(0, D // TB)
        def _(r):
            if t < 4:
                stage[slot, rows_at(r, TB), :] = mm(ht[pl.ds(pl.multiple_of(D * j + r * TB, TB), TB), :], gm[...]).astype(BF16)
            else:
                stage[slot, rows_at(r, TB), :] = mm(a2t[rows_at(r, TB), :], gu[:, D * j : D * j + D]).astype(BF16)

        pending[slot] = tile_out(j, slot) if t < 4 else tile_in(j, slot)
        pending[slot].start()
    for c in pending:
        c.wait()
    for c in outs:
        c.wait()
    for i in range(blocks):
        for c in out_copies(i):
            c.wait()


def call_b(sid, x, o, gout, vecs, wout, win, wdown):
    out = [sds(TOK, F32), sds(TOK, F32)] + [sds(TOK, BF16)] * 3 + [sds((16, BLOCK), F32), sds((FF, D), BF16), sds((D, FF), BF16), sds((9, 8, D), F32)]
    return pl.pallas_call(
        kernel_b,
        name="part_b",
        out_shape=out,
        in_specs=[SMEM, ANY, ANY, ANY, VMEM, ANY, ANY, ANY],
        out_specs=[ANY] * 5 + [VMEM, ANY, ANY, VMEM],
        scratch_shapes=[vm(TOK, F32), vm(TOK, BF16), vm(TOK, F32), vm((D, D), BF16), vm((4, D, D), BF16), vm((4, D, D), BF16),
                        vm(TOK, BF16), vm(TOKT, BF16), vm((FF, BLOCK), BF16), vm((BLOCK, FF), BF16),
                        vm(TOK, BF16), vm(TOK, BF16), vm(TOK, BF16), vm((2, D, D), BF16), pltpu.SemaphoreType.DMA((20,))],
        compiler_params=pltpu.CompilerParams(vmem_limit_bytes=VMEM_LIMIT),
    )(sid, x, o, gout, vecs, wout, win, wdown)


def attention_back_step(step, q0, q1, k0, k1, v, kt, go0, go1, lse, dots, gk_acc, gv_acc, gqkv):
    parts = BLOCK // QB
    pair, part = step // parts, step % parts
    lanes, at = rows_at(pair, 128), rows_at(part, QB)
    gk_parts, gq_parts, pbs = [], [], []
    vv = v[:, lanes]
    for h, (q, k, go) in enumerate(((q0, k0, go0), (q1, k1, go1))):
        scores = mm_t(k[:, lanes], q[at, lanes])
        p = jnp.exp(scores - lse[pl.ds(2 * pair + h, 1), at])
        gp = mm_t(vv, go[at, lanes])
        gs = (p * (gp - dots[pl.ds(2 * pair + h, 1), at])).astype(BF16)
        pbs.append(mm(p.astype(BF16), go[at, lanes]))
        gk_parts.append(mm(gs, q[at, lanes]))
        gq_parts.append(mm(kt[lanes, :], gs))
    gk = jnp.where(low_lanes((BLOCK, 128)), gk_parts[0], gk_parts[1])
    gv = pbs[0] + pbs[1]
    gq = jnp.where(low_rows((128, QB)), gq_parts[0], gq_parts[1]) * (HEAD_DIM**-0.5)
    gqkv[0, at, lanes] = gq.T.astype(BF16)
    first = part == 0
    gk_acc[...] = jnp.where(first, gk, gk_acc[...] + gk)
    gv_acc[...] = jnp.where(first, gv, gv_acc[...] + gv)

    @pl.when(part == parts - 1)
    def _():
        gqkv[1, :, lanes] = gk_acc[...].astype(BF16)
        gqkv[2, :, lanes] = gv_acc[...].astype(BF16)


def kernel_c(linked, sid, x_h, a1t_h, q0_h, q1_h, k0_h, k1_h, v_h, kt_h, ot_h, lse, gx1_h, gb_h, go0_h, go1_h, dots, vecs, wqkv_h, *refs):
    if linked:
        parts, refs = refs[:2], refs[2:]
    (ig_h, tg, gqkvw_h, goutw_h, sums), refs = refs[:5], refs[5:]
    if linked:
        owns, refs = refs[:2], refs[2:]
    (x, a1t, q0, q1, k0, k1, v, kt, ot, gx1, gb, go0, go1, w, gqkv, gk_acc, gv_acc, gw, gwo, tsum, sems), refs = refs[:21], refs[21:]
    hooks, rest = {}, []
    if linked:
        bufs, (local_sems, send, recv) = refs[:14], refs[14:]
        peers = Peers()
        links = Links(peers, send, recv)
        peers.greet()
        down, inn = [Scatter(n, links, parts[n], owns[n], bufs[7 * n : 7 * n + 7], local_sems.at[n]) for n in range(2)]
        down.begin()
        inn.begin()
        hooks = {0: down.first, 2: inn.first, 5: down.second, 9: inn.second, 13: down.third, 17: inn.third}
        rest = [down.last, inn.last, links.finish]
    mv = Mover(sems)
    early = [mv.start(s, d) for s, d in ((ot_h, ot), (gb_h, gb), (q0_h, q0), (q1_h, q1), (k0_h, k0), (k1_h, k1), (v_h, v), (kt_h, kt), (go0_h, go0), (go1_h, go1))]
    late = [mv.start(a1t_h, a1t), mv.start(x_h, x), mv.start(gx1_h, gx1)]
    late += [mv.start(wqkv_h.at[:, pl.ds(D * j, D)], w.at[j]) for j in range(3)]
    for c in early[:2]:
        c.wait()
    sums[...] = jnp.zeros_like(sums)

    @pl.loop(0, D // TB)
    def _(r):
        gwo[rows_at(r, TB), :] = mm(ot[rows_at(r, TB), :], gb[...]).astype(BF16)

    outs = [mv.start(gwo, goutw_h)]
    for c in early[2:]:
        c.wait()

    @pl.loop(0, PAIRS * (BLOCK // QB))
    def _(step):
        attention_back_step(step, q0, q1, k0, k1, v, kt, go0, go1, lse, dots, gk_acc, gv_acc, gqkv)
        run_hooks(step, hooks)

    for c in late:
        c.wait()
    for j in range(3):
        @pl.loop(0, D // TB)
        def _(r):
            gw[j, rows_at(r, TB), :] = mm(a1t[rows_at(r, TB), :], gqkv[j]).astype(BF16)

        outs.append(mv.start(gw.at[j], gqkvw_h.at[:, pl.ds(D * j, D)]))
    gain = vecs[0:1, :]

    @pl.loop(0, BLOCK // TB)
    def _(i):
        at = rows_at(i, TB)
        ga1 = mm_t(gqkv[0, at, :], w[0]) + mm_t(gqkv[1, at, :], w[1]) + mm_t(gqkv[2, at, :], w[2])
        sums[2] += fold8(gqkv[0, at, :].astype(F32))
        sums[3] += fold8(gqkv[2, at, :].astype(F32))
        n1, r1 = normalize(x[at, :])
        sums[0] += fold8(ga1 * n1)
        sums[1] += fold8(ga1)
        total = gx1[at, :] + norm_back(ga1, gain, n1, r1)
        for g in range(TB // SHORT):
            s = sid[(TB // SHORT) * i + g]
            live = (s >= 0).astype(F32)
            part = total[SHORT * g : SHORT * g + SHORT, :] * live
            x[rows_at((TB // SHORT) * i + g, SHORT), :] = part
            tsum[pl.ds((TB // SHORT) * i + g, 1), :] = jnp.sum(part, axis=0, keepdims=True)

    outs.append(mv.start(x, ig_h))
    row = lax.broadcasted_iota(jnp.int32, (GROUPS, D), 0)
    acc = jnp.zeros((GROUPS, D), F32)
    for g in range(GROUPS):
        acc = acc + jnp.where(row == sid[g], tsum[g : g + 1, :], 0.0)
    tg[...] = acc
    for action in rest:
        action()
    for c in outs:
        c.wait()


def call_c(linked, *args):
    out = [sds(TOK, F32), sds((GROUPS, D), F32), sds((D, 3 * D), BF16), sds((D, D), BF16), sds((4, 8, D), F32)]
    in_specs = [SMEM] + [ANY] * 9 + [VMEM] + [ANY] * 4 + [VMEM, VMEM, ANY]
    out_specs = [ANY, VMEM, ANY, ANY, VMEM]
    scratch = [vm(TOK, F32), vm(TOKT, BF16)] + [vm(TOK, BF16)] * 5 + [vm(TOKT, BF16)] * 2 + [vm(TOK, F32)] + [vm(TOK, BF16)] * 3
    scratch += [vm((3, D, D), BF16), vm((3, BLOCK, D), BF16), vm((BLOCK, 128), F32), vm((BLOCK, 128), F32), vm((3, D, D), BF16), vm((D, D), BF16),
                vm((GROUPS, D), F32), pltpu.SemaphoreType.DMA((24,))]
    extra = {}
    if linked:
        args, parts = args[:-2], args[-2:]
        shapes = [(p.shape[0] // 32, p.shape[1]) for p in parts]
        args = args + tuple(p.reshape(4, 4, 2, r, p.shape[1]) for p, (r, _) in zip(parts, shapes))
        in_specs += [ANY] * 2
        out += [sds(s, F32) for s in shapes]
        out_specs += [VMEM] * 2
        scratch += [b for s in shapes for b in scatter_bufs(*s)]
        scratch += [pltpu.SemaphoreType.DMA((n,)) for n in (2, 2 * SCATTER_SLOTS, 2 * SCATTER_SLOTS)]
        extra = dict(collective_id=3, has_side_effects=True)
    return pl.pallas_call(
        functools.partial(kernel_c, linked),
        name="part_c",
        out_shape=out,
        in_specs=in_specs,
        out_specs=out_specs,
        scratch_shapes=scratch,
        compiler_params=pltpu.CompilerParams(vmem_limit_bytes=VMEM_LIMIT, **extra),
    )(*args)


AXES = ("dp", "fsdp")
MESH = pl.DeviceIdType.MESH
SMALL = ((0, 24, 0), (24, 24, 1), (48, 48, 2), (96, 24, 4), (120, 24, 5), (144, 24, 6), (168, 96, 7), (264, 24, 11))
SMALL_LEN = 384


class Peers:
    def __init__(self):
        self.z, self.f = lax.axis_index("dp"), lax.axis_index("fsdp")
        self.c = self.f % 2
        self.yx = self.f // 2
        x, y = self.yx % 2, self.yx // 2
        self.partner = self.f + 1 - 2 * self.c
        self.fx, self.fy = self.f + 2 - 4 * x, self.f + 4 - 8 * y
        self.fd = self.fx + 4 - 8 * y
        self.qx, self.qy, self.qd = self.fx // 2, self.fy // 2, self.fd // 2
        self.dev = self.z * 8 + self.f
        self.other = 1 - self.c
        self.ups = [(self.z + d) % 4 for d in range(4)]

    def up(self, d):
        return self.ups[d]

    def at(self, name, d=0):
        if name == "z":
            return (self.up(d), self.f)
        return (self.z, {"x": self.fx, "y": self.fy, "p": self.partner}[name])

    def greet(self):
        barrier = pltpu.get_barrier_semaphore()
        for target in [self.at("p"), self.at("x"), self.at("y")] + [self.at("z", d) for d in (1, 2, 3)]:
            pl.semaphore_signal(barrier, inc=1, device_id=target, device_id_type=MESH)
        pl.semaphore_wait(barrier, 6)


class View:
    def __init__(self, ref, *index):
        self.ref, self.index = ref, index

    def get(self):
        return self.ref.at[self.index] if self.index else self.ref


class Links:
    def __init__(self, peers, send, recv):
        self.peers, self.send, self.recv = peers, send, recv
        self.slots, self.sent = {}, []

    def copy(self, key, src, dst, target):
        n = self.slots.setdefault(key, len(self.slots))
        return pltpu.make_async_remote_copy(
            src_ref=src.get(), dst_ref=dst.get(), send_sem=self.send.at[n], recv_sem=self.recv.at[n],
            device_id=target, device_id_type=MESH)

    def start(self, key, src, dst, name, d=0):
        args = (key, src, dst, self.peers.at(name, d))
        self.copy(*args).start()
        self.sent.append(args)

    def arrived(self, key, dst):
        self.copy(key, dst, dst, self.peers.at("p")).wait_recv()

    def finish(self):
        for args in self.sent:
            self.copy(*args).wait_send()
        self.sent = []


GATHER_SLOTS = 19


class Gather:
    def __init__(self, name, links, own, full, sem):
        self.name, self.links, self.own, self.full, self.sem = name, links, View(own), full, sem
        p, self.rows = links.peers, own.shape[0]
        self.at = {n: pl.multiple_of(f * self.rows, 8) for n, f in (("f", p.f), ("x", p.fx), ("y", p.fy), ("d", p.fd))}
        self.across = {n: pl.multiple_of((f + 1 - 2 * p.c) * self.rows, 8)
                       for n, f in (("f", p.f), ("x", p.fx), ("y", p.fy), ("d", p.fd))}

    def key(self, *k):
        return (self.name,) + k

    def piece(self, d, n):
        return View(self.full, self.links.peers.up((4 - d) % 4), pl.ds(self.at[n], self.rows))

    def column(self, at):
        return View(self.full, slice(None), pl.ds(at, self.rows))

    def begin(self):
        here = self.piece(0, "f")
        for d in (1, 3, 2):
            self.links.start(self.key("z", d), self.own, here, "z", d)
        self.local_copy().start()

    def local_copy(self):
        return pltpu.make_async_copy(self.own.get(), self.piece(0, "f").get(), self.sem)

    def first(self, ds=(0, 1, 3, 2)):
        links = self.links
        for d in ds:
            piece = self.piece(d, "f")
            if d:
                links.arrived(self.key("z", d), piece)
            src = piece if d else self.own
            links.start(self.key("x", d), src, piece, "x")
            links.start(self.key("y", d), src, piece, "y")
        if 2 in ds:
            self.local_copy().wait()
            mine = self.column(self.at["f"])
            links.start(self.key("p", "f"), mine, mine, "p")

    def first_own(self):
        self.first((0,))

    def first_rest(self):
        self.first((1, 3, 2))

    def second(self):
        links = self.links
        for d in (0, 1, 3, 2):
            px, py = self.piece(d, "x"), self.piece(d, "y")
            links.arrived(self.key("x", d), px)
            links.arrived(self.key("y", d), py)
            if d < 2:
                links.start(self.key("d", d), px, px, "y")
            else:
                links.start(self.key("d", d), py, py, "x")
        for n in ("x", "y"):
            part = self.column(self.at[n])
            links.start(self.key("p", n), part, part, "p")

    def third(self):
        for d in range(4):
            self.links.arrived(self.key("d", d), self.piece(d, "d"))
        part = self.column(self.at["d"])
        self.links.start(self.key("p", "d"), part, part, "p")

    def last(self):
        for n in ("f", "x", "y", "d"):
            self.links.arrived(self.key("p", n), self.column(self.across[n]))


SCATTER_SLOTS = 10


class Scatter:
    def __init__(self, name, links, parts, out, bufs, sem):
        self.name, self.links, self.parts, self.out, self.sem = name, links, parts, out, sem
        self.t, self.p, self.dx, self.dy, self.xr, self.yr, self.zr = bufs

    def key(self, *k):
        return (self.name,) + k

    def begin(self):
        p = self.links.peers
        self.links.start(self.key("p"), View(self.parts, slice(None), slice(None), p.other), View(self.p), "p")
        self.local_copy().start()

    def local_copy(self):
        return pltpu.make_async_copy(self.parts.at[:, :, self.links.peers.c], self.t, self.sem)

    def add(self, q, zs, ref, base=0):
        t = self.t

        @pl.loop(zs[0], zs[1])
        def _(i):
            t[i, q] = (t[i, q].astype(F32) + ref(i - base).astype(F32)).astype(BF16)

    def first(self):
        p, links, t = self.links.peers, self.links, self.t
        self.local_copy().wait()
        links.arrived(self.key("p"), View(self.p))
        self.add(p.qd, (0, 4), lambda i: self.p[i, p.qd])
        links.start(self.key("dx"), View(t, pl.ds(0, 2), p.qd), View(self.dx), "x")
        links.start(self.key("dy"), View(t, pl.ds(2, 2), p.qd), View(self.dy), "y")
        self.add(p.qx, (0, 4), lambda i: self.p[i, p.qx])
        links.start(self.key("x", 0), View(t, pl.ds(0, 2), p.qx), View(self.xr, pl.ds(0, 2)), "x")
        self.add(p.qy, (0, 4), lambda i: self.p[i, p.qy])
        links.start(self.key("y", 1), View(t, pl.ds(2, 2), p.qy), View(self.yr, pl.ds(2, 2)), "y")
        self.add(p.yx, (0, 4), lambda i: self.p[i, p.yx])

    def second(self):
        p, links, t = self.links.peers, self.links, self.t
        links.arrived(self.key("dy"), View(self.dy))
        self.add(p.qx, (2, 4), lambda i: self.dy[i], 2)
        links.start(self.key("x", 1), View(t, pl.ds(2, 2), p.qx), View(self.xr, pl.ds(2, 2)), "x")
        links.arrived(self.key("dx"), View(self.dx))
        self.add(p.qy, (0, 2), lambda i: self.dx[i])
        links.start(self.key("y", 0), View(t, pl.ds(0, 2), p.qy), View(self.yr, pl.ds(0, 2)), "y")

    def third(self):
        p, links, t = self.links.peers, self.links, self.t
        for n in range(2):
            links.arrived(self.key("x", n), View(self.xr, pl.ds(2 * n, 2)))
            links.arrived(self.key("y", n), View(self.yr, pl.ds(2 * n, 2)))

        @pl.loop(0, 4)
        def _(i):
            t[i, p.yx] = (t[i, p.yx].astype(F32) + self.xr[i].astype(F32) + self.yr[i].astype(F32)).astype(BF16)

        for d in (2, 1, 3):
            links.start(self.key("z", d), View(t, p.up(d), p.yx), View(self.zr, d - 1), "z", d)

    def last(self):
        p, links = self.links.peers, self.links
        for d in (1, 2, 3):
            links.arrived(self.key("z", d), View(self.zr, d - 1))
        total = self.t[p.z, p.yx].astype(F32)
        for n in range(3):
            total = total + self.zr[n].astype(F32)
        self.out[...] = total


def scatter_bufs(rows, cols):
    return [pltpu.VMEM(lead + (rows, cols), BF16) for lead in ((4, 4), (4, 4), (2,), (2,), (4,), (4,), (3,))]


class SmallSum:
    def __init__(self, links, value, bufs):
        self.links, self.value, self.bufs = links, value, bufs

    def send(self, n, name):
        self.links.start(("s", n), View(self.value, n), View(self.bufs, n), name)

    def take(self, n):
        self.links.arrived(("s", n), View(self.bufs, n))
        self.value[n + 1] = self.value[n] + self.bufs[n]

    def spread(self):
        for d in (1, 2, 3):
            self.links.start(("s", 2 + d), View(self.value, 3), View(self.bufs, 2 + d), "z", d)

    def total(self):
        for d in (1, 2, 3):
            self.links.arrived(("s", 2 + d), View(self.bufs, 2 + d))
        return self.value[3] + self.bufs[3] + self.bufs[4] + self.bufs[5]


def small_places(dev):
    i = lax.broadcasted_iota(jnp.int32, (1, SMALL_LEN), 1)
    row, col = jnp.full((1, SMALL_LEN), 15, jnp.int32), jnp.full((1, SMALL_LEN), -1, jnp.int32)
    for start, n, base in SMALL:
        here = (i >= start) & (i < start + n)
        row = jnp.where(here, base + (dev * n) // D, row)
        col = jnp.where(here, (dev * n) % D + i - start, col)
    return row, col


def small_select(col):
    return (lax.broadcasted_iota(jnp.int32, (D, SMALL_LEN), 0) == col).astype(F32)


def kernel_prep(small, wqkv, wout, win, wdown, small_o, qkv_o, out_o, in_o, down_o):
    row, col = small_places(lax.axis_index("dp") * 8 + lax.axis_index("fsdp"))
    at_row = lax.broadcasted_iota(jnp.int32, (16, SMALL_LEN), 0) == row
    values = jnp.where(at_row, small[...].astype(BF16).astype(F32), 0.0).astype(BF16)
    small_o[...] = mm_t(values, small_select(col).astype(BF16)).astype(BF16)
    qkv_o[...] = wqkv[...].astype(BF16)
    out_o[...] = wout[...].astype(BF16)
    in_o[...] = win[...].astype(BF16)
    down_o[...] = wdown[...].astype(BF16)


def call_prep(small, weights):
    return pl.pallas_call(
        kernel_prep, name="prep",
        out_shape=[sds((16, D), BF16)] + [sds(w.shape, BF16) for w in weights],
        in_specs=[VMEM] * 5, out_specs=[VMEM] * 5,
    )(small, *weights)


def sum_small(gathered, staged, sem, vecs):
    copy = pltpu.make_async_copy(gathered, staged, sem)
    copy.start()
    copy.wait()
    total = jnp.zeros((16, D), F32)
    for i in range(4):
        for j in range(8):
            total = total + staged[i, 16 * j : 16 * j + 16, :].astype(F32)
    vecs[...] = total


def kernel_scatter(sums_b, sums_c, out, qkv, small_o, out_o, qkv_o, value, small_b, *rest):
    bufs, (sems, send, recv) = rest[:14], rest[14:]
    peers = Peers()
    links = Links(peers, send, recv)
    pick = lambda ref, n: jnp.sum(ref[n], axis=0, keepdims=True)
    rows = [pick(sums_c, n) for n in range(4)] + [pick(sums_b, n) for n in range(1, 9)] + [jnp.zeros((4, D), F32)]
    value[0] = jnp.concatenate(rows, axis=0)
    peers.greet()
    small = SmallSum(links, value, small_b)
    s = [Scatter(n, links, parts, o, bufs[7 * n : 7 * n + 7], sems.at[n]) for n, (parts, o) in enumerate(((out, out_o), (qkv, qkv_o)))]
    s[0].begin()
    s[1].begin()
    small.send(0, "p")
    s[0].first()
    small.take(0)
    small.send(1, "x")
    s[1].first()
    small.take(1)
    small.send(2, "y")
    s[0].second()
    s[1].second()
    small.take(2)
    small.spread()
    s[0].third()
    s[1].third()
    total = small.total()
    row, col = small_places(peers.dev)
    picked = lax.dot_general(total, small_select(col), (((1,), (0,)), ((), ())),
                             precision=lax.Precision.HIGHEST, preferred_element_type=F32)
    at_row = lax.broadcasted_iota(jnp.int32, (16, SMALL_LEN), 0) == row
    small_o[...] = jnp.sum(jnp.where(at_row, picked, 0.0), axis=0, keepdims=True)
    s[0].last()
    s[1].last()
    links.finish()


def call_scatter(sums_b, sums_c, parts):
    shapes = [(p.shape[0] // 32, p.shape[1]) for p in parts]
    parts = [p.reshape(4, 4, 2, r, p.shape[1]) for p, (r, _) in zip(parts, shapes)]
    bufs = [b for s in shapes for b in scatter_bufs(*s)]
    slots = SCATTER_SLOTS * len(parts) + 6
    return pl.pallas_call(
        kernel_scatter, name="scatter",
        out_shape=[sds((1, SMALL_LEN), F32)] + [sds(s, F32) for s in shapes],
        in_specs=[VMEM, VMEM] + [ANY] * 2, out_specs=[VMEM] * 3,
        scratch_shapes=[vm((4, 16, D), F32), vm((6, 16, D), F32)] + bufs
        + [pltpu.SemaphoreType.DMA((2,)), pltpu.SemaphoreType.DMA((slots,)), pltpu.SemaphoreType.DMA((slots,))],
        compiler_params=pltpu.CompilerParams(vmem_limit_bytes=VMEM_LIMIT, collective_id=2, has_side_effects=True),
    )(sums_b, sums_c, *parts)


def gather_all(a):
    return lax.all_gather(a.astype(BF16), AXES, axis=0, tiled=True)


def scatter_sum(a):
    return lax.psum_scatter(a, AXES, scatter_dimension=0, tiled=True)


def split_small(row, small):
    parts, at = [], 0
    for s in small:
        parts.append(row[at : at + s.shape[0]])
        at += s.shape[0]
    return parts


def gather_plain(small, weights):
    every = lax.all_gather(jnp.concatenate([s.astype(BF16) for s in small]), AXES, axis=0, tiled=False)
    vecs, at = [], 0
    for s in small:
        vecs.append(every[:, at : at + s.shape[0]].reshape(-1, D))
        at += s.shape[0]
    vecs = jnp.concatenate(vecs + [jnp.zeros((4, D), BF16)], axis=0).astype(F32)
    return vecs, [gather_all(w) for w in weights]


def scatter_plain(sums_b, sums_c, grads, small):
    sb, sc = jnp.sum(sums_b, axis=1), jnp.sum(sums_c, axis=1)
    vectors = (sc[0], sc[1], sc[2:4].reshape(-1), sb[1], sb[2], sb[3], sb[4:8].reshape(-1), sb[8])
    devices = D // small[0].shape[0]
    packed = jnp.concatenate([g.reshape(devices, -1) for g in vectors], axis=1)
    return scatter_sum(packed).reshape(-1), [scatter_sum(g.astype(F32)) for g in grads]


def local(
    own_links,
    hidden_in, time_embed, seg_ids, pre_gain, pre_shift, qkv_weight, qv_bias, out_weight, out_bias,
    mid_gain, mid_shift, in_weight, in_bias, down_weight, down_bias, grad_out,
):
    sid = seg_ids.reshape(GROUPS, SHORT)[:, 0]
    small = (pre_gain, pre_shift, qv_bias, out_bias, mid_gain, mid_shift, in_bias, down_bias)
    weights = (qkv_weight, out_weight, in_weight, down_weight)
    if own_links:
        row = jnp.concatenate(small + (jnp.zeros((SMALL_LEN - 288,), F32),)).reshape(1, SMALL_LEN)
        vecs, made, (wqkv, wout, win, wdown) = call_a_links(sid, hidden_in, time_embed, call_prep(row, weights))
    else:
        vecs, (wqkv, wout, win, wdown) = gather_plain(small, weights)
        made = call_a(sid, hidden_in, time_embed, vecs, wqkv)
    x, a1t, q0, q1, k0, k1, v, kt, o, ot, lse = made
    block_out, gx1, gb, go0, go1, dots, gdown, gin, sums_b = call_b(sid, x, o, grad_out, vecs, wout, win, wdown)
    args_c = (sid, x, a1t, q0, q1, k0, k1, v, kt, ot, lse, gx1, gb, go0, go1, dots, vecs, wqkv)
    if own_links:
        input_grad, time_grad, gqkv, gout, sums_c, gdown, gin = call_c(True, *args_c, gdown, gin)
        mine, gout, gqkv = call_scatter(sums_b, sums_c, (gout, gqkv))
        mine = mine.reshape(-1)
    else:
        input_grad, time_grad, gqkv, gout, sums_c = call_c(False, *args_c)
        mine, (gdown, gin, gout, gqkv) = scatter_plain(sums_b, sums_c, (gdown, gin, gout, gqkv), small)
    gpg, gps, gqvb, gob, gmg, gms, gib, gdb = split_small(mine, small)
    return (block_out, input_grad, time_grad, gpg, gps, gqkv, gqvb, gout, gob, gmg, gms, gin, gib, gdown, gdb)


def solution(mesh):
    rows, flat = P(AXES, None), P(AXES)
    own_links = dict(mesh.shape) == {"dp": 4, "fsdp": 8}
    return jax.shard_map(
        functools.partial(local, own_links),
        mesh=mesh,
        in_specs=(rows, rows, flat, flat, flat, rows, flat, rows, flat, flat, flat, rows, flat, rows, flat, rows),
        out_specs=(rows, rows, rows, flat, flat, rows, flat, rows, flat, flat, flat, rows, flat, rows, flat),
        check_vma=False,
    )
```

```python
import functools

import jax
import jax.numpy as jnp
from jax import lax
from jax.experimental import pallas as pl
from jax.experimental.pallas import tpu as pltpu
from jax.sharding import PartitionSpec as P

D = 768
HEADS = 12
HEAD_DIM = 64
FF = 3072
BLOCK = 1024
SHORT = 64
GROUPS = BLOCK // SHORT
PAIRS = HEADS // 2
TB = 256
NEG = -1e30
F32 = jnp.float32
BF16 = jnp.bfloat16
VMEM_LIMIT = 62 * 1024 * 1024
ANY = pl.BlockSpec(memory_space=pl.ANY)
VMEM = pl.BlockSpec(memory_space=pltpu.VMEM)
SMEM = pl.BlockSpec(memory_space=pltpu.SMEM)
ERFC_SCALE = 0.44
ERFC_POLY = (
    0.24822097621403005,
    0.2488708795734658,
    0.21731516533725015,
    0.21580763970434977,
    -0.020173037922183695,
    0.2966799647080617,
    -0.2779439059726245,
    0.07122249905985603,
)


def rows_at(i, size):
    return pl.ds(pl.multiple_of(i * size, size), size)


def mm(a, b):
    return lax.dot_general(a, b, (((1,), (0,)), ((), ())), preferred_element_type=F32)


def mm_t(a, b):
    return lax.dot_general(a, b, (((1,), (1,)), ((), ())), preferred_element_type=F32)


def normalize(v):
    center = v - jnp.mean(v, axis=-1, keepdims=True)
    spread = jnp.mean(center * center, axis=-1, keepdims=True)
    scale = lax.rsqrt(spread + 1e-05)
    return center * scale, scale


def norm_back(grad, gain, n, scale):
    g = grad * gain
    return scale * (
        g - jnp.mean(g, axis=-1, keepdims=True) - n * jnp.mean(g * n, axis=-1, keepdims=True)
    )


def fold8(v):
    return jnp.sum(v.reshape(v.shape[0] // 8, 8, v.shape[1]), axis=0)


def gelu_parts(u):
    z = jnp.abs(u) * 0.7071067811865476
    t = 1.0 / (1.0 + ERFC_SCALE * z)
    poly = jnp.full_like(t, ERFC_POLY[-1])
    for c in ERFC_POLY[-2::-1]:
        poly = poly * t + c
    e = jnp.exp(-(z * z))
    tail = 0.5 * poly * t * e
    phi = jnp.where(u >= 0, 1.0 - tail, tail)
    return u * phi, phi + u * e * 0.3989422804014327


class Mover:
    def __init__(self, sems):
        self.sems, self.next = sems, 0

    def start(self, src, dst):
        copy = pltpu.make_async_copy(src, dst, self.sems.at[self.next])
        self.next += 1
        copy.start()
        return copy


def run_hooks(step, hooks):
    for n, actions in hooks.items():
        if not actions:
            continue

        @pl.when(step == n)
        def _():
            for action in actions:
                action()


def stage_norm1(sid, time, vecs, x, a1, a1t, hooks):
    gain, shift = vecs[0:1, :], vecs[1:2, :]

    @pl.loop(0, BLOCK // 128)
    def _(i):
        parts = []
        for half in range(2):
            s = sid[2 * i + half]
            live = (s >= 0).astype(F32)
            row = time[pl.ds(jnp.maximum(s, 0), 1), :]
            parts.append((x[rows_at(2 * i + half, SHORT), :] + row) * live)
        block = jnp.concatenate(parts, axis=0)
        at = rows_at(i, 128)
        x[at, :] = block
        n, _ = normalize(block)
        a = n * gain + shift
        a1[at, :] = a.astype(BF16)
        a1t[:, at] = a.T.astype(BF16)
        run_hooks(i, hooks)


def mask_rows(sid, i, groups):
    lane = lax.rem(lax.broadcasted_iota(jnp.int32, (SHORT, 128), 1), 64)
    mq, mk = [], []
    for g in range(groups):
        s = sid[groups * i + g]
        own = jnp.where(s >= 0, s, 16)
        mk.append((lane == own).astype(F32))
        bad = ((lane < 16) & (lane != s)) | (lane == 16)
        mq.append(jnp.where(bad, NEG, 0.0))
    return jnp.concatenate(mq, axis=0), jnp.concatenate(mk, axis=0)


def low_lanes(shape):
    return lax.broadcasted_iota(jnp.int32, shape, 1) < 64


def low_rows(shape):
    return lax.broadcasted_iota(jnp.int32, shape, 0) < 64


def stage_q(sid, vecs, a1, w, q0, q1, hooks):
    @pl.loop(0, BLOCK // TB)
    def _(i):
        at = rows_at(i, TB)
        mq, _ = mask_rows(sid, i, TB // SHORT)
        acc = mm(a1[at, :], w) + vecs[2:3, :]
        acc = acc.astype(BF16).astype(F32) * (HEAD_DIM**-0.5)
        low = low_lanes((TB, 128))
        for p in range(PAIRS):
            part = acc[:, 128 * p : 128 * p + 128]
            q0[at, 128 * p : 128 * p + 128] = jnp.where(low, part, mq).astype(BF16)
            q1[at, 128 * p : 128 * p + 128] = jnp.where(low, mq, part).astype(BF16)
        run_hooks(i, hooks)


def stage_k(sid, a1, w, k0, k1, kt, hooks):
    @pl.loop(0, BLOCK // TB)
    def _(i):
        at = rows_at(i, TB)
        _, mk = mask_rows(sid, i, TB // SHORT)
        acc = mm(a1[at, :], w)
        low = low_lanes((TB, 128))
        for p in range(PAIRS):
            part = acc[:, 128 * p : 128 * p + 128]
            k0[at, 128 * p : 128 * p + 128] = jnp.where(low, part, mk).astype(BF16)
            k1[at, 128 * p : 128 * p + 128] = jnp.where(low, mk, part).astype(BF16)
        kt[:, at] = acc.T.astype(BF16)
        run_hooks(i, hooks)


def stage_v(vecs, a1, w, v, vt0, vt1, hooks):
    @pl.loop(0, BLOCK // TB)
    def _(i):
        at = rows_at(i, TB)
        acc = mm(a1[at, :], w) + vecs[3:4, :]
        v[at, :] = acc.astype(BF16)
        accT = acc.T
        low = low_rows((128, TB))
        for p in range(PAIRS):
            part = accT[128 * p : 128 * p + 128, :]
            vt0[128 * p : 128 * p + 128, at] = jnp.where(low, part, 1.0).astype(BF16)
            vt1[128 * p : 128 * p + 128, at] = jnp.where(low, 1.0, part).astype(BF16)
        run_hooks(i, hooks)


QB = 256


def attention_step(step, q0, q1, k0, k1, vt0, vt1, o, ot, lse):
    pair, part = step // (BLOCK // QB), step % (BLOCK // QB)
    lanes, at = rows_at(pair, 128), rows_at(part, QB)
    outs, logs = [], []
    for q, k, vt, total_row in ((q0, k0, vt0, 64), (q1, k1, vt1, 0)):
        scores = mm_t(k[:, lanes], q[at, lanes])
        top = jnp.max(scores, axis=0, keepdims=True)
        e = jnp.exp(scores - top).astype(BF16)
        res = mm(vt[lanes, :], e)
        total = res[total_row : total_row + 1, :]
        outs.append(res * (1.0 / total))
        logs.append(top + jnp.log(total))
    both = jnp.where(low_rows((128, QB)), outs[0], outs[1])
    ot[lanes, at] = both.astype(BF16)
    o[at, lanes] = both.T.astype(BF16)
    lse[pl.ds(2 * pair, 1), at] = logs[0]
    lse[pl.ds(2 * pair + 1, 1), at] = logs[1]


SCHEDULE_A = {
    ("pre", 0): ("s.F0", "q.F0", "k.F0", "s.F1", "s.F3", "s.F2", "s.S0", "q.F1", "s.S1", "s.S3", "s.S2", "q.F3", "q.F2", "q.S0", "q.S1", "s.T", "k.F1", "q.S3", "k.F3", "s.L",),
    ("norm", 0): ("q.S2",),
    ("norm", 1): ("k.F2", "k.S0", "v.F0",),
    ("norm", 3): ("v.F1",),
    ("norm", 5): ("k.S1", "v.F3",),
    ("norm", 6): ("k.S3",),
    ("norm", 7): ("q.T", "v.F2", "o.F0",),
    ("q", -1): ("k.S2", "o.F1", "v.S0", "o.F3", "q.L",),
    ("q", 1): ("v.S1",),
    ("q", 2): ("o.F2",),
    ("k", -1): ("v.S3", "v.S2", "i.F0", "o.S0", "k.T", "o.S1", "i.F1", "k.L",),
    ("k", 1): ("o.S3",),
    ("v", -1): ("v.T", "o.S2", "i.F3", "v.L",),
    ("att", 1): ("i.F2", "i.S0", "d.F0",),
    ("att", 2): ("o.T", "i.S1",),
    ("att", 4): ("o.L", "d.F1",),
    ("att", 5): ("i.S3",),
    ("att", 7): ("i.S2", "d.F3",),
    ("att", 10): ("d.F2",),
    ("att", 11): ("d.S0",),
    ("att", 15): ("d.S1",),
    ("att", 16): ("i.T",),
    ("att", 18): ("d.S3",),
    ("att", 19): ("i.L",),
    ("att", 20): ("d.S2",),
    ("end", 0): ("d.T", "d.L",),
}
SCHEDULE_B = {
    ("gd", 1): ("x.B",),
    ("gd", 2): ("y.B",),
    ("wd", 0): ("z.B",),
    ("p2", 0): ("x.F", "y.F", "z.F",),
    ("p2", 1): ("x.S",),
    ("p2", 3): ("y.S",),
    ("p2", 4): ("z.S",),
    ("p2", 6): ("x.T", "y.T",),
    ("p2", 7): ("z.T",),
    ("gi", 1): ("x.L",),
    ("gi", 3): ("y.L",),
    ("end", 0): ("z.L",),
}
SCHEDULE_C = {
    ("pre", 0): ("0.B", "1.B", "2.B", "3.B",),
    ("att", 0): ("0.F", "1.F", "2.F", "3.F",),
    ("att", 1): ("o.B", "0.S",),
    ("att", 3): ("o.F", "1.S",),
    ("att", 4): ("2.S",),
    ("att", 6): ("3.S",),
    ("gw", 0): ("0.T",),
    ("att", 8): ("o.S",),
    ("att", 9): ("a.B", "1.T",),
    ("att", 10): ("2.T",),
    ("att", 11): ("a.F", "o.T", "0.L", "3.T",),
    ("att", 12): ("1.L",),
    ("att", 13): ("a.S",),
    ("att", 14): ("2.L",),
    ("gw", 1): ("a.T", "o.L",),
    ("att", 16): ("3.L",),
    ("att", 17): ("b.B",),
    ("att", 19): ("a.L", "b.F",),
    ("att", 22): ("b.S",),
    ("gw", 3): ("b.T", "c.B",),
    ("ln", 1): ("c.F",),
    ("ln", 2): ("b.L",),
    ("ln", 3): ("c.S",),
    ("end", 0): ("c.T", "c.L",),
}


class Schedule:
    def __init__(self, table):
        self.table, self.units = table, {}

    def actions(self, seg, step):
        found = self.table.get((seg, step), ()) if self.units else ()
        return [functools.partial(self.units[a[0]].do, a[2:]) for a in found]

    def hooks(self, seg, first=0, last=24):
        return {n: self.actions(seg, n) for n in range(first, last) if self.actions(seg, n)}

    def run(self, seg, step, part=slice(None)):
        for action in self.actions(seg, step)[part]:
            action()


def kernel_a(linked, sid, hidden, time, *refs):
    if linked:
        own, refs = refs[:5], refs[5:]
        vecs, refs = refs[0], refs[1:]
    else:
        (vecs, *wq), refs = refs[:4], refs[4:]
    (x_h, a1t_h, q0_h, q1_h, k0_h, k1_h, v_h, kt_h, o_h, ot_h, lse), refs = refs[:11], refs[11:]
    if linked:
        full, refs = refs[:7], refs[7:]
        wq = full[1:4]
    (x, a1, a1t, q0, q1, k0, k1, v, kt, vt0, vt1, o, ot, w, sems), refs = refs[:15], refs[15:]
    mv = Mover(sems)
    cx = mv.start(hidden, x)
    plan = Schedule(SCHEDULE_A)
    if linked:
        staged, local_sems, send, recv = refs
        peers = Peers()
        links = Links(peers, send, recv)
        peers.greet()
        small, qkv, out, inn, down = own
        pieces = [View(small)] + [View(qkv, slice(None), pl.ds(D * n, D)) for n in range(3)] + [View(out), View(inn), View(down)]
        rows = (small.shape[0], D // 32, D // 32, D // 32, D // 32, D // 32, FF // 32)
        for n, name in enumerate("sqkvoid"):
            plan.units[name] = Gather(n, links, pieces[n], rows[n], full[n], local_sems.at[n])
            plan.units[name].begin()
    run, hooks = plan.run, plan.hooks
    run("pre", 0)
    if linked:
        build_table(full[0], staged, local_sems.at[7], vecs)
    cx.wait()
    stage_norm1(sid, time, vecs, x, a1, a1t, hooks("norm"))
    outs = [mv.start(x, x_h), mv.start(a1t, a1t_h)]

    def weight(name, j):
        run(name, -1)
        copy = mv.start(wq[j], w.at[j])
        copy.wait()
        return w[j].reshape(D, D)

    stage_q(sid, vecs, a1, weight("q", 0), q0, q1, hooks("q"))
    outs += [mv.start(q0, q0_h), mv.start(q1, q1_h)]
    stage_k(sid, a1, weight("k", 1), k0, k1, kt, hooks("k"))
    outs += [mv.start(k0, k0_h), mv.start(k1, k1_h), mv.start(kt, kt_h)]
    stage_v(vecs, a1, weight("v", 2), v, vt0, vt1, hooks("v"))
    outs += [mv.start(v, v_h)]
    attention_hooks = hooks("att")

    @pl.loop(0, PAIRS * (BLOCK // QB))
    def _(step):
        attention_step(step, q0, q1, k0, k1, vt0, vt1, o, ot, lse)
        run_hooks(step, attention_hooks)

    outs += [mv.start(o, o_h), mv.start(ot, ot_h)]
    run("end", 0)
    for copy in outs:
        copy.wait()
    if linked:
        links.finish()


def sds(shape, dtype):
    return jax.ShapeDtypeStruct(shape, dtype)


TOK = (BLOCK, D)
TOKT = (D, BLOCK)


def vm(shape, dtype):
    return pltpu.VMEM(shape, dtype)


OUT_A = [sds(TOK, F32), sds(TOKT, BF16)] + [sds(TOK, BF16)] * 5 + [sds(TOKT, BF16), sds(TOK, BF16), sds(TOKT, BF16), sds((16, BLOCK), F32)]
SCRATCH_A = [vm(TOK, F32), vm(TOK, BF16), vm(TOKT, BF16)] + [vm(TOK, BF16)] * 5 + [vm(TOKT, BF16)] * 3 + [
    vm(TOK, BF16), vm(TOKT, BF16), vm((3, 4, D // 4, D), BF16), pltpu.SemaphoreType.DMA((16,))]


def call_a(sid, hidden, time, vecs, wq):
    return pl.pallas_call(
        functools.partial(kernel_a, False),
        name="part_a",
        out_shape=OUT_A,
        in_specs=[SMEM, ANY, VMEM, VMEM, ANY, ANY, ANY],
        out_specs=[ANY] * 10 + [VMEM],
        scratch_shapes=SCRATCH_A,
        compiler_params=pltpu.CompilerParams(vmem_limit_bytes=VMEM_LIMIT),
    )(sid, hidden, time, vecs, *[a.reshape(4, D // 4, D) for a in wq])


def call_a_links(sid, hidden, time, own):
    small, qkv, out, inn, down = own
    sizes = [small.shape] + [(D // 32, D)] * 4 + [inn.shape, down.shape]
    slots = GATHER_SLOTS * 7
    res = pl.pallas_call(
        functools.partial(kernel_a, True),
        name="part_a",
        out_shape=[sds((16, D), F32)] + OUT_A + [sds((4, 8 * r, c), BF16) for r, c in sizes],
        in_specs=[SMEM, ANY, VMEM] + [VMEM] * 5,
        out_specs=[VMEM] + [ANY] * 10 + [VMEM] + [ANY] * 7,
        scratch_shapes=SCRATCH_A + [vm((4, 64, SMALL_LEN), BF16)] + [pltpu.SemaphoreType.DMA((n,)) for n in (8, slots, slots)],
        compiler_params=pltpu.CompilerParams(vmem_limit_bytes=VMEM_LIMIT, collective_id=1, has_side_effects=True),
    )(sid, hidden, time, *own)
    full = [a.reshape(-1, a.shape[-1]) for a in res[13:]]
    return res[0], res[1:12], full[:3], full[3:]


def kernel_b(linked, sid, x_h, o_h, gout_h, vecs, wout_h, win_h, wdown_h,
             out_h, gx1_h, gb_h, go0_h, go1_h, dots, gdown_h, gin_h, sums, *refs):
    if linked:
        gdown_o, refs = refs[0], refs[1:]
    (x, o, gy, wout, win, wdown, gm, a2t, ht, h, gu, gb, go0, go1, stage_d, stage, sems), refs = refs[:17], refs[17:]
    plan = Schedule(SCHEDULE_B)
    if linked:
        bufs, (local_sems, send, recv) = refs[:21], refs[21:]
        peers = Peers()
        links = Links(peers, send, recv)
        peers.greet()
        for n, name in enumerate("xyz"):
            keep = functools.partial(store_lanes, gdown_o, ((0, DT * n, DT),))
            plan.units[name] = Scatter(n, links, (gdown_h, n), keep, bufs[7 * n : 7 * n + 7], local_sems.at[n])
    mv = Mover(sems)
    cx, co, cg = mv.start(x_h, x), mv.start(o_h, o), mv.start(gout_h, gy)
    cwo = mv.start(wout_h, wout)
    cwi = [mv.start(win_h.at[:, pl.ds(D * j, D)], win.at[j]) for j in range(4)]
    cwd = [mv.start(wdown_h.at[pl.ds(D * j, D), :], wdown.at[j]) for j in range(4)]
    sums[...] = jnp.zeros_like(sums)
    for c in [cx, co, cg, cwo] + cwi:
        c.wait()
    lane = lax.broadcasted_iota(jnp.int32, (16, D), 1) // HEAD_DIM
    heads = (lane == lax.broadcasted_iota(jnp.int32, (16, D), 0)).astype(BF16)
    blocks = BLOCK // TB
    outs = []
    so = mv.sems

    def out_copies(i):
        at = rows_at(i, TB)
        return [pltpu.make_async_copy(x.at[at, :], out_h.at[at, :], so.at[16]),
                pltpu.make_async_copy(gy.at[at, :], gx1_h.at[at, :], so.at[17])]

    def live_rows(i):
        return jnp.concatenate(
            [jnp.full((SHORT, 1), (sid[(TB // SHORT) * i + g] >= 0).astype(F32), F32) for g in range(TB // SHORT)], axis=0)

    @pl.loop(0, blocks)
    def _(i):
        at = rows_at(i, TB)
        x1 = x[at, :] + mm(o[at, :], wout[...]) + vecs[4:5, :]
        x[at, :] = x1
        n2, _ = normalize(x1)
        a2f = n2 * vecs[5:6, :] + vecs[6:7, :]
        a2 = a2f.astype(BF16)
        a2t[:, at] = a2f.T.astype(BF16)
        gyb = gy[at, :] * live_rows(i)
        gy[at, :] = gyb
        gm[at, :] = gyb.astype(BF16)
        for j in range(4):
            u = mm(a2, win[j]) + vecs[7 + j : 8 + j, :]
            hf, slope = gelu_parts(u)
            ht[D * j : D * j + D, at] = hf.T.astype(BF16)
            h[at, D * j : D * j + D] = hf.astype(BF16)
            gu[at, D * j : D * j + D] = slope.astype(BF16)

    pending = None
    for t in range(D // DT):
        if pending is not None:
            pending.wait()

        @pl.loop(0, FF // 384)
        def _(r):
            part = mm(ht[rows_at(r, 384), :], gm[:, DT * t : DT * t + DT]).astype(BF16)
            stage_d[r // 2, pl.ds(2 * (r % 2), 2)] = part.reshape(2, 192, DT)

        plan.run("gd", t)
        pending = pltpu.make_async_copy(stage_d, gdown_h.at[t], so.at[18])
        pending.start()
    for c in cwd:
        c.wait()
    pending.wait()
    plan.run("wd", 0)
    first_hooks, second_hooks = ({n: plan.actions("p2", n) for n in range(k, 2 * blocks, 2)} for k in range(2))

    @pl.loop(0, blocks)
    def _(i):
        at = rows_at(i, TB)
        n2, r2 = normalize(x[at, :])
        gmb = gm[at, :]
        acc = x[at, :] + vecs[11:12, :]
        ga2 = jnp.zeros((TB, D), F32)
        for j in range(4):
            acc = acc + mm(h[at, D * j : D * j + D], wdown[j])
            guf = mm_t(gmb, wdown[j]) * gu[at, D * j : D * j + D].astype(F32)
            gub = guf.astype(BF16)
            gu[at, D * j : D * j + D] = gub
            sums[4 + j] += fold8(gub.astype(F32))
            ga2 = ga2 + mm_t(gub, win[j])
        x[at, :] = acc * live_rows(i)
        run_hooks(2 * i, first_hooks)
        gyb = gy[at, :]
        sums[8] += fold8(gmb.astype(F32))
        sums[2] += fold8(ga2 * n2)
        sums[3] += fold8(ga2)
        gx1 = gyb + norm_back(ga2, vecs[5:6, :], n2, r2)
        gy[at, :] = gx1
        for c in out_copies(i):
            c.start()
        gbb = gx1.astype(BF16)
        gb[at, :] = gbb
        sums[1] += fold8(gbb.astype(F32))
        go = mm_t(gbb, wout[...]).astype(BF16).astype(F32)
        prod = go * o[at, :].astype(F32)
        hi = prod.astype(BF16)
        lo = (prod - hi.astype(F32)).astype(BF16)
        dots[:, at] = mm_t(heads, hi) + mm_t(heads, lo)
        low = lax.rem(lax.broadcasted_iota(jnp.int32, (TB, D), 1), 128) < 64
        go0[at, :] = jnp.where(low, go, 0.0).astype(BF16)
        go1[at, :] = jnp.where(low, 0.0, go).astype(BF16)
        run_hooks(2 * i + 1, second_hooks)

    outs += [mv.start(gb, gb_h), mv.start(go0, go0_h), mv.start(go1, go1_h)]
    copies = []
    for j in range(4):
        if j > 1:
            copies[j - 2].wait()

        @pl.loop(0, 2)
        def _(r):
            part = mm(a2t[rows_at(r, 384), :], gu[:, D * j : D * j + D]).astype(BF16)
            stage[j % 2, pl.ds(2 * r, 2)] = part.reshape(2, 4, 48, D)

        plan.run("gi", j)
        copies.append(pltpu.make_async_copy(stage.at[j % 2], gin_h.at[j], so.at[19 + j % 2]))
        copies[j].start()
    plan.run("end", 0)
    for c in copies[2:] + outs:
        c.wait()
    for i in range(blocks):
        for c in out_copies(i):
            c.wait()
    if linked:
        links.finish()


DT = 256


def store_lanes(out, places, total):
    for source, target, width in places:
        out[:, target : target + width] = total[:, source : source + width]


def call_b(linked, sid, x, o, gout, vecs, wout, win, wdown):
    out = [sds(TOK, F32), sds(TOK, F32)] + [sds(TOK, BF16)] * 3 + [
        sds((16, BLOCK), F32), sds((D // DT, 4, 4, 192, DT), BF16), sds((4, 4, 4, 48, D), BF16), sds((9, 8, D), F32)]
    out_specs = [ANY] * 5 + [VMEM, ANY, ANY, VMEM]
    scratch = [vm(TOK, F32), vm(TOK, BF16), vm(TOK, F32), vm((D, D), BF16), vm((4, D, D), BF16), vm((4, D, D), BF16),
               vm(TOK, BF16), vm(TOKT, BF16), vm((FF, BLOCK), BF16), vm((BLOCK, FF), BF16), vm((BLOCK, FF), BF16),
               vm(TOK, BF16), vm(TOK, BF16), vm(TOK, BF16), vm((4, 4, 192, DT), BF16), vm((2, 4, 4, 48, D), BF16), pltpu.SemaphoreType.DMA((21,))]
    extra = {}
    if linked:
        out.append(sds((FF // 32, D), F32))
        out_specs.append(VMEM)
        scratch += 3 * scatter_bufs(FF // 32, DT) + [pltpu.SemaphoreType.DMA((n,)) for n in (3, 3 * SCATTER_SLOTS, 3 * SCATTER_SLOTS)]
        extra = dict(collective_id=2, has_side_effects=True)
    return pl.pallas_call(
        functools.partial(kernel_b, linked),
        name="part_b",
        out_shape=out,
        in_specs=[SMEM, ANY, ANY, ANY, VMEM, ANY, ANY, ANY],
        out_specs=out_specs,
        scratch_shapes=scratch,
        compiler_params=pltpu.CompilerParams(vmem_limit_bytes=VMEM_LIMIT, **extra),
    )(sid, x, o, gout, vecs, wout, win, wdown)


def attention_back_step(step, q0, q1, k0, k1, v, kt, go0, go1, lse, dots, gk_acc, gv_acc, gqkv):
    parts = BLOCK // QB
    pair, part = step // parts, step % parts
    lanes, at = rows_at(pair, 128), rows_at(part, QB)
    gk_parts, gq_parts, pbs = [], [], []
    vv = v[:, lanes]
    for h, (q, k, go) in enumerate(((q0, k0, go0), (q1, k1, go1))):
        scores = mm_t(k[:, lanes], q[at, lanes])
        p = jnp.exp(scores - lse[pl.ds(2 * pair + h, 1), at])
        gp = mm_t(vv, go[at, lanes])
        gs = (p * (gp - dots[pl.ds(2 * pair + h, 1), at])).astype(BF16)
        pbs.append(mm(p.astype(BF16), go[at, lanes]))
        gk_parts.append(mm(gs, q[at, lanes]))
        gq_parts.append(mm(kt[lanes, :], gs))
    gk = jnp.where(low_lanes((BLOCK, 128)), gk_parts[0], gk_parts[1])
    gv = pbs[0] + pbs[1]
    gq = jnp.where(low_rows((128, QB)), gq_parts[0], gq_parts[1]) * (HEAD_DIM**-0.5)
    gqkv[0, at, lanes] = gq.T.astype(BF16)
    first = part == 0
    gk_acc[...] = jnp.where(first, gk, gk_acc[...] + gk)
    gv_acc[...] = jnp.where(first, gv, gv_acc[...] + gv)

    @pl.when(part == parts - 1)
    def _():
        gqkv[1, :, lanes] = gk_acc[...].astype(BF16)
        gqkv[2, :, lanes] = gv_acc[...].astype(BF16)


UNITS_C = "0123oabc"


def kernel_c(linked, sid, x_h, a1t_h, q0_h, q1_h, k0_h, k1_h, v_h, kt_h, ot_h, lse, gx1_h, gb_h, go0_h, go1_h, dots, vecs, wq_h, wk_h, wv_h, *refs):
    if linked:
        (gin_h, sums_b), refs = refs[:2], refs[2:]
    (ig_h, tg, gqkv_h, gwo_h, sums), refs = refs[:5], refs[5:]
    if linked:
        (gin_o, gout_o, gqkv_o, small_o), refs = refs[:4], refs[4:]
    (x, a1t, q0, q1, k0, k1, v, kt, ot, gx1, gb, go0, go1, w, gqkv, gk_acc, gv_acc, gw, gwo, tsum, sems), refs = refs[:21], refs[21:]
    plan = Schedule(SCHEDULE_C)
    if linked:
        bufs, (value, small_b, local_sems, send, recv) = refs[:56], refs[56:]
        peers = Peers()
        links = Links(peers, send, recv)
        peers.greet()
        third = D // 3
        for n, name in enumerate(UNITS_C):
            if n < 4:
                parts, keep = (gin_h, n), functools.partial(store_lanes, gin_o, ((0, D * n, D),))
            elif n == 4:
                parts, keep = (gwo_h,), functools.partial(store_lanes, gout_o, ((0, 0, D),))
            else:
                places = tuple((third * m, D * m + third * (n - 5), third) for m in range(3))
                parts, keep = (gqkv_h, n - 5), functools.partial(store_lanes, gqkv_o, places)
            plan.units[name] = Scatter(n, links, parts, keep, bufs[7 * n : 7 * n + 7], local_sems.at[n])
        plan.run("pre", 0)
    mv = Mover(sems)
    early = [mv.start(s, d) for s, d in ((ot_h, ot), (gb_h, gb), (q0_h, q0), (q1_h, q1), (k0_h, k0), (k1_h, k1), (v_h, v), (kt_h, kt), (go0_h, go0), (go1_h, go1))]
    late = [mv.start(a1t_h, a1t), mv.start(x_h, x), mv.start(gx1_h, gx1)]
    late += [mv.start(part, w.at[j]) for j, part in enumerate((wq_h, wk_h, wv_h))]
    for c in early[:2]:
        c.wait()
    sums[...] = jnp.zeros_like(sums)

    @pl.loop(0, 2)
    def _(r):
        gwo[pl.ds(2 * r, 2)] = mm(ot[rows_at(r, 384), :], gb[...]).astype(BF16).reshape(2, 4, 48, D)

    gwo_copy = mv.start(gwo, gwo_h)
    for c in early[2:]:
        c.wait()
    gwo_copy.wait()
    plan.run("gwo", 0)
    steps = 2 * (BLOCK // QB)
    gw_copies = []
    for chunk in range(3):
        hooks = plan.hooks("att", steps * chunk, steps * chunk + steps)

        @pl.loop(steps * chunk, steps * chunk + steps)
        def _(step):
            attention_back_step(step, q0, q1, k0, k1, v, kt, go0, go1, lse, dots, gk_acc, gv_acc, gqkv)
            run_hooks(step, hooks)

        if chunk == 0:
            late[0].wait()
        for j in range(3):
            for r in range(2):
                part = mm(a1t[384 * r : 384 * r + 384, :], gqkv[j, :, 256 * chunk : 256 * chunk + 256]).astype(BF16)
                gw[chunk, 2 * r : 2 * r + 2, :, :, 256 * j : 256 * j + 256] = part.reshape(2, 4, 48, 256)
        gw_copies.append(mv.start(gw.at[chunk], gqkv_h.at[chunk]))
        plan.run("gw", chunk)
        gw_copies[chunk].wait()
    for c in late[1:]:
        c.wait()
    plan.run("gw", 3)
    gain = vecs[0:1, :]
    ln_hooks = plan.hooks("ln")

    @pl.loop(0, BLOCK // TB)
    def _(i):
        at = rows_at(i, TB)
        ga1 = mm_t(gqkv[0, at, :], w[0]) + mm_t(gqkv[1, at, :], w[1]) + mm_t(gqkv[2, at, :], w[2])
        sums[2] += fold8(gqkv[0, at, :].astype(F32))
        sums[3] += fold8(gqkv[2, at, :].astype(F32))
        n1, r1 = normalize(x[at, :])
        sums[0] += fold8(ga1 * n1)
        sums[1] += fold8(ga1)
        total = gx1[at, :] + norm_back(ga1, gain, n1, r1)
        for g in range(TB // SHORT):
            s = sid[(TB // SHORT) * i + g]
            live = (s >= 0).astype(F32)
            part = total[SHORT * g : SHORT * g + SHORT, :] * live
            x[rows_at((TB // SHORT) * i + g, SHORT), :] = part
            tsum[pl.ds((TB // SHORT) * i + g, 1), :] = jnp.sum(part, axis=0, keepdims=True)
        run_hooks(i, ln_hooks)

    ig_copy = mv.start(x, ig_h)
    if linked:
        pick = lambda ref, n: jnp.sum(ref[n], axis=0, keepdims=True)
        rows = [pick(sums, n) for n in range(4)] + [pick(sums_b, n) for n in range(1, 9)] + [jnp.zeros((4, D), F32)]
        value[0] = jnp.concatenate(rows, axis=0)
        small = SmallSum(links, value, small_b)
        small.send(0, "p")
    row = lax.broadcasted_iota(jnp.int32, (GROUPS, D), 0)
    acc = jnp.zeros((GROUPS, D), F32)
    for g in range(GROUPS):
        acc = acc + jnp.where(row == sid[g], tsum[g : g + 1, :], 0.0)
    tg[...] = acc
    if linked:
        small.take(0)
        small.send(1, "x")
        small.take(1)
        small.send(2, "y")
        plan.run("end", 0, slice(0, -1))
        small.take(2)
        small.spread()
        row, col = small_places(peers.dev)
        select = small_select(col)
        plan.run("end", 0, slice(-1, None))
        picked = lax.dot_general(small.total(), select, (((1,), (0,)), ((), ())),
                                 precision=lax.Precision.HIGHEST, preferred_element_type=F32)
        at_row = lax.broadcasted_iota(jnp.int32, (16, SMALL_LEN), 0) == row
        small_o[...] = jnp.sum(jnp.where(at_row, picked, 0.0), axis=0, keepdims=True)
        links.finish()
    ig_copy.wait()


def call_c(linked, *args):
    out = [sds(TOK, F32), sds((GROUPS, D), F32), sds((3, 4, 4, 48, D), BF16), sds((4, 4, 48, D), BF16), sds((4, 8, D), F32)]
    in_specs = [SMEM] + [ANY] * 9 + [VMEM] + [ANY] * 4 + [VMEM, VMEM, ANY, ANY, ANY]
    out_specs = [ANY, VMEM, ANY, ANY, VMEM]
    scratch = [vm(TOK, F32), vm(TOKT, BF16)] + [vm(TOK, BF16)] * 5 + [vm(TOKT, BF16)] * 2 + [vm(TOK, F32)] + [vm(TOK, BF16)] * 3
    scratch += [vm((3, D, D), BF16), vm((3, BLOCK, D), BF16), vm((BLOCK, 128), F32), vm((BLOCK, 128), F32), vm((3, 4, 4, 48, D), BF16), vm((4, 4, 48, D), BF16),
                vm((GROUPS, D), F32), pltpu.SemaphoreType.DMA((24,))]
    extra = {}
    if linked:
        in_specs += [ANY, VMEM]
        out += [sds((D // 32, n * D), F32) for n in (4, 1, 3)] + [sds((1, SMALL_LEN), F32)]
        out_specs += [VMEM] * 4
        units = len(UNITS_C)
        slots = SCATTER_SLOTS * units + 6
        scratch += units * scatter_bufs(D // 32, D) + [vm((4, 16, D), F32), vm((6, 16, D), F32)]
        scratch += [pltpu.SemaphoreType.DMA((n,)) for n in (units, slots, slots)]
        extra = dict(collective_id=3, has_side_effects=True)
    return pl.pallas_call(
        functools.partial(kernel_c, linked),
        name="part_c",
        out_shape=out,
        in_specs=in_specs,
        out_specs=out_specs,
        scratch_shapes=scratch,
        compiler_params=pltpu.CompilerParams(vmem_limit_bytes=VMEM_LIMIT, **extra),
    )(*args)


AXES = ("dp", "fsdp")
MESH = pl.DeviceIdType.MESH
SMALL = ((0, 24, 0), (24, 24, 1), (48, 24, 4), (72, 24, 5), (96, 24, 6), (120, 24, 11), (144, 48, 2), (192, 96, 7))
SMALL_ORDER = (0, 1, 3, 4, 5, 7, 2, 6)
SMALL_LEN = 384


class Peers:
    def __init__(self):
        self.z, self.f = lax.axis_index("dp"), lax.axis_index("fsdp")
        self.c = self.f % 2
        self.yx = self.f // 2
        x, y = self.yx % 2, self.yx // 2
        self.partner = self.f + 1 - 2 * self.c
        self.fx, self.fy = self.f + 2 - 4 * x, self.f + 4 - 8 * y
        self.fd = self.fx + 4 - 8 * y
        self.qx, self.qy, self.qd = self.fx // 2, self.fy // 2, self.fd // 2
        self.dev = self.z * 8 + self.f
        self.other = 1 - self.c
        self.ups = [(self.z + d) % 4 for d in range(4)]

    def up(self, d):
        return self.ups[d]

    def at(self, name, d=0):
        if name == "z":
            return (self.up(d), self.f)
        return (self.z, {"x": self.fx, "y": self.fy, "p": self.partner}[name])

    def greet(self):
        barrier = pltpu.get_barrier_semaphore()
        for target in [self.at("p"), self.at("x"), self.at("y")] + [self.at("z", d) for d in (1, 2, 3)]:
            pl.semaphore_signal(barrier, inc=1, device_id=target, device_id_type=MESH)
        pl.semaphore_wait(barrier, 6)


class View:
    def __init__(self, ref, *index):
        self.ref, self.index = ref, index

    def get(self):
        return self.ref.at[self.index] if self.index else self.ref


class Links:
    def __init__(self, peers, send, recv):
        self.peers, self.send, self.recv = peers, send, recv
        self.slots, self.sent = {}, []

    def copy(self, key, src, dst, target):
        n = self.slots.setdefault(key, len(self.slots))
        return pltpu.make_async_remote_copy(
            src_ref=src.get(), dst_ref=dst.get(), send_sem=self.send.at[n], recv_sem=self.recv.at[n],
            device_id=target, device_id_type=MESH)

    def start(self, key, src, dst, name, d=0):
        args = (key, src, dst, self.peers.at(name, d))
        self.copy(*args).start()
        self.sent.append(args)

    def arrived(self, key, dst):
        self.copy(key, dst, dst, self.peers.at("p")).wait_recv()

    def finish(self):
        for args in self.sent:
            self.copy(*args).wait_send()
        self.sent = []


GATHER_SLOTS = 19


class Gather:
    def __init__(self, name, links, own, rows, full, sem):
        self.name, self.links, self.own, self.rows, self.full, self.sem = name, links, own, rows, full, sem
        p = links.peers
        self.at = {n: pl.multiple_of(f * self.rows, 8) for n, f in (("f", p.f), ("x", p.fx), ("y", p.fy), ("d", p.fd))}
        self.across = {n: pl.multiple_of((f + 1 - 2 * p.c) * self.rows, 8)
                       for n, f in (("f", p.f), ("x", p.fx), ("y", p.fy), ("d", p.fd))}

    def key(self, *k):
        return (self.name,) + k

    def piece(self, d, n):
        return View(self.full, self.links.peers.up((4 - d) % 4), pl.ds(self.at[n], self.rows))

    def column(self, at):
        return View(self.full, slice(None), pl.ds(at, self.rows))

    def begin(self):
        here = self.piece(0, "f")
        for d in (1, 3, 2):
            self.links.start(self.key("z", d), self.own, here, "z", d)
        self.local_copy().start()

    def local_copy(self):
        return pltpu.make_async_copy(self.own.get(), self.piece(0, "f").get(), self.sem)

    def do(self, action):
        links, kind, d = self.links, action[0], int(action[1:] or 0)
        if kind == "F":
            piece = self.piece(d, "f")
            if d:
                links.arrived(self.key("z", d), piece)
            src = piece if d else self.own
            links.start(self.key("x", d), src, piece, "x")
            links.start(self.key("y", d), src, piece, "y")
            if d == 2:
                self.local_copy().wait()
                mine = self.column(self.at["f"])
                links.start(self.key("p", "f"), mine, mine, "p")
        elif kind == "S":
            px, py = self.piece(d, "x"), self.piece(d, "y")
            links.arrived(self.key("x", d), px)
            links.arrived(self.key("y", d), py)
            via, part = ("y", px) if d < 2 else ("x", py)
            links.start(self.key("d", d), part, part, via)
            if d == 2:
                for n in ("x", "y"):
                    part = self.column(self.at[n])
                    links.start(self.key("p", n), part, part, "p")
        elif kind == "T":
            for n in range(4):
                links.arrived(self.key("d", n), self.piece(n, "d"))
            part = self.column(self.at["d"])
            links.start(self.key("p", "d"), part, part, "p")
        else:
            for n in ("f", "x", "y", "d"):
                links.arrived(self.key("p", n), self.column(self.across[n]))


SCATTER_SLOTS = 10


class Scatter:
    def __init__(self, name, links, parts, keep, bufs, sem):
        self.name, self.links, self.parts, self.keep, self.sem = name, links, parts, keep, sem
        self.t, self.p, self.dx, self.dy, self.xr, self.yr, self.zr = bufs
        p, self.rows = links.peers, self.t.shape[2]
        self.here, self.there = (pl.multiple_of(c * self.rows, 8) for c in (p.c, p.other))

    def half(self, at):
        return View(self.parts[0], *self.parts[1:], slice(None), slice(None), pl.ds(at, self.rows))

    def do(self, action):
        {"B": self.begin, "F": self.first, "S": self.second, "T": self.third, "L": self.last}[action]()

    def key(self, *k):
        return (self.name,) + k

    def begin(self):
        p = self.links.peers
        self.links.start(self.key("p"), self.half(self.there), View(self.p), "p")
        self.local_copy().start()

    def local_copy(self):
        return pltpu.make_async_copy(self.half(self.here).get(), self.t, self.sem)

    def add(self, q, zs, ref, base=0):
        t = self.t

        @pl.loop(zs[0], zs[1])
        def _(i):
            t[i, q] = (t[i, q].astype(F32) + ref(i - base).astype(F32)).astype(BF16)

    def first(self):
        p, links, t = self.links.peers, self.links, self.t
        self.local_copy().wait()
        links.arrived(self.key("p"), View(self.p))
        self.add(p.qd, (0, 4), lambda i: self.p[i, p.qd])
        links.start(self.key("dx"), View(t, pl.ds(0, 2), p.qd), View(self.dx), "x")
        links.start(self.key("dy"), View(t, pl.ds(2, 2), p.qd), View(self.dy), "y")
        self.add(p.qx, (0, 4), lambda i: self.p[i, p.qx])
        links.start(self.key("x", 0), View(t, pl.ds(0, 2), p.qx), View(self.xr, pl.ds(0, 2)), "x")
        self.add(p.qy, (0, 4), lambda i: self.p[i, p.qy])
        links.start(self.key("y", 1), View(t, pl.ds(2, 2), p.qy), View(self.yr, pl.ds(2, 2)), "y")
        self.add(p.yx, (0, 4), lambda i: self.p[i, p.yx])

    def second(self):
        p, links, t = self.links.peers, self.links, self.t
        links.arrived(self.key("dy"), View(self.dy))
        self.add(p.qx, (2, 4), lambda i: self.dy[i], 2)
        links.start(self.key("x", 1), View(t, pl.ds(2, 2), p.qx), View(self.xr, pl.ds(2, 2)), "x")
        links.arrived(self.key("dx"), View(self.dx))
        self.add(p.qy, (0, 2), lambda i: self.dx[i])
        links.start(self.key("y", 0), View(t, pl.ds(0, 2), p.qy), View(self.yr, pl.ds(0, 2)), "y")

    def third(self):
        p, links, t = self.links.peers, self.links, self.t
        for n in range(2):
            links.arrived(self.key("x", n), View(self.xr, pl.ds(2 * n, 2)))
            links.arrived(self.key("y", n), View(self.yr, pl.ds(2 * n, 2)))

        @pl.loop(0, 4)
        def _(i):
            t[i, p.yx] = (t[i, p.yx].astype(F32) + self.xr[i].astype(F32) + self.yr[i].astype(F32)).astype(BF16)

        for d in (2, 1, 3):
            links.start(self.key("z", d), View(t, p.up(d), p.yx), View(self.zr, d - 1), "z", d)

    def last(self):
        p, links = self.links.peers, self.links
        for d in (1, 2, 3):
            links.arrived(self.key("z", d), View(self.zr, d - 1))
        total = self.t[p.z, p.yx].astype(F32)
        for n in range(3):
            total = total + self.zr[n].astype(F32)
        self.keep(total)


def scatter_bufs(rows, cols):
    return [pltpu.VMEM(lead + (rows, cols), BF16) for lead in ((4, 4), (4, 4), (2,), (2,), (4,), (4,), (3,))]


class SmallSum:
    def __init__(self, links, value, bufs):
        self.links, self.value, self.bufs = links, value, bufs

    def send(self, n, name):
        self.links.start(("s", n), View(self.value, n), View(self.bufs, n), name)

    def take(self, n):
        self.links.arrived(("s", n), View(self.bufs, n))
        self.value[n + 1] = self.value[n] + self.bufs[n]

    def spread(self):
        for d in (1, 2, 3):
            self.links.start(("s", 2 + d), View(self.value, 3), View(self.bufs, 2 + d), "z", d)

    def total(self):
        for d in (1, 2, 3):
            self.links.arrived(("s", 2 + d), View(self.bufs, 2 + d))
        return self.value[3] + self.bufs[3] + self.bufs[4] + self.bufs[5]


def small_places(dev):
    i = lax.broadcasted_iota(jnp.int32, (1, SMALL_LEN), 1)
    row, col = jnp.full((1, SMALL_LEN), 15, jnp.int32), jnp.full((1, SMALL_LEN), -1, jnp.int32)
    for start, n, base in SMALL:
        here = (i >= start) & (i < start + n)
        row = jnp.where(here, base + (dev * n) // D, row)
        col = jnp.where(here, (dev * n) % D + i - start, col)
    return row, col


def small_select(col):
    return (lax.broadcasted_iota(jnp.int32, (D, SMALL_LEN), 0) == col).astype(F32)


def kernel_prep(small, wqkv, wout, win, wdown, small_o, qkv_o, out_o, in_o, down_o):
    small_o[...] = jnp.broadcast_to(small[...], (8, SMALL_LEN)).astype(BF16)
    qkv_o[...] = wqkv[...].astype(BF16)
    out_o[...] = wout[...].astype(BF16)
    in_o[...] = win[...].astype(BF16)
    down_o[...] = wdown[...].astype(BF16)


def call_prep(small, weights):
    return pl.pallas_call(
        kernel_prep, name="prep",
        out_shape=[sds((8, SMALL_LEN), BF16)] + [sds(w.shape, BF16) for w in weights],
        in_specs=[VMEM] * 5, out_specs=[VMEM] * 5,
    )(small, *weights)


def build_table(gathered, staged, sem, vecs):
    copy = pltpu.make_async_copy(gathered, staged, sem)
    copy.start()
    copy.wait()
    rows = staged[...].reshape(256, SMALL_LEN).astype(F32).T
    r = lax.broadcasted_iota(jnp.int32, (256, D), 0)
    lane = lax.broadcasted_iota(jnp.int32, (256, D), 1)
    vecs[...] = jnp.zeros_like(vecs)
    for n in (24, 48, 96):
        part = [(start, base) for start, size, base in SMALL if size == n]
        values = rows[part[0][0] : part[-1][0] + n, :].astype(BF16)
        own = lax.broadcasted_iota(jnp.int32, (n, D), 0) == lax.rem(lax.broadcasted_iota(jnp.int32, (n, D), 1), n)
        for line in range(n // 24):
            source = ((lane + line * D) // n) * 8
            spread = mm(values, (r == source).astype(BF16))
            for m, (_, base) in enumerate(part):
                picked = jnp.where(own, spread[n * m : n * m + n, :], 0.0)
                vecs[base + line : base + line + 1, :] = jnp.sum(picked, axis=0, keepdims=True)


def gather_all(a):
    return lax.all_gather(a.astype(BF16), AXES, axis=0, tiled=True)


def scatter_sum(a):
    return lax.psum_scatter(a, AXES, scatter_dimension=0, tiled=True)


def split_small(row, small):
    parts, at = [], 0
    for s in small:
        parts.append(row[at : at + s.shape[0]])
        at += s.shape[0]
    return parts


def gather_plain(small, weights):
    every = lax.all_gather(jnp.concatenate([s.astype(BF16) for s in small]), AXES, axis=0, tiled=False)
    vecs, at = [], 0
    for s in small:
        vecs.append(every[:, at : at + s.shape[0]].reshape(-1, D))
        at += s.shape[0]
    vecs = jnp.concatenate(vecs + [jnp.zeros((4, D), BF16)], axis=0).astype(F32)
    return vecs, [gather_all(w) for w in weights]


def scatter_plain(sums_b, sums_c, grads, small):
    sb, sc = jnp.sum(sums_b, axis=1), jnp.sum(sums_c, axis=1)
    vectors = (sc[0], sc[1], sc[2:4].reshape(-1), sb[1], sb[2], sb[3], sb[4:8].reshape(-1), sb[8])
    devices = D // small[0].shape[0]
    packed = jnp.concatenate([g.reshape(devices, -1) for g in vectors], axis=1)
    return scatter_sum(packed).reshape(-1), [scatter_sum(g.astype(F32)) for g in grads]


def local(
    own_links,
    hidden_in, time_embed, seg_ids, pre_gain, pre_shift, qkv_weight, qv_bias, out_weight, out_bias,
    mid_gain, mid_shift, in_weight, in_bias, down_weight, down_bias, grad_out,
):
    sid = seg_ids.reshape(GROUPS, SHORT)[:, 0]
    small = (pre_gain, pre_shift, qv_bias, out_bias, mid_gain, mid_shift, in_bias, down_bias)
    weights = (qkv_weight, out_weight, in_weight, down_weight)
    if own_links:
        ordered = tuple(small[n] for n in SMALL_ORDER)
        row = jnp.concatenate(ordered + (jnp.zeros((SMALL_LEN - 288,), F32),)).reshape(1, SMALL_LEN)
        vecs, made, wq, (wout, win, wdown) = call_a_links(sid, hidden_in, time_embed, call_prep(row, weights))
    else:
        vecs, (wqkv, wout, win, wdown) = gather_plain(small, weights)
        wq = [wqkv[:, D * n : D * n + D] for n in range(3)]
        made = call_a(sid, hidden_in, time_embed, vecs, wq)
    x, a1t, q0, q1, k0, k1, v, kt, o, ot, lse = made
    block_out, gx1, gb, go0, go1, dots, gdown, gin, sums_b, *more = call_b(own_links, sid, x, o, grad_out, vecs, wout, win, wdown)
    args_c = (sid, x, a1t, q0, q1, k0, k1, v, kt, ot, lse, gx1, gb, go0, go1, dots, vecs, *wq)
    if own_links:
        input_grad, time_grad, _, _, _, gin, gout, gqkv, mine = call_c(True, *args_c, gin, sums_b)
        gdown = more[0]
        parts = split_small(mine.reshape(-1), ordered)
        parts = [parts[SMALL_ORDER.index(n)] for n in range(8)]
    else:
        input_grad, time_grad, gqkv, gout, sums_c = call_c(False, *args_c)
        gdown = gdown.reshape(D // DT, FF, DT).transpose(1, 0, 2).reshape(FF, D)
        gin = gin.reshape(4, D, D).transpose(1, 0, 2).reshape(D, FF)
        gqkv = gqkv.reshape(3, D, 3, D // 3).transpose(1, 2, 0, 3).reshape(D, 3 * D)
        mine, (gdown, gin, gout, gqkv) = scatter_plain(sums_b, sums_c, (gdown, gin, gout.reshape(D, D), gqkv), small)
        parts = split_small(mine, small)
    gpg, gps, gqvb, gob, gmg, gms, gib, gdb = parts
    return (block_out, input_grad, time_grad, gpg, gps, gqkv, gqvb, gout, gob, gmg, gms, gin, gib, gdown, gdb)


def solution(mesh):
    rows, flat = P(AXES, None), P(AXES)
    own_links = dict(mesh.shape) == {"dp": 4, "fsdp": 8}
    return jax.shard_map(
        functools.partial(local, own_links),
        mesh=mesh,
        in_specs=(rows, rows, flat, flat, flat, rows, flat, rows, flat, flat, flat, rows, flat, rows, flat, rows),
        out_specs=(rows, rows, rows, flat, flat, rows, flat, rows, flat, flat, flat, rows, flat, rows, flat),
        check_vma=False,
    )
```

```python
import functools

import jax
import jax.numpy as jnp
from jax import lax
from jax.experimental import pallas as pl
from jax.experimental.pallas import tpu as pltpu
from jax.sharding import PartitionSpec as P

D = 768
HEADS = 12
HEAD_DIM = 64
FF = 3072
BLOCK = 1024
SHORT = 64
GROUPS = BLOCK // SHORT
PAIRS = HEADS // 2
TB = 256
NEG = -1e30
F32 = jnp.float32
BF16 = jnp.bfloat16
VMEM_LIMIT = 62 * 1024 * 1024
ANY = pl.BlockSpec(memory_space=pl.ANY)
VMEM = pl.BlockSpec(memory_space=pltpu.VMEM)
SMEM = pl.BlockSpec(memory_space=pltpu.SMEM)
ERFC_SCALE = 0.44
ERFC_POLY = (
    0.24822097621403005,
    0.2488708795734658,
    0.21731516533725015,
    0.21580763970434977,
    -0.020173037922183695,
    0.2966799647080617,
    -0.2779439059726245,
    0.07122249905985603,
)


def rows_at(i, size):
    return pl.ds(pl.multiple_of(i * size, size), size)


def mm(a, b):
    return lax.dot_general(a, b, (((1,), (0,)), ((), ())), preferred_element_type=F32)


def mm_t(a, b):
    return lax.dot_general(a, b, (((1,), (1,)), ((), ())), preferred_element_type=F32)


def normalize(v):
    center = v - jnp.mean(v, axis=-1, keepdims=True)
    spread = jnp.mean(center * center, axis=-1, keepdims=True)
    scale = lax.rsqrt(spread + 1e-05)
    return center * scale, scale


def norm_back(grad, gain, n, scale):
    g = grad * gain
    return scale * (
        g - jnp.mean(g, axis=-1, keepdims=True) - n * jnp.mean(g * n, axis=-1, keepdims=True)
    )


def fold8(v):
    return jnp.sum(v.reshape(v.shape[0] // 8, 8, v.shape[1]), axis=0)


def gelu_parts(u):
    z = jnp.abs(u) * 0.7071067811865476
    t = 1.0 / (1.0 + ERFC_SCALE * z)
    poly = jnp.full_like(t, ERFC_POLY[-1])
    for c in ERFC_POLY[-2::-1]:
        poly = poly * t + c
    e = jnp.exp(-(z * z))
    tail = 0.5 * poly * t * e
    phi = jnp.where(u >= 0, 1.0 - tail, tail)
    return u * phi, phi + u * e * 0.3989422804014327


class Mover:
    def __init__(self, sems):
        self.sems, self.next = sems, 0

    def start(self, src, dst):
        copy = pltpu.make_async_copy(src, dst, self.sems.at[self.next])
        self.next += 1
        copy.start()
        return copy


def run_hooks(step, hooks):
    for n, actions in hooks.items():
        if not actions:
            continue

        @pl.when(step == n)
        def _():
            for action in actions:
                action()


def stage_norm1(sid, time, vecs, x, a1, a1t, hooks):
    gain, shift = vecs[0:1, :], vecs[1:2, :]

    @pl.loop(0, BLOCK // 128)
    def _(i):
        parts = []
        for half in range(2):
            s = sid[2 * i + half]
            live = (s >= 0).astype(F32)
            row = time[pl.ds(jnp.maximum(s, 0), 1), :]
            parts.append((x[rows_at(2 * i + half, SHORT), :] + row) * live)
        block = jnp.concatenate(parts, axis=0)
        at = rows_at(i, 128)
        x[at, :] = block
        n, _ = normalize(block)
        a = n * gain + shift
        a1[at, :] = a.astype(BF16)
        a1t[:, at] = a.T.astype(BF16)
        run_hooks(i, hooks)


def mask_rows(sid, i, groups):
    lane = lax.rem(lax.broadcasted_iota(jnp.int32, (SHORT, 128), 1), 64)
    mq, mk = [], []
    for g in range(groups):
        s = sid[groups * i + g]
        own = jnp.where(s >= 0, s, 16)
        mk.append((lane == own).astype(F32))
        bad = ((lane < 16) & (lane != s)) | (lane == 16)
        mq.append(jnp.where(bad, NEG, 0.0))
    return jnp.concatenate(mq, axis=0), jnp.concatenate(mk, axis=0)


def low_lanes(shape):
    return lax.broadcasted_iota(jnp.int32, shape, 1) < 64


def low_rows(shape):
    return lax.broadcasted_iota(jnp.int32, shape, 0) < 64


def stage_q(sid, vecs, a1, w, q0, q1, hooks):
    @pl.loop(0, BLOCK // TB)
    def _(i):
        at = rows_at(i, TB)
        mq, _ = mask_rows(sid, i, TB // SHORT)
        acc = mm(a1[at, :], w) + vecs[2:3, :]
        acc = acc.astype(BF16).astype(F32) * (HEAD_DIM**-0.5)
        low = low_lanes((TB, 128))
        for p in range(PAIRS):
            part = acc[:, 128 * p : 128 * p + 128]
            q0[at, 128 * p : 128 * p + 128] = jnp.where(low, part, mq).astype(BF16)
            q1[at, 128 * p : 128 * p + 128] = jnp.where(low, mq, part).astype(BF16)
        run_hooks(i, hooks)


def stage_k(sid, a1, w, k0, k1, kt, hooks):
    @pl.loop(0, BLOCK // TB)
    def _(i):
        at = rows_at(i, TB)
        _, mk = mask_rows(sid, i, TB // SHORT)
        acc = mm(a1[at, :], w)
        low = low_lanes((TB, 128))
        for p in range(PAIRS):
            part = acc[:, 128 * p : 128 * p + 128]
            k0[at, 128 * p : 128 * p + 128] = jnp.where(low, part, mk).astype(BF16)
            k1[at, 128 * p : 128 * p + 128] = jnp.where(low, mk, part).astype(BF16)
        kt[:, at] = acc.T.astype(BF16)
        run_hooks(i, hooks)


def stage_v(vecs, a1, w, v, vt0, vt1, hooks):
    @pl.loop(0, BLOCK // TB)
    def _(i):
        at = rows_at(i, TB)
        acc = mm(a1[at, :], w) + vecs[3:4, :]
        v[at, :] = acc.astype(BF16)
        accT = acc.T
        low = low_rows((128, TB))
        for p in range(PAIRS):
            part = accT[128 * p : 128 * p + 128, :]
            vt0[128 * p : 128 * p + 128, at] = jnp.where(low, part, 1.0).astype(BF16)
            vt1[128 * p : 128 * p + 128, at] = jnp.where(low, 1.0, part).astype(BF16)
        run_hooks(i, hooks)


QB = 256


STEPS = PAIRS * (BLOCK // QB)


def step_place(step):
    return rows_at(step // (BLOCK // QB), 128), rows_at(lax.rem(step, BLOCK // QB), QB)


def attention_scores(step, q0, q1, k0, k1, s_ref, m_ref):
    lanes, at = step_place(step)
    for h, (q, k) in enumerate(((q0, k0), (q1, k1))):
        scores = mm_t(k[:, lanes], q[at, lanes])
        s_ref[h] = scores
        m_ref[h : h + 1, :] = jnp.max(scores, axis=0, keepdims=True)


def attention_apply(step, s_ref, m_ref, vt0, vt1, o, ot, lse):
    lanes, at = step_place(step)
    outs = []
    for h, (vt, total_row) in enumerate(((vt0, 64), (vt1, 0))):
        top = m_ref[h : h + 1, :]
        e = jnp.exp(s_ref[h] - top).astype(BF16)
        res = mm(vt[lanes, :], e)
        total = res[total_row : total_row + 1, :]
        outs.append(res * (1.0 / total))
        lse[pl.ds(2 * (step // (BLOCK // QB)) + h, 1), at] = top + jnp.log(total)
    both = jnp.where(low_rows((128, QB)), outs[0], outs[1])
    ot[lanes, at] = both.astype(BF16)
    o[at, lanes] = both.T.astype(BF16)


def paired_steps(first, count, slots, ahead, apply, hooks):
    parity = [{n: a for n, a in hooks.items() if n % 2 == k} for k in range(2)]

    @pl.loop(0, count // 2)
    def _(i):
        for k in range(2):
            step = first + 2 * i + k
            ahead(jnp.minimum(step + 1, STEPS - 1), slots[1 - k])
            apply(step, slots[k])
            run_hooks(step, parity[k])


SCHEDULE_A = {
    ("pre", 0): ("s.F0", "q.F0", "k.F0", "s.F1", "s.F3", "s.F2", "s.S0", "q.F1", "s.S1", "q.F3", "s.S3", "s.S2", "q.F2", "q.S0", "q.S1", "k.F1", "k.F3", "q.S3", "s.T", "q.S2", "k.F2", "k.S0", "v.F0", "s.L",),
    ("norm", 0): ("v.F1",),
    ("norm", 2): ("v.F3",),
    ("norm", 3): ("k.S1",),
    ("norm", 4): ("k.S3", "v.F2", "o.F0",),
    ("norm", 5): ("q.T",),
    ("norm", 7): ("k.S2", "o.F1",),
    ("q", -1): ("o.F3", "v.S0", "v.S1", "q.L",),
    ("q", 0): ("o.F2",),
    ("q", 2): ("v.S3",),
    ("k", -1): ("v.S2", "i.F0", "o.S0", "k.T", "i.F1", "o.S1", "o.S3", "k.L",),
    ("k", 3): ("o.S2",),
    ("v", -1): ("v.T", "i.F3", "v.L",),
    ("att", 0): ("i.F2", "i.S0",),
    ("att", 2): ("i.S1",),
    ("att", 3): ("o.T",),
    ("att", 7): ("o.L",),
    ("att", 8): ("i.S3",),
    ("att", 12): ("i.S2",),
    ("att", 21): ("i.T",),
    ("end", 0): ("i.L",),
}
SCHEDULE_B = {
    ("pre", 0): ("d.F0",),
    ("p1", 2): ("d.F1",),
    ("p1", 3): ("d.F3",),
    ("p1", 5): ("d.F2", "d.S0", "d.S1",),
    ("p1", 6): ("d.S3",),
    ("gd", 0): ("d.S2",),
    ("gd", 1): ("x.B",),
    ("gd", 2): ("y.B",),
    ("wd", 0): ("z.B", "d.T", "x.F", "y.F", "z.F", "d.L",),
    ("wd", 1): ("x.S",),
    ("p2", 1): ("y.S",),
    ("p2", 2): ("z.S",),
    ("p2", 4): ("x.T",),
    ("p2", 5): ("y.T", "z.T",),
    ("p2", 7): ("x.L",),
    ("gi", 2): ("y.L",),
    ("end", 0): ("z.L",),
}
SCHEDULE_C = {
    ("pre", 0): ("0.B", "1.B", "2.B", "3.B",),
    ("att", 0): ("0.F",),
    ("att", 1): ("o.B", "1.F", "2.F",),
    ("att", 2): ("3.F",),
    ("att", 3): ("o.F", "0.S",),
    ("att", 5): ("1.S",),
    ("att", 7): ("2.S",),
    ("att", 8): ("3.S",),
    ("att", 9): ("a.B",),
    ("att", 10): ("o.S",),
    ("att", 12): ("a.F", "0.T",),
    ("att", 13): ("1.T",),
    ("att", 14): ("2.T",),
    ("att", 15): ("3.T",),
    ("gw", 1): ("o.T",),
    ("att", 16): ("a.S", "0.L",),
    ("att", 17): ("b.B",),
    ("att", 18): ("1.L",),
    ("att", 19): ("a.T",),
    ("att", 20): ("b.F", "2.L",),
    ("att", 22): ("3.L",),
    ("gw", 2): ("b.S", "o.L",),
    ("gw", 3): ("c.B",),
    ("ln", 0): ("a.L",),
    ("ln", 1): ("b.T", "c.F",),
    ("end", 0): ("c.S", "b.L", "c.T", "c.L",),
}


class Schedule:
    def __init__(self, table):
        self.table, self.units = table, {}

    def actions(self, seg, step):
        found = self.table.get((seg, step), ()) if self.units else ()
        return [functools.partial(self.units[a[0]].do, a[2:]) for a in found]

    def hooks(self, seg, first=0, last=24):
        return {n: self.actions(seg, n) for n in range(first, last) if self.actions(seg, n)}

    def run(self, seg, step, part=slice(None)):
        for action in self.actions(seg, step)[part]:
            action()


def kernel_a(linked, sid, hidden, time, *refs):
    if linked:
        own, refs = refs[:4], refs[4:]
        vecs, refs = refs[0], refs[1:]
    else:
        (vecs, *wq), refs = refs[:4], refs[4:]
    (x_h, a1t_h, q0_h, q1_h, k0_h, k1_h, v_h, kt_h, o_h, ot_h, lse), refs = refs[:11], refs[11:]
    if linked:
        full, refs = refs[:6], refs[6:]
        wq = full[1:4]
    (x, a1, a1t, q0, q1, k0, k1, v, kt, vt0, vt1, o, ot, w, s0, m0, s1, m1, sems), refs = refs[:19], refs[19:]
    mv = Mover(sems)
    cx = mv.start(hidden, x)
    plan = Schedule(SCHEDULE_A)
    if linked:
        staged, local_sems, send, recv = refs
        peers = Peers()
        links = Links(peers, send, recv)
        peers.greet()
        small, qkv, out, inn = own
        pieces = [View(small)] + [View(qkv, slice(None), pl.ds(D * n, D)) for n in range(3)] + [View(out), View(inn)]
        rows = (small.shape[0],) + 5 * (D // 32,)
        for n, name in enumerate("sqkvoi"):
            plan.units[name] = Gather(n, links, pieces[n], rows[n], full[n], local_sems.at[n])
            plan.units[name].begin()
    run, hooks = plan.run, plan.hooks
    run("pre", 0)
    if linked:
        build_table(full[0], staged, local_sems.at[7], vecs)
    cx.wait()
    stage_norm1(sid, time, vecs, x, a1, a1t, hooks("norm"))
    outs = [mv.start(x, x_h), mv.start(a1t, a1t_h)]

    def weight(name, j):
        run(name, -1)
        copy = mv.start(wq[j], w.at[j])
        copy.wait()
        return w[j].reshape(D, D)

    stage_q(sid, vecs, a1, weight("q", 0), q0, q1, hooks("q"))
    outs += [mv.start(q0, q0_h), mv.start(q1, q1_h)]
    stage_k(sid, a1, weight("k", 1), k0, k1, kt, hooks("k"))
    outs += [mv.start(k0, k0_h), mv.start(k1, k1_h), mv.start(kt, kt_h)]
    stage_v(vecs, a1, weight("v", 2), v, vt0, vt1, hooks("v"))
    outs += [mv.start(v, v_h)]
    attention_hooks = hooks("att")

    slots = ((s0, m0), (s1, m1))

    def ahead(step, slot):
        attention_scores(step, q0, q1, k0, k1, *slot)

    def apply(step, slot):
        attention_apply(step, *slot, vt0, vt1, o, ot, lse)

    ahead(0, slots[0])
    paired_steps(0, STEPS, slots, ahead, apply, attention_hooks)
    outs += [mv.start(o, o_h), mv.start(ot, ot_h)]
    run("end", 0)
    for copy in outs:
        copy.wait()
    if linked:
        links.finish()


def sds(shape, dtype):
    return jax.ShapeDtypeStruct(shape, dtype)


TOK = (BLOCK, D)
TOKT = (D, BLOCK)


def vm(shape, dtype):
    return pltpu.VMEM(shape, dtype)


OUT_A = [sds(TOK, F32), sds(TOKT, BF16)] + [sds(TOK, BF16)] * 5 + [sds(TOKT, BF16), sds(TOK, BF16), sds(TOKT, BF16), sds((16, BLOCK), F32)]
SCRATCH_A = [vm(TOK, F32), vm(TOK, BF16), vm(TOKT, BF16)] + [vm(TOK, BF16)] * 5 + [vm(TOKT, BF16)] * 3 + [
    vm(TOK, BF16), vm(TOKT, BF16), vm((3, 4, D // 4, D), BF16)] + 2 * [vm((2, BLOCK, QB), F32), vm((8, QB), F32)] + [pltpu.SemaphoreType.DMA((16,))]


def call_a(sid, hidden, time, vecs, wq):
    return pl.pallas_call(
        functools.partial(kernel_a, False),
        name="part_a",
        out_shape=OUT_A,
        in_specs=[SMEM, ANY, VMEM, VMEM, ANY, ANY, ANY],
        out_specs=[ANY] * 10 + [VMEM],
        scratch_shapes=SCRATCH_A,
        compiler_params=pltpu.CompilerParams(vmem_limit_bytes=VMEM_LIMIT),
    )(sid, hidden, time, vecs, *[a.reshape(4, D // 4, D) for a in wq])


def call_a_links(sid, hidden, time, own):
    small, qkv, out, inn = own
    sizes = [small.shape] + [(D // 32, D)] * 4 + [inn.shape]
    slots = GATHER_SLOTS * 6
    res = pl.pallas_call(
        functools.partial(kernel_a, True),
        name="part_a",
        out_shape=[sds((16, D), F32)] + OUT_A + [sds((4, 8 * r, c), BF16) for r, c in sizes],
        in_specs=[SMEM, ANY, VMEM] + [VMEM] * 4,
        out_specs=[VMEM] + [ANY] * 10 + [VMEM] + [ANY] * 6,
        scratch_shapes=SCRATCH_A + [vm((4, 64, SMALL_LEN), BF16)] + [pltpu.SemaphoreType.DMA((n,)) for n in (8, slots, slots)],
        compiler_params=pltpu.CompilerParams(vmem_limit_bytes=VMEM_LIMIT, collective_id=1, has_side_effects=True),
    )(sid, hidden, time, *own)
    full = [a.reshape(-1, a.shape[-1]) for a in res[13:]]
    return res[0], res[1:12], full[:3], full[3:]


def kernel_b(linked, sid, x_h, o_h, gout_h, vecs, wout_h, win_h, wdown_h,
             out_h, gx1_h, gb_h, go0_h, go1_h, dots, gdown_h, gin_h, sums, *refs):
    if linked:
        (gdown_o, down_f), refs = refs[:2], refs[2:]
    (x, o, gy, wout, win, wdown, gm, a2t, ht, h, gu, gb, go0, go1, stage_d, stage, sems), refs = refs[:17], refs[17:]
    plan = Schedule(SCHEDULE_B)
    if linked:
        bufs, (local_sems, send, recv) = refs[:21], refs[21:]
        peers = Peers()
        links = Links(peers, send, recv)
        peers.greet()
        plan.units["d"] = Gather(3, links, View(wdown_h), FF // 32, down_f, local_sems.at[3])
        plan.units["d"].begin()
        for n, name in enumerate("xyz"):
            keep = functools.partial(store_lanes, gdown_o, ((0, DT * n, DT),))
            plan.units[name] = Scatter(n, links, (gdown_h, n), keep, bufs[7 * n : 7 * n + 7], local_sems.at[n])
        plan.run("pre", 0)
    mv = Mover(sems)
    cx, co, cg = mv.start(x_h, x), mv.start(o_h, o), mv.start(gout_h, gy)
    cwo = mv.start(wout_h, wout)
    cwi = [mv.start(win_h.at[:, pl.ds(D * j, D)], win.at[j]) for j in range(4)]
    down_parts = [down_f.at[j] if linked else wdown_h.at[pl.ds(D * j, D), :] for j in range(4)]
    p1_hooks = [{n: plan.actions("p1", n) for n in range(k, 8, 2)} for k in range(2)]
    sums[...] = jnp.zeros_like(sums)
    for c in [cx, co, cg, cwo] + cwi:
        c.wait()
    lane = lax.broadcasted_iota(jnp.int32, (16, D), 1) // HEAD_DIM
    heads = (lane == lax.broadcasted_iota(jnp.int32, (16, D), 0)).astype(BF16)
    blocks = BLOCK // TB
    outs = []
    so = mv.sems

    def out_copies(i):
        at = rows_at(i, TB)
        return [pltpu.make_async_copy(x.at[at, :], out_h.at[at, :], so.at[16]),
                pltpu.make_async_copy(gy.at[at, :], gx1_h.at[at, :], so.at[17])]

    def live_rows(i):
        return jnp.concatenate(
            [jnp.full((SHORT, 1), (sid[(TB // SHORT) * i + g] >= 0).astype(F32), F32) for g in range(TB // SHORT)], axis=0)

    @pl.loop(0, blocks)
    def _(i):
        at = rows_at(i, TB)
        x1 = x[at, :] + mm(o[at, :], wout[...]) + vecs[4:5, :]
        x[at, :] = x1
        n2, _ = normalize(x1)
        a2f = n2 * vecs[5:6, :] + vecs[6:7, :]
        a2 = a2f.astype(BF16)
        a2t[:, at] = a2f.T.astype(BF16)
        gyb = gy[at, :] * live_rows(i)
        gy[at, :] = gyb
        gm[at, :] = gyb.astype(BF16)
        for j in range(4):
            u = mm(a2, win[j]) + vecs[7 + j : 8 + j, :]
            hf, slope = gelu_parts(u)
            ht[D * j : D * j + D, at] = hf.T.astype(BF16)
            h[at, D * j : D * j + D] = hf.astype(BF16)
            gu[at, D * j : D * j + D] = slope.astype(BF16)
            if j % 2:
                run_hooks(2 * i + j // 2, p1_hooks[j // 2])

    pending = None
    for t in range(D // DT):
        if pending is not None:
            pending.wait()

        @pl.loop(0, FF // 384)
        def _(r):
            part = mm(ht[rows_at(r, 384), :], gm[:, DT * t : DT * t + DT]).astype(BF16)
            stage_d[r // 2, pl.ds(2 * (r % 2), 2)] = part.reshape(2, 192, DT)

        plan.run("gd", t)
        pending = pltpu.make_async_copy(stage_d, gdown_h.at[t], so.at[18])
        pending.start()
    pending.wait()
    plan.run("wd", 0)
    cwd = [mv.start(part, wdown.at[j]) for j, part in enumerate(down_parts)]
    plan.run("wd", 1)
    for c in cwd:
        c.wait()
    first_hooks, second_hooks = ({n: plan.actions("p2", n) for n in range(k, 2 * blocks, 2)} for k in range(2))

    @pl.loop(0, blocks)
    def _(i):
        at = rows_at(i, TB)
        n2, r2 = normalize(x[at, :])
        gmb = gm[at, :]
        acc = x[at, :] + vecs[11:12, :]
        ga2 = jnp.zeros((TB, D), F32)
        for j in range(4):
            acc = acc + mm(h[at, D * j : D * j + D], wdown[j])
            guf = mm_t(gmb, wdown[j]) * gu[at, D * j : D * j + D].astype(F32)
            gub = guf.astype(BF16)
            gu[at, D * j : D * j + D] = gub
            sums[4 + j] += fold8(gub.astype(F32))
            ga2 = ga2 + mm_t(gub, win[j])
        x[at, :] = acc * live_rows(i)
        run_hooks(2 * i, first_hooks)
        gyb = gy[at, :]
        sums[8] += fold8(gmb.astype(F32))
        sums[2] += fold8(ga2 * n2)
        sums[3] += fold8(ga2)
        gx1 = gyb + norm_back(ga2, vecs[5:6, :], n2, r2)
        gy[at, :] = gx1
        for c in out_copies(i):
            c.start()
        gbb = gx1.astype(BF16)
        gb[at, :] = gbb
        sums[1] += fold8(gbb.astype(F32))
        go = mm_t(gbb, wout[...]).astype(BF16).astype(F32)
        prod = go * o[at, :].astype(F32)
        hi = prod.astype(BF16)
        lo = (prod - hi.astype(F32)).astype(BF16)
        dots[:, at] = mm_t(heads, hi) + mm_t(heads, lo)
        low = lax.rem(lax.broadcasted_iota(jnp.int32, (TB, D), 1), 128) < 64
        go0[at, :] = jnp.where(low, go, 0.0).astype(BF16)
        go1[at, :] = jnp.where(low, 0.0, go).astype(BF16)
        run_hooks(2 * i + 1, second_hooks)

    outs += [mv.start(gb, gb_h), mv.start(go0, go0_h), mv.start(go1, go1_h)]
    copies = []
    for j in range(4):
        if j > 1:
            copies[j - 2].wait()

        @pl.loop(0, 2)
        def _(r):
            part = mm(a2t[rows_at(r, 384), :], gu[:, D * j : D * j + D]).astype(BF16)
            stage[j % 2, pl.ds(2 * r, 2)] = part.reshape(2, 4, 48, D)

        plan.run("gi", j)
        copies.append(pltpu.make_async_copy(stage.at[j % 2], gin_h.at[j], so.at[19 + j % 2]))
        copies[j].start()
    plan.run("end", 0)
    for c in copies[2:] + outs:
        c.wait()
    for i in range(blocks):
        for c in out_copies(i):
            c.wait()
    if linked:
        links.finish()


DT = 256


def store_lanes(out, places, total):
    for source, target, width in places:
        out[:, target : target + width] = total[:, source : source + width]


def call_b(linked, sid, x, o, gout, vecs, wout, win, wdown):
    out = [sds(TOK, F32), sds(TOK, F32)] + [sds(TOK, BF16)] * 3 + [
        sds((16, BLOCK), F32), sds((D // DT, 4, 4, 192, DT), BF16), sds((4, 4, 4, 48, D), BF16), sds((9, 8, D), F32)]
    out_specs = [ANY] * 5 + [VMEM, ANY, ANY, VMEM]
    scratch = [vm(TOK, F32), vm(TOK, BF16), vm(TOK, F32), vm((D, D), BF16), vm((4, D, D), BF16), vm((4, D, D), BF16),
               vm(TOK, BF16), vm(TOKT, BF16), vm((FF, BLOCK), BF16), vm((BLOCK, FF), BF16), vm((BLOCK, FF), BF16),
               vm(TOK, BF16), vm(TOK, BF16), vm(TOK, BF16), vm((4, 4, 192, DT), BF16), vm((2, 4, 4, 48, D), BF16), pltpu.SemaphoreType.DMA((21,))]
    extra = {}
    if linked:
        out += [sds((FF // 32, D), F32), sds((4, FF // 4, D), BF16)]
        out_specs += [VMEM, ANY]
        slots = 3 * SCATTER_SLOTS + GATHER_SLOTS
        scratch += 3 * scatter_bufs(FF // 32, DT) + [pltpu.SemaphoreType.DMA((n,)) for n in (4, slots, slots)]
        extra = dict(collective_id=2, has_side_effects=True)
    return pl.pallas_call(
        functools.partial(kernel_b, linked),
        name="part_b",
        out_shape=out,
        in_specs=[SMEM, ANY, ANY, ANY, VMEM, ANY, ANY, VMEM if linked else ANY],
        out_specs=out_specs,
        scratch_shapes=scratch,
        compiler_params=pltpu.CompilerParams(vmem_limit_bytes=VMEM_LIMIT, **extra),
    )(sid, x, o, gout, vecs, wout, win, wdown)


def attention_back_scores(step, q0, q1, k0, k1, v, go0, go1, lse, dots, p_ref, g_ref):
    lanes, at = step_place(step)
    row = 2 * (step // (BLOCK // QB))
    vv = v[:, lanes]
    for h, (q, k, go) in enumerate(((q0, k0, go0), (q1, k1, go1))):
        scores = mm_t(k[:, lanes], q[at, lanes])
        p = jnp.exp(scores - lse[pl.ds(row + h, 1), at])
        gp = mm_t(vv, go[at, lanes])
        g_ref[h] = (p * (gp - dots[pl.ds(row + h, 1), at])).astype(BF16)
        p_ref[h] = p.astype(BF16)


def attention_back_apply(step, p_ref, g_ref, q0, q1, kt, go0, go1, gk_acc, gv_acc, gqkv):
    lanes, at = step_place(step)
    part = lax.rem(step, BLOCK // QB)
    gk_parts, gq_parts, gv_parts = [], [], []
    for h, (q, go) in enumerate(((q0, go0), (q1, go1))):
        gv_parts.append(mm(p_ref[h], go[at, lanes]))
        gk_parts.append(mm(g_ref[h], q[at, lanes]))
        gq_parts.append(mm(kt[lanes, :], g_ref[h]))
    gk = jnp.where(low_lanes((BLOCK, 128)), gk_parts[0], gk_parts[1])
    gv = gv_parts[0] + gv_parts[1]
    gq = jnp.where(low_rows((128, QB)), gq_parts[0], gq_parts[1]) * (HEAD_DIM**-0.5)
    gqkv[0, at, lanes] = gq.T.astype(BF16)
    first = part == 0
    gk_acc[...] = jnp.where(first, gk, gk_acc[...] + gk)
    gv_acc[...] = jnp.where(first, gv, gv_acc[...] + gv)

    @pl.when(part == BLOCK // QB - 1)
    def _():
        gqkv[1, :, lanes] = gk_acc[...].astype(BF16)
        gqkv[2, :, lanes] = gv_acc[...].astype(BF16)


UNITS_C = "0123oabc"


def kernel_c(linked, sid, x_h, a1t_h, q0_h, q1_h, k0_h, k1_h, v_h, kt_h, ot_h, lse, gx1_h, gb_h, go0_h, go1_h, dots, vecs, wq_h, wk_h, wv_h, *refs):
    if linked:
        (gin_h, sums_b), refs = refs[:2], refs[2:]
    (ig_h, tg, gqkv_h, gwo_h, sums), refs = refs[:5], refs[5:]
    if linked:
        (gin_o, gout_o, gqkv_o, small_o), refs = refs[:4], refs[4:]
    (x, a1t, q0, q1, k0, k1, v, kt, ot, gx1, gb, go0, go1, w, gqkv, gk_acc, gv_acc, gw, gwo, tsum, p0, g0, p1, g1, sems), refs = refs[:25], refs[25:]
    plan = Schedule(SCHEDULE_C)
    if linked:
        bufs, (value, small_b, local_sems, send, recv) = refs[:56], refs[56:]
        peers = Peers()
        links = Links(peers, send, recv)
        peers.greet()
        third = D // 3
        for n, name in enumerate(UNITS_C):
            if n < 4:
                parts, keep = (gin_h, n), functools.partial(store_lanes, gin_o, ((0, D * n, D),))
            elif n == 4:
                parts, keep = (gwo_h,), functools.partial(store_lanes, gout_o, ((0, 0, D),))
            else:
                places = tuple((third * m, D * m + third * (n - 5), third) for m in range(3))
                parts, keep = (gqkv_h, n - 5), functools.partial(store_lanes, gqkv_o, places)
            plan.units[name] = Scatter(n, links, parts, keep, bufs[7 * n : 7 * n + 7], local_sems.at[n])
        plan.run("pre", 0)
    mv = Mover(sems)
    early = [mv.start(s, d) for s, d in ((ot_h, ot), (gb_h, gb), (q0_h, q0), (q1_h, q1), (k0_h, k0), (k1_h, k1), (v_h, v), (kt_h, kt), (go0_h, go0), (go1_h, go1))]
    late = [mv.start(a1t_h, a1t), mv.start(x_h, x), mv.start(gx1_h, gx1)]
    late += [mv.start(part, w.at[j]) for j, part in enumerate((wq_h, wk_h, wv_h))]
    for c in early[:2]:
        c.wait()
    sums[...] = jnp.zeros_like(sums)

    @pl.loop(0, 2)
    def _(r):
        gwo[pl.ds(2 * r, 2)] = mm(ot[rows_at(r, 384), :], gb[...]).astype(BF16).reshape(2, 4, 48, D)

    gwo_copy = mv.start(gwo, gwo_h)
    for c in early[2:]:
        c.wait()
    gwo_copy.wait()
    plan.run("gwo", 0)
    steps = 2 * (BLOCK // QB)
    slots = ((p0, g0), (p1, g1))

    def ahead(step, slot):
        attention_back_scores(step, q0, q1, k0, k1, v, go0, go1, lse, dots, *slot)

    def apply(step, slot):
        attention_back_apply(step, *slot, q0, q1, kt, go0, go1, gk_acc, gv_acc, gqkv)

    ahead(0, slots[0])
    late[0].wait()
    step_hooks, chunk_hooks = plan.hooks("att"), plan.hooks("gw", 0, 3)

    @pl.loop(0, 3)
    def _(chunk):
        paired_steps(steps * chunk, steps, slots, ahead, apply, step_hooks)
        for j in range(3):
            for r in range(2):
                part = mm(a1t[384 * r : 384 * r + 384, :], gqkv[j, :, rows_at(chunk, 256)]).astype(BF16)
                gw[chunk, 2 * r : 2 * r + 2, :, :, 256 * j : 256 * j + 256] = part.reshape(2, 4, 48, 256)
        copy = pltpu.make_async_copy(gw.at[chunk], gqkv_h.at[chunk], sems.at[23])
        copy.start()
        run_hooks(chunk, chunk_hooks)
        copy.wait()

    for c in late[1:]:
        c.wait()
    plan.run("gw", 3)
    gain = vecs[0:1, :]
    ln_hooks = plan.hooks("ln")

    @pl.loop(0, BLOCK // TB)
    def _(i):
        at = rows_at(i, TB)
        ga1 = mm_t(gqkv[0, at, :], w[0]) + mm_t(gqkv[1, at, :], w[1]) + mm_t(gqkv[2, at, :], w[2])
        sums[2] += fold8(gqkv[0, at, :].astype(F32))
        sums[3] += fold8(gqkv[2, at, :].astype(F32))
        n1, r1 = normalize(x[at, :])
        sums[0] += fold8(ga1 * n1)
        sums[1] += fold8(ga1)
        total = gx1[at, :] + norm_back(ga1, gain, n1, r1)
        for g in range(TB // SHORT):
            s = sid[(TB // SHORT) * i + g]
            live = (s >= 0).astype(F32)
            part = total[SHORT * g : SHORT * g + SHORT, :] * live
            x[rows_at((TB // SHORT) * i + g, SHORT), :] = part
            tsum[pl.ds((TB // SHORT) * i + g, 1), :] = jnp.sum(part, axis=0, keepdims=True)
        run_hooks(i, ln_hooks)

    ig_copy = mv.start(x, ig_h)
    if linked:
        pick = lambda ref, n: jnp.sum(ref[n], axis=0, keepdims=True)
        rows = [pick(sums, n) for n in range(4)] + [pick(sums_b, n) for n in range(1, 9)] + [jnp.zeros((4, D), F32)]
        value[0] = jnp.concatenate(rows, axis=0)
        small = SmallSum(links, value, small_b)
        small.send(0, "p")
    row = lax.broadcasted_iota(jnp.int32, (GROUPS, D), 0)
    acc = jnp.zeros((GROUPS, D), F32)
    for g in range(GROUPS):
        acc = acc + jnp.where(row == sid[g], tsum[g : g + 1, :], 0.0)
    tg[...] = acc
    if linked:
        small.take(0)
        small.send(1, "x")
        small.take(1)
        small.send(2, "y")
        plan.run("end", 0, slice(0, -1))
        small.take(2)
        small.spread()
        row, col = small_places(peers.dev)
        select = small_select(col)
        plan.run("end", 0, slice(-1, None))
        picked = lax.dot_general(small.total(), select, (((1,), (0,)), ((), ())),
                                 precision=lax.Precision.HIGHEST, preferred_element_type=F32)
        at_row = lax.broadcasted_iota(jnp.int32, (16, SMALL_LEN), 0) == row
        small_o[...] = jnp.sum(jnp.where(at_row, picked, 0.0), axis=0, keepdims=True)
        links.finish()
    ig_copy.wait()


def call_c(linked, *args):
    out = [sds(TOK, F32), sds((GROUPS, D), F32), sds((3, 4, 4, 48, D), BF16), sds((4, 4, 48, D), BF16), sds((4, 8, D), F32)]
    in_specs = [SMEM] + [ANY] * 9 + [VMEM] + [ANY] * 4 + [VMEM, VMEM, ANY, ANY, ANY]
    out_specs = [ANY, VMEM, ANY, ANY, VMEM]
    scratch = [vm(TOK, F32), vm(TOKT, BF16)] + [vm(TOK, BF16)] * 5 + [vm(TOKT, BF16)] * 2 + [vm(TOK, F32)] + [vm(TOK, BF16)] * 3
    scratch += [vm((3, D, D), BF16), vm((3, BLOCK, D), BF16), vm((BLOCK, 128), F32), vm((BLOCK, 128), F32), vm((3, 4, 4, 48, D), BF16), vm((4, 4, 48, D), BF16),
                vm((GROUPS, D), F32)] + 4 * [vm((2, BLOCK, QB), BF16)] + [pltpu.SemaphoreType.DMA((24,))]
    extra = {}
    if linked:
        in_specs += [ANY, VMEM]
        out += [sds((D // 32, n * D), F32) for n in (4, 1, 3)] + [sds((1, SMALL_LEN), F32)]
        out_specs += [VMEM] * 4
        units = len(UNITS_C)
        slots = SCATTER_SLOTS * units + 6
        scratch += units * scatter_bufs(D // 32, D) + [vm((4, 16, D), F32), vm((6, 16, D), F32)]
        scratch += [pltpu.SemaphoreType.DMA((n,)) for n in (units, slots, slots)]
        extra = dict(collective_id=3, has_side_effects=True)
    return pl.pallas_call(
        functools.partial(kernel_c, linked),
        name="part_c",
        out_shape=out,
        in_specs=in_specs,
        out_specs=out_specs,
        scratch_shapes=scratch,
        compiler_params=pltpu.CompilerParams(vmem_limit_bytes=VMEM_LIMIT, **extra),
    )(*args)


AXES = ("dp", "fsdp")
MESH = pl.DeviceIdType.MESH
SMALL = ((0, 24, 0), (24, 24, 1), (48, 24, 4), (72, 24, 5), (96, 24, 6), (120, 24, 11), (144, 48, 2), (192, 96, 7))
SMALL_ORDER = (0, 1, 3, 4, 5, 7, 2, 6)
SMALL_LEN = 384


class Peers:
    def __init__(self):
        self.z, self.f = lax.axis_index("dp"), lax.axis_index("fsdp")
        self.c = self.f % 2
        self.yx = self.f // 2
        x, y = self.yx % 2, self.yx // 2
        self.partner = self.f + 1 - 2 * self.c
        self.fx, self.fy = self.f + 2 - 4 * x, self.f + 4 - 8 * y
        self.fd = self.fx + 4 - 8 * y
        self.qx, self.qy, self.qd = self.fx // 2, self.fy // 2, self.fd // 2
        self.dev = self.z * 8 + self.f
        self.other = 1 - self.c
        self.ups = [(self.z + d) % 4 for d in range(4)]

    def up(self, d):
        return self.ups[d]

    def at(self, name, d=0):
        if name == "z":
            return (self.up(d), self.f)
        return (self.z, {"x": self.fx, "y": self.fy, "p": self.partner}[name])

    def greet(self):
        barrier = pltpu.get_barrier_semaphore()
        for target in [self.at("p"), self.at("x"), self.at("y")] + [self.at("z", d) for d in (1, 2, 3)]:
            pl.semaphore_signal(barrier, inc=1, device_id=target, device_id_type=MESH)
        pl.semaphore_wait(barrier, 6)


class View:
    def __init__(self, ref, *index):
        self.ref, self.index = ref, index

    def get(self):
        return self.ref.at[self.index] if self.index else self.ref


class Links:
    def __init__(self, peers, send, recv):
        self.peers, self.send, self.recv = peers, send, recv
        self.slots, self.sent = {}, []

    def copy(self, key, src, dst, target):
        n = self.slots.setdefault(key, len(self.slots))
        return pltpu.make_async_remote_copy(
            src_ref=src.get(), dst_ref=dst.get(), send_sem=self.send.at[n], recv_sem=self.recv.at[n],
            device_id=target, device_id_type=MESH)

    def start(self, key, src, dst, name, d=0):
        args = (key, src, dst, self.peers.at(name, d))
        self.copy(*args).start()
        self.sent.append(args)

    def arrived(self, key, dst):
        self.copy(key, dst, dst, self.peers.at("p")).wait_recv()

    def finish(self):
        for args in self.sent:
            self.copy(*args).wait_send()
        self.sent = []


GATHER_SLOTS = 19


class Gather:
    def __init__(self, name, links, own, rows, full, sem):
        self.name, self.links, self.own, self.rows, self.full, self.sem = name, links, own, rows, full, sem
        p = links.peers
        self.at = {n: pl.multiple_of(f * self.rows, 8) for n, f in (("f", p.f), ("x", p.fx), ("y", p.fy), ("d", p.fd))}
        self.across = {n: pl.multiple_of((f + 1 - 2 * p.c) * self.rows, 8)
                       for n, f in (("f", p.f), ("x", p.fx), ("y", p.fy), ("d", p.fd))}

    def key(self, *k):
        return (self.name,) + k

    def piece(self, d, n):
        return View(self.full, self.links.peers.up((4 - d) % 4), pl.ds(self.at[n], self.rows))

    def column(self, at):
        return View(self.full, slice(None), pl.ds(at, self.rows))

    def begin(self):
        here = self.piece(0, "f")
        for d in (1, 3, 2):
            self.links.start(self.key("z", d), self.own, here, "z", d)
        self.local_copy().start()

    def local_copy(self):
        return pltpu.make_async_copy(self.own.get(), self.piece(0, "f").get(), self.sem)

    def do(self, action):
        links, kind, d = self.links, action[0], int(action[1:] or 0)
        if kind == "F":
            piece = self.piece(d, "f")
            if d:
                links.arrived(self.key("z", d), piece)
            src = piece if d else self.own
            links.start(self.key("x", d), src, piece, "x")
            links.start(self.key("y", d), src, piece, "y")
            if d == 2:
                self.local_copy().wait()
                mine = self.column(self.at["f"])
                links.start(self.key("p", "f"), mine, mine, "p")
        elif kind == "S":
            px, py = self.piece(d, "x"), self.piece(d, "y")
            links.arrived(self.key("x", d), px)
            links.arrived(self.key("y", d), py)
            via, part = ("y", px) if d < 2 else ("x", py)
            links.start(self.key("d", d), part, part, via)
            if d == 2:
                for n in ("x", "y"):
                    part = self.column(self.at[n])
                    links.start(self.key("p", n), part, part, "p")
        elif kind == "T":
            for n in range(4):
                links.arrived(self.key("d", n), self.piece(n, "d"))
            part = self.column(self.at["d"])
            links.start(self.key("p", "d"), part, part, "p")
        else:
            for n in ("f", "x", "y", "d"):
                links.arrived(self.key("p", n), self.column(self.across[n]))


SCATTER_SLOTS = 10


class Scatter:
    def __init__(self, name, links, parts, keep, bufs, sem):
        self.name, self.links, self.parts, self.keep, self.sem = name, links, parts, keep, sem
        self.t, self.p, self.dx, self.dy, self.xr, self.yr, self.zr = bufs
        p, self.rows = links.peers, self.t.shape[2]
        self.here, self.there = (pl.multiple_of(c * self.rows, 8) for c in (p.c, p.other))

    def half(self, at):
        return View(self.parts[0], *self.parts[1:], slice(None), slice(None), pl.ds(at, self.rows))

    def do(self, action):
        {"B": self.begin, "F": self.first, "S": self.second, "T": self.third, "L": self.last}[action]()

    def key(self, *k):
        return (self.name,) + k

    def begin(self):
        p = self.links.peers
        self.links.start(self.key("p"), self.half(self.there), View(self.p), "p")
        self.local_copy().start()

    def local_copy(self):
        return pltpu.make_async_copy(self.half(self.here).get(), self.t, self.sem)

    def add(self, q, zs, ref, base=0):
        t = self.t

        @pl.loop(zs[0], zs[1])
        def _(i):
            t[i, q] = (t[i, q].astype(F32) + ref(i - base).astype(F32)).astype(BF16)

    def first(self):
        p, links, t = self.links.peers, self.links, self.t
        self.local_copy().wait()
        links.arrived(self.key("p"), View(self.p))
        self.add(p.qd, (0, 4), lambda i: self.p[i, p.qd])
        links.start(self.key("dx"), View(t, pl.ds(0, 2), p.qd), View(self.dx), "x")
        links.start(self.key("dy"), View(t, pl.ds(2, 2), p.qd), View(self.dy), "y")
        self.add(p.qx, (0, 4), lambda i: self.p[i, p.qx])
        links.start(self.key("x", 0), View(t, pl.ds(0, 2), p.qx), View(self.xr, pl.ds(0, 2)), "x")
        self.add(p.qy, (0, 4), lambda i: self.p[i, p.qy])
        links.start(self.key("y", 1), View(t, pl.ds(2, 2), p.qy), View(self.yr, pl.ds(2, 2)), "y")
        self.add(p.yx, (0, 4), lambda i: self.p[i, p.yx])

    def second(self):
        p, links, t = self.links.peers, self.links, self.t
        links.arrived(self.key("dy"), View(self.dy))
        self.add(p.qx, (2, 4), lambda i: self.dy[i], 2)
        links.start(self.key("x", 1), View(t, pl.ds(2, 2), p.qx), View(self.xr, pl.ds(2, 2)), "x")
        links.arrived(self.key("dx"), View(self.dx))
        self.add(p.qy, (0, 2), lambda i: self.dx[i])
        links.start(self.key("y", 0), View(t, pl.ds(0, 2), p.qy), View(self.yr, pl.ds(0, 2)), "y")

    def third(self):
        p, links, t = self.links.peers, self.links, self.t
        for n in range(2):
            links.arrived(self.key("x", n), View(self.xr, pl.ds(2 * n, 2)))
            links.arrived(self.key("y", n), View(self.yr, pl.ds(2 * n, 2)))

        @pl.loop(0, 4)
        def _(i):
            t[i, p.yx] = (t[i, p.yx].astype(F32) + self.xr[i].astype(F32) + self.yr[i].astype(F32)).astype(BF16)

        for d in (2, 1, 3):
            links.start(self.key("z", d), View(t, p.up(d), p.yx), View(self.zr, d - 1), "z", d)

    def last(self):
        p, links = self.links.peers, self.links
        for d in (1, 2, 3):
            links.arrived(self.key("z", d), View(self.zr, d - 1))
        total = self.t[p.z, p.yx].astype(F32)
        for n in range(3):
            total = total + self.zr[n].astype(F32)
        self.keep(total)


def scatter_bufs(rows, cols):
    return [pltpu.VMEM(lead + (rows, cols), BF16) for lead in ((4, 4), (4, 4), (2,), (2,), (4,), (4,), (3,))]


class SmallSum:
    def __init__(self, links, value, bufs):
        self.links, self.value, self.bufs = links, value, bufs

    def send(self, n, name):
        self.links.start(("s", n), View(self.value, n), View(self.bufs, n), name)

    def take(self, n):
        self.links.arrived(("s", n), View(self.bufs, n))
        self.value[n + 1] = self.value[n] + self.bufs[n]

    def spread(self):
        for d in (1, 2, 3):
            self.links.start(("s", 2 + d), View(self.value, 3), View(self.bufs, 2 + d), "z", d)

    def total(self):
        for d in (1, 2, 3):
            self.links.arrived(("s", 2 + d), View(self.bufs, 2 + d))
        return self.value[3] + self.bufs[3] + self.bufs[4] + self.bufs[5]


def small_places(dev):
    i = lax.broadcasted_iota(jnp.int32, (1, SMALL_LEN), 1)
    row, col = jnp.full((1, SMALL_LEN), 15, jnp.int32), jnp.full((1, SMALL_LEN), -1, jnp.int32)
    for start, n, base in SMALL:
        here = (i >= start) & (i < start + n)
        row = jnp.where(here, base + (dev * n) // D, row)
        col = jnp.where(here, (dev * n) % D + i - start, col)
    return row, col


def small_select(col):
    return (lax.broadcasted_iota(jnp.int32, (D, SMALL_LEN), 0) == col).astype(F32)


def kernel_prep(small, wqkv, wout, win, wdown, small_o, qkv_o, out_o, in_o, down_o):
    small_o[...] = jnp.broadcast_to(small[...], (8, SMALL_LEN)).astype(BF16)
    qkv_o[...] = wqkv[...].astype(BF16)
    out_o[...] = wout[...].astype(BF16)
    in_o[...] = win[...].astype(BF16)
    down_o[...] = wdown[...].astype(BF16)


def call_prep(small, weights):
    return pl.pallas_call(
        kernel_prep, name="prep",
        out_shape=[sds((8, SMALL_LEN), BF16)] + [sds(w.shape, BF16) for w in weights],
        in_specs=[VMEM] * 5, out_specs=[VMEM] * 5,
    )(small, *weights)


def build_table(gathered, staged, sem, vecs):
    copy = pltpu.make_async_copy(gathered, staged, sem)
    copy.start()
    copy.wait()
    rows = staged[...].reshape(256, SMALL_LEN).astype(F32).T
    r = lax.broadcasted_iota(jnp.int32, (256, D), 0)
    lane = lax.broadcasted_iota(jnp.int32, (256, D), 1)
    vecs[...] = jnp.zeros_like(vecs)
    for n in (24, 48, 96):
        part = [(start, base) for start, size, base in SMALL if size == n]
        values = rows[part[0][0] : part[-1][0] + n, :].astype(BF16)
        own = lax.broadcasted_iota(jnp.int32, (n, D), 0) == lax.rem(lax.broadcasted_iota(jnp.int32, (n, D), 1), n)
        for line in range(n // 24):
            source = ((lane + line * D) // n) * 8
            spread = mm(values, (r == source).astype(BF16))
            for m, (_, base) in enumerate(part):
                picked = jnp.where(own, spread[n * m : n * m + n, :], 0.0)
                vecs[base + line : base + line + 1, :] = jnp.sum(picked, axis=0, keepdims=True)


def gather_all(a):
    return lax.all_gather(a.astype(BF16), AXES, axis=0, tiled=True)


def scatter_sum(a):
    return lax.psum_scatter(a, AXES, scatter_dimension=0, tiled=True)


def split_small(row, small):
    parts, at = [], 0
    for s in small:
        parts.append(row[at : at + s.shape[0]])
        at += s.shape[0]
    return parts


def gather_plain(small, weights):
    every = lax.all_gather(jnp.concatenate([s.astype(BF16) for s in small]), AXES, axis=0, tiled=False)
    vecs, at = [], 0
    for s in small:
        vecs.append(every[:, at : at + s.shape[0]].reshape(-1, D))
        at += s.shape[0]
    vecs = jnp.concatenate(vecs + [jnp.zeros((4, D), BF16)], axis=0).astype(F32)
    return vecs, [gather_all(w) for w in weights]


def scatter_plain(sums_b, sums_c, grads, small):
    sb, sc = jnp.sum(sums_b, axis=1), jnp.sum(sums_c, axis=1)
    vectors = (sc[0], sc[1], sc[2:4].reshape(-1), sb[1], sb[2], sb[3], sb[4:8].reshape(-1), sb[8])
    devices = D // small[0].shape[0]
    packed = jnp.concatenate([g.reshape(devices, -1) for g in vectors], axis=1)
    return scatter_sum(packed).reshape(-1), [scatter_sum(g.astype(F32)) for g in grads]


def local(
    own_links,
    hidden_in, time_embed, seg_ids, pre_gain, pre_shift, qkv_weight, qv_bias, out_weight, out_bias,
    mid_gain, mid_shift, in_weight, in_bias, down_weight, down_bias, grad_out,
):
    sid = seg_ids.reshape(GROUPS, SHORT)[:, 0]
    small = (pre_gain, pre_shift, qv_bias, out_bias, mid_gain, mid_shift, in_bias, down_bias)
    weights = (qkv_weight, out_weight, in_weight, down_weight)
    if own_links:
        ordered = tuple(small[n] for n in SMALL_ORDER)
        row = jnp.concatenate(ordered + (jnp.zeros((SMALL_LEN - 288,), F32),)).reshape(1, SMALL_LEN)
        own = call_prep(row, weights)
        vecs, made, wq, (wout, win) = call_a_links(sid, hidden_in, time_embed, own[:4])
        wdown = own[4]
    else:
        vecs, (wqkv, wout, win, wdown) = gather_plain(small, weights)
        wq = [wqkv[:, D * n : D * n + D] for n in range(3)]
        made = call_a(sid, hidden_in, time_embed, vecs, wq)
    x, a1t, q0, q1, k0, k1, v, kt, o, ot, lse = made
    block_out, gx1, gb, go0, go1, dots, gdown, gin, sums_b, *more = call_b(own_links, sid, x, o, grad_out, vecs, wout, win, wdown)
    args_c = (sid, x, a1t, q0, q1, k0, k1, v, kt, ot, lse, gx1, gb, go0, go1, dots, vecs, *wq)
    if own_links:
        input_grad, time_grad, _, _, _, gin, gout, gqkv, mine = call_c(True, *args_c, gin, sums_b)
        gdown = more[0]
        parts = split_small(mine.reshape(-1), ordered)
        parts = [parts[SMALL_ORDER.index(n)] for n in range(8)]
    else:
        input_grad, time_grad, gqkv, gout, sums_c = call_c(False, *args_c)
        gdown = gdown.reshape(D // DT, FF, DT).transpose(1, 0, 2).reshape(FF, D)
        gin = gin.reshape(4, D, D).transpose(1, 0, 2).reshape(D, FF)
        gqkv = gqkv.reshape(3, D, 3, D // 3).transpose(1, 2, 0, 3).reshape(D, 3 * D)
        mine, (gdown, gin, gout, gqkv) = scatter_plain(sums_b, sums_c, (gdown, gin, gout.reshape(D, D), gqkv), small)
        parts = split_small(mine, small)
    gpg, gps, gqvb, gob, gmg, gms, gib, gdb = parts
    return (block_out, input_grad, time_grad, gpg, gps, gqkv, gqvb, gout, gob, gmg, gms, gin, gib, gdown, gdb)


def solution(mesh):
    rows, flat = P(AXES, None), P(AXES)
    own_links = dict(mesh.shape) == {"dp": 4, "fsdp": 8}
    return jax.shard_map(
        functools.partial(local, own_links),
        mesh=mesh,
        in_specs=(rows, rows, flat, flat, flat, rows, flat, rows, flat, flat, flat, rows, flat, rows, flat, rows),
        out_specs=(rows, rows, rows, flat, flat, rows, flat, rows, flat, flat, flat, rows, flat, rows, flat),
        check_vma=False,
    )
```

```python
import functools

import jax
import jax.numpy as jnp
from jax import lax
from jax.experimental import pallas as pl
from jax.experimental.pallas import tpu as pltpu
from jax.sharding import PartitionSpec as P

D = 768
HEADS = 12
HEAD_DIM = 64
FF = 3072
BLOCK = 1024
SHORT = 64
GROUPS = BLOCK // SHORT
PAIRS = HEADS // 2
TB = 256
NEG = -1e30
F32 = jnp.float32
BF16 = jnp.bfloat16
VMEM_LIMIT = 62 * 1024 * 1024
ANY = pl.BlockSpec(memory_space=pl.ANY)
VMEM = pl.BlockSpec(memory_space=pltpu.VMEM)
SMEM = pl.BlockSpec(memory_space=pltpu.SMEM)
ERFC_SCALE = 0.44
ERFC_POLY = (
    0.24822097621403005,
    0.2488708795734658,
    0.21731516533725015,
    0.21580763970434977,
    -0.020173037922183695,
    0.2966799647080617,
    -0.2779439059726245,
    0.07122249905985603,
)


def rows_at(i, size):
    return pl.ds(pl.multiple_of(i * size, size), size)


def mm(a, b):
    return lax.dot_general(a, b, (((1,), (0,)), ((), ())), preferred_element_type=F32)


def mm_t(a, b):
    return lax.dot_general(a, b, (((1,), (1,)), ((), ())), preferred_element_type=F32)


def normalize(v):
    center = v - jnp.mean(v, axis=-1, keepdims=True)
    spread = jnp.mean(center * center, axis=-1, keepdims=True)
    scale = lax.rsqrt(spread + 1e-05)
    return center * scale, scale


def norm_back(grad, gain, n, scale):
    g = grad * gain
    return scale * (
        g - jnp.mean(g, axis=-1, keepdims=True) - n * jnp.mean(g * n, axis=-1, keepdims=True)
    )


def fold8(v):
    return jnp.sum(v.reshape(v.shape[0] // 8, 8, v.shape[1]), axis=0)


def gelu_parts(u):
    v = jnp.abs(u)
    t = 1.0 / (1.0 + (ERFC_SCALE * 0.7071067811865476) * v)
    poly = t * (0.5 * ERFC_POLY[-1]) + 0.5 * ERFC_POLY[-2]
    for c in ERFC_POLY[-3::-1]:
        poly = poly * t + 0.5 * c
    e = jnp.exp2((u * u) * -0.7213475204444817)
    tail = poly * t * e
    inner = tail - v * e * 0.3989422804014327
    return jnp.maximum(u, 0.0) - v * tail, jnp.where(u >= 0, 1.0 - inner, inner)


class Mover:
    def __init__(self, sems):
        self.sems, self.next = sems, 0

    def start(self, src, dst):
        copy = pltpu.make_async_copy(src, dst, self.sems.at[self.next])
        self.next += 1
        copy.start()
        return copy


def run_hooks(step, hooks):
    for n, actions in hooks.items():
        if not actions:
            continue

        @pl.when(step == n)
        def _():
            for action in actions:
                action()


def stage_norm1(sid, time, vecs, x, a1, a1t, hooks):
    gain, shift = vecs[0:1, :], vecs[1:2, :]

    @pl.loop(0, BLOCK // 128)
    def _(i):
        parts = []
        for half in range(2):
            s = sid[2 * i + half]
            live = (s >= 0).astype(F32)
            row = time[pl.ds(jnp.maximum(s, 0), 1), :]
            parts.append((x[rows_at(2 * i + half, SHORT), :] + row) * live)
        block = jnp.concatenate(parts, axis=0)
        at = rows_at(i, 128)
        x[at, :] = block
        n, _ = normalize(block)
        a = n * gain + shift
        a1[at, :] = a.astype(BF16)
        a1t[:, at] = a.T.astype(BF16)
        run_hooks(i, hooks)


def mask_rows(sid, i, groups):
    lane = lax.rem(lax.broadcasted_iota(jnp.int32, (SHORT, 128), 1), 64)
    mq, mk = [], []
    for g in range(groups):
        s = sid[groups * i + g]
        own = jnp.where(s >= 0, s, 16)
        mk.append((lane == own).astype(F32))
        bad = ((lane < 16) & (lane != s)) | (lane == 16)
        mq.append(jnp.where(bad, NEG, 0.0))
    return jnp.concatenate(mq, axis=0), jnp.concatenate(mk, axis=0)


def low_lanes(shape):
    return lax.broadcasted_iota(jnp.int32, shape, 1) < 64


def low_rows(shape):
    return lax.broadcasted_iota(jnp.int32, shape, 0) < 64


def stage_qkv(c, sid, vecs, a1, w, q0, q1, k0, k1, kt, v, vt0, vt1, hooks):
    lo = 256 * c

    @pl.loop(0, BLOCK // TB)
    def _(i):
        at = rows_at(i, TB)
        mq, mk = mask_rows(sid, i, TB // SHORT)
        acc = mm(a1[at, :], w)
        q = (acc[:, :256] + vecs[2:3, lo : lo + 256]).astype(BF16).astype(F32) * (HEAD_DIM**-0.5)
        k = acc[:, 256:512]
        value = acc[:, 512:] + vecs[3:4, lo : lo + 256]
        kt[lo : lo + 256, at] = k.T.astype(BF16)
        v[at, lo : lo + 256] = value.astype(BF16)
        value_t = value.T
        low, low_t = low_lanes((TB, 128)), low_rows((128, TB))
        for p in range(2):
            here = slice(128 * p, 128 * p + 128)
            to = slice(lo + 128 * p, lo + 128 * p + 128)
            q0[at, to] = jnp.where(low, q[:, here], mq).astype(BF16)
            q1[at, to] = jnp.where(low, mq, q[:, here]).astype(BF16)
            k0[at, to] = jnp.where(low, k[:, here], mk).astype(BF16)
            k1[at, to] = jnp.where(low, mk, k[:, here]).astype(BF16)
            vt0[to, at] = jnp.where(low_t, value_t[here, :], 1.0).astype(BF16)
            vt1[to, at] = jnp.where(low_t, 1.0, value_t[here, :]).astype(BF16)
        run_hooks(i, hooks)


QB = 256


STEPS = PAIRS * (BLOCK // QB)


def step_place(step):
    return rows_at(step // (BLOCK // QB), 128), rows_at(lax.rem(step, BLOCK // QB), QB)


def attention_scores(step, q0, q1, k0, k1, s_ref, m_ref):
    lanes, at = step_place(step)
    for h, (q, k) in enumerate(((q0, k0), (q1, k1))):
        scores = mm_t(k[:, lanes], q[at, lanes])
        s_ref[h] = scores
        m_ref[h : h + 1, :] = jnp.max(scores, axis=0, keepdims=True)


def attention_apply(step, s_ref, m_ref, vt0, vt1, o, ot, lse):
    lanes, at = step_place(step)
    outs = []
    for h, (vt, total_row) in enumerate(((vt0, 64), (vt1, 0))):
        top = m_ref[h : h + 1, :]
        e = jnp.exp(s_ref[h] - top).astype(BF16)
        res = mm(vt[lanes, :], e)
        total = res[total_row : total_row + 1, :]
        outs.append(res * (1.0 / total))
        lse[pl.ds(2 * (step // (BLOCK // QB)) + h, 1), at] = top + jnp.log(total)
    both = jnp.where(low_rows((128, QB)), outs[0], outs[1])
    ot[lanes, at] = both.astype(BF16)
    o[at, lanes] = both.T.astype(BF16)


def paired_steps(first, count, end, slots, ahead, apply, hooks):
    parity = [{n: a for n, a in hooks.items() if n % 2 == k} for k in range(2)]

    @pl.loop(0, count // 2)
    def _(i):
        for k in range(2):
            step = first + 2 * i + k
            ahead(jnp.minimum(step + 1, end - 1), slots[1 - k])
            apply(step, slots[k])
            run_hooks(step, parity[k])


SCHEDULE_A = {
    ("pre", 0): ("s.F0", "q.F0", "k.F0", "s.F1", "s.F3", "s.F2", "s.S0", "q.F1", "s.S1", "q.F3", "s.S3", "s.S2", "q.F2", "q.S0", "q.S1", "k.F1", "k.F3", "q.S3", "s.T", "q.S2", "k.F2", "k.S0", "v.F0", "s.L",),
    ("pre", 1): ("v.F1",),
    ("norm", 1): ("v.F3", "k.S1",),
    ("norm", 3): ("k.S3", "v.F2", "o.F0",),
    ("norm", 4): ("q.T",),
    ("norm", 5): ("o.F1",),
    ("norm", 6): ("k.S2",),
    ("q", -1): ("v.S0", "o.F3", "v.S1", "o.F2", "q.L",),
    ("q", 0): ("v.S3",),
    ("q", 2): ("v.S2", "i.F0",),
    ("q", 3): ("o.S0",),
    ("att", 0): ("k.T", "o.S1", "i.F1",),
    ("att", 2): ("o.S3",),
    ("att", 4): ("k.L", "v.T", "o.S2",),
    ("att", 6): ("i.F3",),
    ("k", 0): ("v.L",),
    ("k", 2): ("i.F2", "i.S0",),
    ("att", 9): ("o.T", "i.S1",),
    ("att", 13): ("o.L", "i.S3",),
    ("v", 0): ("i.S2",),
    ("att", 17): ("d.Z",),
    ("att", 21): ("i.T",),
    ("end", 0): ("i.L",),
}
SCHEDULE_B = {
    ("pre", 0): ("d.F0", "d.F1", "d.F3", "d.F2",),
    ("p1", 1): ("d.S0",),
    ("p1", 2): ("d.S1",),
    ("p1", 3): ("d.S3",),
    ("p1", 4): ("d.S2",),
    ("p1", 7): ("d.T",),
    ("gd", 1): ("d.L", "x.B",),
    ("gd", 2): ("y.B",),
    ("p2", 0): ("x.F", "y.F",),
    ("p2", 2): ("x.S",),
    ("p2", 4): ("y.S",),
    ("p2", 5): ("x.T",),
    ("p2", 6): ("y.T",),
    ("gi", 1): ("x.L",),
    ("end", 0): ("y.L",),
}
SCHEDULE_C = {
    ("pre", 0): ("z.B", "0.B", "1.B", "2.B", "3.B",),
    ("att", 0): ("z.F",),
    ("att", 1): ("o.B", "0.F",),
    ("att", 2): ("1.F", "2.F",),
    ("att", 3): ("z.S", "3.F", "o.F",),
    ("att", 5): ("0.S",),
    ("att", 7): ("1.S",),
    ("att", 8): ("2.S",),
    ("att", 9): ("a.B",),
    ("att", 11): ("z.T",),
    ("att", 12): ("a.F", "3.S",),
    ("att", 14): ("o.S",),
    ("gw", 1): ("0.T",),
    ("att", 16): ("z.L", "1.T",),
    ("att", 17): ("b.B", "2.T",),
    ("att", 18): ("a.S",),
    ("att", 20): ("b.F", "0.L", "3.T",),
    ("att", 21): ("o.T",),
    ("att", 22): ("a.T", "1.L",),
    ("att", 23): ("b.S",),
    ("gw", 2): ("2.L",),
    ("gw", 3): ("c.B",),
    ("ln", 0): ("3.L",),
    ("ln", 1): ("b.T", "c.F", "o.L",),
    ("ln", 3): ("a.L",),
    ("end", 0): ("c.S", "b.L", "c.T", "c.L",),
}


class Schedule:
    def __init__(self, table):
        self.table, self.units = table, {}

    def actions(self, seg, step):
        found = self.table.get((seg, step), ()) if self.units else ()
        return [functools.partial(self.units[a[0]].do, a[2:]) for a in found]

    def hooks(self, seg, first=0, last=24):
        return {n: self.actions(seg, n) for n in range(first, last) if self.actions(seg, n)}

    def run(self, seg, step, part=slice(None)):
        for action in self.actions(seg, step)[part]:
            action()


def kernel_a(linked, sid, hidden, time, *refs):
    if linked:
        own, refs = refs[:5], refs[5:]
        vecs, refs = refs[0], refs[1:]
    else:
        (vecs, *wq), refs = refs[:4], refs[4:]
    (x_h, a1t_h, q0_h, q1_h, k0_h, k1_h, v_h, kt_h, o_h, ot_h, lse), refs = refs[:11], refs[11:]
    if linked:
        full, refs = refs[:7], refs[7:]
        wq = full[1:4]
    (x, a1, a1t, q0, q1, k0, k1, v, kt, vt0, vt1, o, ot, w, s0, m0, s1, m1, sems), refs = refs[:19], refs[19:]
    mv = Mover(sems)
    cx = mv.start(hidden, x)
    plan = Schedule(SCHEDULE_A)
    if linked:
        staged, local_sems, send, recv = refs
        peers = Peers()
        links = Links(peers, send, recv)
        peers.greet()
        small, qkv, out, inn, down = own
        pieces = [View(small)] + [View(qkv, slice(None), pl.ds(D * n, D)) for n in range(3)] + [View(out), View(inn), View(down)]
        rows = (small.shape[0],) + 5 * (D // 32,) + (FF // 32,)
        for n, name in enumerate("sqkvoid"):
            kind = Line if name == "d" else Gather
            plan.units[name] = kind(n, links, pieces[n], rows[n], full[n], local_sems.at[n])
            plan.units[name].begin()
    run, hooks = plan.run, plan.hooks
    run("pre", 0)
    if linked:
        build_table(full[0], staged, local_sems.at[7], vecs)
    run("pre", 1)
    cx.wait()
    stage_norm1(sid, time, vecs, x, a1, a1t, hooks("norm"))
    outs = [mv.start(x, x_h), mv.start(a1t, a1t_h)]

    def weight(name, j):
        run(name, -1)
        copy = mv.start(wq[j], w.at[j])
        copy.wait()
        return w[j].reshape(D, D)

    slots = ((s0, m0), (s1, m1))

    def ahead(step, slot):
        attention_scores(step, q0, q1, k0, k1, *slot)

    def apply(step, slot):
        attention_apply(step, *slot, vt0, vt1, o, ot, lse)

    steps = STEPS // 3
    for c, name in enumerate("qkv"):
        stage_qkv(c, sid, vecs, a1, weight(name, c), q0, q1, k0, k1, kt, v, vt0, vt1, hooks(name))
        if c == 2:
            outs += [mv.start(a, b) for a, b in ((q0, q0_h), (q1, q1_h), (k0, k0_h), (k1, k1_h), (kt, kt_h), (v, v_h))]
        ahead(steps * c, slots[0])
        paired_steps(steps * c, steps, steps * (c + 1), slots, ahead, apply, plan.hooks("att", steps * c, steps * (c + 1)))
    outs += [mv.start(o, o_h), mv.start(ot, ot_h)]
    run("end", 0)
    for copy in outs:
        copy.wait()
    if linked:
        links.finish()


def sds(shape, dtype):
    return jax.ShapeDtypeStruct(shape, dtype)


TOK = (BLOCK, D)
TOKT = (D, BLOCK)


def vm(shape, dtype):
    return pltpu.VMEM(shape, dtype)


OUT_A = [sds(TOK, F32), sds(TOKT, BF16)] + [sds(TOK, BF16)] * 5 + [sds(TOKT, BF16), sds(TOK, BF16), sds(TOKT, BF16), sds((16, BLOCK), F32)]
SCRATCH_A = [vm(TOK, F32), vm(TOK, BF16), vm(TOKT, BF16)] + [vm(TOK, BF16)] * 5 + [vm(TOKT, BF16)] * 3 + [
    vm(TOK, BF16), vm(TOKT, BF16), vm((3, 4, D // 4, D), BF16)] + 2 * [vm((2, BLOCK, QB), F32), vm((8, QB), F32)] + [pltpu.SemaphoreType.DMA((16,))]


def call_a(sid, hidden, time, vecs, wq):
    return pl.pallas_call(
        functools.partial(kernel_a, False),
        name="part_a",
        out_shape=OUT_A,
        in_specs=[SMEM, ANY, VMEM, VMEM, ANY, ANY, ANY],
        out_specs=[ANY] * 10 + [VMEM],
        scratch_shapes=SCRATCH_A,
        compiler_params=pltpu.CompilerParams(vmem_limit_bytes=VMEM_LIMIT),
    )(sid, hidden, time, vecs, *[a.reshape(4, D // 4, D) for a in wq])


def call_a_links(sid, hidden, time, own):
    small, qkv, out, inn, down = own
    sizes = [small.shape] + [(D // 32, D)] * 4 + [inn.shape]
    slots = GATHER_SLOTS * 7
    res = pl.pallas_call(
        functools.partial(kernel_a, True),
        name="part_a",
        out_shape=[sds((16, D), F32)] + OUT_A + [sds((4, 8 * r, c), BF16) for r, c in sizes] + [sds((4, FF // 32, D), BF16)],
        in_specs=[SMEM, ANY, VMEM] + [VMEM] * 5,
        out_specs=[VMEM] + [ANY] * 10 + [VMEM] + [ANY] * 7,
        scratch_shapes=SCRATCH_A + [vm((4, 64, SMALL_LEN), BF16)] + [pltpu.SemaphoreType.DMA((n,)) for n in (8, slots, slots)],
        compiler_params=pltpu.CompilerParams(vmem_limit_bytes=VMEM_LIMIT, collective_id=1, has_side_effects=True),
    )(sid, hidden, time, *own)
    full = [a.reshape(-1, a.shape[-1]) for a in res[13:18]]
    return res[0], res[1:12], full[:3], full[3:], res[18]


def kernel_b(linked, sid, x_h, o_h, gout_h, vecs, wout_h, win_h, wdown_h,
             out_h, gx1_h, gb_h, go0_h, go1_h, dots, gdown_h, gin_h, sums, *refs):
    if linked:
        (gdown_o, down_f), refs = refs[:2], refs[2:]
    (x, o, gy, wout, win, wdown, gm, a2t, ht, h, gu, gb, go0, go1, stage_d, stage, *u_refs, sems), refs = refs[:19], refs[19:]
    plan = Schedule(SCHEDULE_B)
    if linked:
        bufs, (local_sems, send, recv) = refs[:14], refs[14:]
        peers = Peers()
        links = Links(peers, send, recv)
        peers.greet()
        plan.units["d"] = Plane(3, links, View(wdown_h), FF // 32, down_f, local_sems.at[3])
        for n, name in enumerate("xy"):
            keep = functools.partial(store_lanes, gdown_o, ((0, DT * n, DT),))
            plan.units[name] = Scatter(n, links, (gdown_h, n), keep, bufs[7 * n : 7 * n + 7], local_sems.at[n])
        plan.run("pre", 0)
    mv = Mover(sems)
    cx, co, cg = mv.start(x_h, x), mv.start(o_h, o), mv.start(gout_h, gy)
    cwo = mv.start(wout_h, wout)
    cwi = [mv.start(win_h.at[:, pl.ds(D * j, D)], win.at[j]) for j in range(4)]
    p1_hooks = [{n: plan.actions("p1", n) for n in range(k, 8, 2)} for k in range(2)]
    sums[...] = jnp.zeros_like(sums)
    for c in [cx, co, cg, cwo] + cwi:
        c.wait()
    lane = lax.broadcasted_iota(jnp.int32, (16, D), 1) // HEAD_DIM
    heads = (lane == lax.broadcasted_iota(jnp.int32, (16, D), 0)).astype(BF16)
    blocks = BLOCK // TB
    outs = []
    so = mv.sems

    def out_copies(i):
        at = rows_at(i, TB)
        return [pltpu.make_async_copy(x.at[at, :], out_h.at[at, :], so.at[24]),
                pltpu.make_async_copy(gy.at[at, :], gx1_h.at[at, :], so.at[25])]

    def live_rows(i):
        return jnp.concatenate(
            [jnp.full((SHORT, 1), (sid[(TB // SHORT) * i + g] >= 0).astype(F32), F32) for g in range(TB // SHORT)], axis=0)

    @pl.loop(0, blocks)
    def _(i):
        at = rows_at(i, TB)
        x1 = x[at, :] + mm(o[at, :], wout[...]) + vecs[4:5, :]
        x[at, :] = x1
        n2, _ = normalize(x1)
        a2f = n2 * vecs[5:6, :] + vecs[6:7, :]
        a2 = a2f.astype(BF16)
        a2t[:, at] = a2f.T.astype(BF16)
        gyb = gy[at, :] * live_rows(i)
        gy[at, :] = gyb
        gm[at, :] = gyb.astype(BF16)
        u_refs[0][...] = mm(a2, win[0]) + vecs[7:8, :]
        for j in range(4):
            if j < 3:
                u_refs[1 - j % 2][...] = mm(a2, win[j + 1]) + vecs[8 + j : 9 + j, :]
            hf, slope = gelu_parts(u_refs[j % 2][...])
            ht[D * j : D * j + D, at] = hf.T.astype(BF16)
            h[at, D * j : D * j + D] = hf.astype(BF16)
            gu[at, D * j : D * j + D] = slope.astype(BF16)
            if j % 2:
                run_hooks(2 * i + j // 2, p1_hooks[j // 2])

    pending = None
    for t in range(D // DT):
        if pending is not None:
            pending.wait()

        @pl.loop(0, FF // D)
        def _(r):
            part = mm(ht[rows_at(r, D), :], gm[:, DT * t : DT * t + DT]).astype(BF16)
            stage_d[r] = part.reshape(4, 192, DT)

        plan.run("gd", t)
        pending = pltpu.make_async_copy(stage_d, gdown_h.at[t], so.at[26])
        pending.start()
    pending.wait()
    plan.run("wd", 0)
    if linked:
        cwd = [mv.start(wdown_h, wdown.at[:, peers.f])]
        for n in range(1, 8):
            f = (peers.f + n) % 8
            cwd.append(mv.start(down_f.at[:, f], wdown.at[:, f]))
    else:
        cwd = [mv.start(wdown_h, wdown)]
    plan.run("wd", 1)
    for c in cwd:
        c.wait()
    first_hooks, second_hooks = ({n: plan.actions("p2", n) for n in range(k, 2 * blocks, 2)} for k in range(2))

    @pl.loop(0, blocks)
    def _(i):
        at = rows_at(i, TB)
        n2, r2 = normalize(x[at, :])
        gmb = gm[at, :]
        acc = x[at, :] + vecs[11:12, :]
        ga2 = jnp.zeros((TB, D), F32)
        for j in range(4):
            acc = acc + mm(h[at, D * j : D * j + D], wdown[j].reshape(D, D))
            guf = mm_t(gmb, wdown[j].reshape(D, D)) * gu[at, D * j : D * j + D].astype(F32)
            gub = guf.astype(BF16)
            gu[at, D * j : D * j + D] = gub
            sums[4 + j] += fold8(gub.astype(F32))
            ga2 = ga2 + mm_t(gub, win[j])
        x[at, :] = acc * live_rows(i)
        run_hooks(2 * i, first_hooks)
        gyb = gy[at, :]
        sums[8] += fold8(gmb.astype(F32))
        sums[2] += fold8(ga2 * n2)
        sums[3] += fold8(ga2)
        gx1 = gyb + norm_back(ga2, vecs[5:6, :], n2, r2)
        gy[at, :] = gx1
        for c in out_copies(i):
            c.start()
        gbb = gx1.astype(BF16)
        gb[at, :] = gbb
        sums[1] += fold8(gbb.astype(F32))
        go = mm_t(gbb, wout[...]).astype(BF16).astype(F32)
        prod = go * o[at, :].astype(F32)
        hi = prod.astype(BF16)
        lo = (prod - hi.astype(F32)).astype(BF16)
        dots[:, at] = mm_t(heads, hi) + mm_t(heads, lo)
        low = lax.rem(lax.broadcasted_iota(jnp.int32, (TB, D), 1), 128) < 64
        go0[at, :] = jnp.where(low, go, 0.0).astype(BF16)
        go1[at, :] = jnp.where(low, 0.0, go).astype(BF16)
        run_hooks(2 * i + 1, second_hooks)

    outs += [mv.start(gb, gb_h), mv.start(go0, go0_h), mv.start(go1, go1_h)]
    copies = []
    for j in range(4):
        if j > 1:
            copies[j - 2].wait()

        part = mm(a2t[...], gu[:, D * j : D * j + D]).astype(BF16)
        stage[j % 2] = part.reshape(4, 4, 48, D)
        plan.run("gi", j)
        copies.append(pltpu.make_async_copy(stage.at[j % 2], gin_h.at[j], so.at[27 + j % 2]))
        copies[j].start()
    plan.run("end", 0)
    for c in copies[2:] + outs:
        c.wait()
    for i in range(blocks):
        for c in out_copies(i):
            c.wait()
    if linked:
        links.finish()


DT = 256


def store_lanes(out, places, total):
    for source, target, width in places:
        out[:, target : target + width] = total[:, source : source + width]


def call_b(linked, sid, x, o, gout, vecs, wout, win, wdown):
    out = [sds(TOK, F32), sds(TOK, F32)] + [sds(TOK, BF16)] * 3 + [
        sds((16, BLOCK), F32), sds((D // DT, 4, 4, 192, DT), BF16), sds((4, 4, 4, 48, D), BF16), sds((9, 8, D), F32)]
    out_specs = [ANY] * 5 + [VMEM, ANY, ANY, VMEM]
    scratch = [vm(TOK, F32), vm(TOK, BF16), vm(TOK, F32), vm((D, D), BF16), vm((4, D, D), BF16), vm((4, 8, FF // 32, D), BF16),
               vm(TOK, BF16), vm(TOKT, BF16), vm((FF, BLOCK), BF16), vm((BLOCK, FF), BF16), vm((BLOCK, FF), BF16),
               vm(TOK, BF16), vm(TOK, BF16), vm(TOK, BF16), vm((4, 4, 192, DT), BF16), vm((2, 4, 4, 48, D), BF16), vm((TB, D), F32), vm((TB, D), F32), pltpu.SemaphoreType.DMA((29,))]
    extra = {}
    if linked:
        out += [sds((FF // 32, 2 * DT), F32), sds((4, 8, FF // 32, D), BF16)]
        out_specs += [VMEM, ANY]
        slots = 2 * SCATTER_SLOTS + GATHER_SLOTS
        scratch += 2 * scatter_bufs(FF // 32, DT) + [pltpu.SemaphoreType.DMA((n,)) for n in (4, slots, slots)]
        extra = dict(collective_id=2, has_side_effects=True)
    return pl.pallas_call(
        functools.partial(kernel_b, linked),
        name="part_b",
        out_shape=out,
        in_specs=[SMEM, ANY, ANY, ANY, VMEM, ANY, ANY, ANY],
        out_specs=out_specs,
        scratch_shapes=scratch,
        compiler_params=pltpu.CompilerParams(vmem_limit_bytes=VMEM_LIMIT, **extra),
    )(sid, x, o, gout, vecs, wout, win, wdown)


def attention_back_scores(step, q0, q1, k0, k1, v, go0, go1, lse, dots, p_ref, g_ref):
    lanes, at = step_place(step)
    row = 2 * (step // (BLOCK // QB))
    vv = v[:, lanes]
    for h, (q, k, go) in enumerate(((q0, k0, go0), (q1, k1, go1))):
        scores = mm_t(k[:, lanes], q[at, lanes])
        p = jnp.exp(scores - lse[pl.ds(row + h, 1), at])
        gp = mm_t(vv, go[at, lanes])
        g_ref[h] = (p * (gp - dots[pl.ds(row + h, 1), at])).astype(BF16)
        p_ref[h] = p.astype(BF16)


def attention_back_apply(step, p_ref, g_ref, q0, q1, kt, go0, go1, gk_acc, gv_acc, gqkv):
    lanes, at = step_place(step)
    part = lax.rem(step, BLOCK // QB)
    gk_parts, gq_parts, gv_parts = [], [], []
    for h, (q, go) in enumerate(((q0, go0), (q1, go1))):
        gv_parts.append(mm(p_ref[h], go[at, lanes]))
        gk_parts.append(mm(g_ref[h], q[at, lanes]))
        gq_parts.append(mm(kt[lanes, :], g_ref[h]))
    gk = jnp.where(low_lanes((BLOCK, 128)), gk_parts[0], gk_parts[1])
    gv = gv_parts[0] + gv_parts[1]
    gq = jnp.where(low_rows((128, QB)), gq_parts[0], gq_parts[1]) * (HEAD_DIM**-0.5)
    gqkv[0, at, lanes] = gq.T.astype(BF16)
    first = part == 0
    gk_acc[...] = jnp.where(first, gk, gk_acc[...] + gk)
    gv_acc[...] = jnp.where(first, gv, gv_acc[...] + gv)

    @pl.when(part == BLOCK // QB - 1)
    def _():
        gqkv[1, :, lanes] = gk_acc[...].astype(BF16)
        gqkv[2, :, lanes] = gv_acc[...].astype(BF16)


UNITS_C = "0123oabcz"


def kernel_c(linked, sid, x_h, a1t_h, q0_h, q1_h, k0_h, k1_h, v_h, kt_h, ot_h, lse, gx1_h, gb_h, go0_h, go1_h, dots, vecs, w0_h, w1_h, w2_h, *refs):
    if linked:
        (gin_h, sums_b, gdown_h, down_part), refs = refs[:4], refs[4:]
    (ig_h, tg, gqkv_h, gwo_h, sums), refs = refs[:5], refs[5:]
    if linked:
        (gin_o, gout_o, gqkv_o, small_o, gdown_o), refs = refs[:5], refs[5:]
    (x, a1t, q0, q1, k0, k1, v, kt, ot, gx1, gb, go0, go1, w, gqkv, gk_acc, gv_acc, gw, gwo, tsum, p0, g0, p1, g1, sems), refs = refs[:25], refs[25:]
    plan = Schedule(SCHEDULE_C)
    if linked:
        bufs, (value, small_b, local_sems, send, recv) = refs[:63], refs[63:]
        peers = Peers()
        links = Links(peers, send, recv)
        peers.greet()
        third = D // 3
        for n, name in enumerate(UNITS_C):
            if n < 4:
                parts, keep = (gin_h, n), functools.partial(store_lanes, gin_o, ((0, D * n, D),))
            elif n == 4:
                parts, keep = (gwo_h,), functools.partial(store_lanes, gout_o, ((0, 0, D),))
            elif n == 8:
                parts, keep = (gdown_h, 2), functools.partial(store_lanes, gdown_o, ((0, 2 * DT, DT),))
            else:
                places = tuple((third * m, D * m + third * (n - 5), third) for m in range(3))
                parts, keep = (gqkv_h, n - 5), functools.partial(store_lanes, gqkv_o, places)
            plan.units[name] = Scatter(n, links, parts, keep, bufs[7 * n : 7 * n + 7], local_sems.at[n])
        plan.run("pre", 0)
        gdown_o[:, : 2 * DT] = down_part[...]
    mv = Mover(sems)
    early = [mv.start(s, d) for s, d in ((ot_h, ot), (gb_h, gb), (q0_h, q0), (q1_h, q1), (k0_h, k0), (k1_h, k1), (v_h, v), (kt_h, kt), (go0_h, go0), (go1_h, go1))]
    late = [mv.start(a1t_h, a1t), mv.start(x_h, x), mv.start(gx1_h, gx1)]
    late += [mv.start(part.at[:, pl.ds(256 * j, 256)], w.at[j, :, pl.ds(256 * n, 256)]) for n, part in enumerate((w0_h, w1_h, w2_h)) for j in range(3)]
    for c in early[:2]:
        c.wait()
    sums[...] = jnp.zeros_like(sums)

    @pl.loop(0, 2)
    def _(r):
        gwo[pl.ds(2 * r, 2)] = mm(ot[rows_at(r, 384), :], gb[...]).astype(BF16).reshape(2, 4, 48, D)

    gwo_copy = mv.start(gwo, gwo_h)
    for c in early[2:]:
        c.wait()
    gwo_copy.wait()
    plan.run("gwo", 0)
    steps = 2 * (BLOCK // QB)
    slots = ((p0, g0), (p1, g1))

    def ahead(step, slot):
        attention_back_scores(step, q0, q1, k0, k1, v, go0, go1, lse, dots, *slot)

    def apply(step, slot):
        attention_back_apply(step, *slot, q0, q1, kt, go0, go1, gk_acc, gv_acc, gqkv)

    ahead(0, slots[0])
    late[0].wait()
    step_hooks, chunk_hooks = plan.hooks("att"), plan.hooks("gw", 0, 3)

    @pl.loop(0, 3)
    def _(chunk):
        paired_steps(steps * chunk, steps, STEPS, slots, ahead, apply, step_hooks)
        for j in range(3):
            for r in range(2):
                part = mm(a1t[384 * r : 384 * r + 384, :], gqkv[j, :, rows_at(chunk, 256)]).astype(BF16)
                gw[chunk, 2 * r : 2 * r + 2, :, :, 256 * j : 256 * j + 256] = part.reshape(2, 4, 48, 256)
        copy = pltpu.make_async_copy(gw.at[chunk], gqkv_h.at[chunk], sems.at[31])
        copy.start()
        run_hooks(chunk, chunk_hooks)
        copy.wait()

    for c in late[1:]:
        c.wait()
    plan.run("gw", 3)
    gain = vecs[0:1, :]
    ln_hooks = plan.hooks("ln")

    @pl.loop(0, BLOCK // TB)
    def _(i):
        at = rows_at(i, TB)
        ga1 = mm_t(gqkv[0, at, :], w[0]) + mm_t(gqkv[1, at, :], w[1]) + mm_t(gqkv[2, at, :], w[2])
        sums[2] += fold8(gqkv[0, at, :].astype(F32))
        sums[3] += fold8(gqkv[2, at, :].astype(F32))
        n1, r1 = normalize(x[at, :])
        sums[0] += fold8(ga1 * n1)
        sums[1] += fold8(ga1)
        total = gx1[at, :] + norm_back(ga1, gain, n1, r1)
        for g in range(TB // SHORT):
            s = sid[(TB // SHORT) * i + g]
            live = (s >= 0).astype(F32)
            part = total[SHORT * g : SHORT * g + SHORT, :] * live
            x[rows_at((TB // SHORT) * i + g, SHORT), :] = part
            tsum[pl.ds((TB // SHORT) * i + g, 1), :] = jnp.sum(part, axis=0, keepdims=True)
        run_hooks(i, ln_hooks)

    ig_copy = mv.start(x, ig_h)
    if linked:
        pick = lambda ref, n: jnp.sum(ref[n], axis=0, keepdims=True)
        rows = [pick(sums, n) for n in range(4)] + [pick(sums_b, n) for n in range(1, 9)] + [jnp.zeros((4, D), F32)]
        value[0] = jnp.concatenate(rows, axis=0)
        small = SmallSum(links, value, small_b)
        small.send(0, "p")
    row = lax.broadcasted_iota(jnp.int32, (GROUPS, D), 0)
    acc = jnp.zeros((GROUPS, D), F32)
    for g in range(GROUPS):
        acc = acc + jnp.where(row == sid[g], tsum[g : g + 1, :], 0.0)
    tg[...] = acc
    if linked:
        small.take(0)
        small.send(1, "x")
        small.take(1)
        small.send(2, "y")
        plan.run("end", 0, slice(0, -1))
        small.take(2)
        small.spread()
        row, col = small_places(peers.dev)
        select = small_select(col).astype(BF16)
        plan.run("end", 0, slice(-1, None))
        left, picked = small.total(), 0.0
        for _ in range(3):
            part = left.astype(BF16)
            picked = picked + mm(part, select)
            left = left - part.astype(F32)
        at_row = lax.broadcasted_iota(jnp.int32, (16, SMALL_LEN), 0) == row
        small_o[...] = jnp.sum(jnp.where(at_row, picked, 0.0), axis=0, keepdims=True)
        links.finish()
    ig_copy.wait()


def call_c(linked, *args):
    out = [sds(TOK, F32), sds((GROUPS, D), F32), sds((3, 4, 4, 48, D), BF16), sds((4, 4, 48, D), BF16), sds((4, 8, D), F32)]
    in_specs = [SMEM] + [ANY] * 9 + [VMEM] + [ANY] * 4 + [VMEM, VMEM, ANY, ANY, ANY]
    out_specs = [ANY, VMEM, ANY, ANY, VMEM]
    scratch = [vm(TOK, F32), vm(TOKT, BF16)] + [vm(TOK, BF16)] * 5 + [vm(TOKT, BF16)] * 2 + [vm(TOK, F32)] + [vm(TOK, BF16)] * 3
    scratch += [vm((3, D, D), BF16), vm((3, BLOCK, D), BF16), vm((BLOCK, 128), F32), vm((BLOCK, 128), F32), vm((3, 4, 4, 48, D), BF16), vm((4, 4, 48, D), BF16),
                vm((GROUPS, D), F32)] + 4 * [vm((2, BLOCK, QB), BF16)] + [pltpu.SemaphoreType.DMA((32,))]
    extra = {}
    if linked:
        in_specs += [ANY, VMEM, ANY, VMEM]
        out += [sds((D // 32, n * D), F32) for n in (4, 1, 3)] + [sds((1, SMALL_LEN), F32), sds((FF // 32, D), F32)]
        out_specs += [VMEM] * 5
        units = len(UNITS_C)
        slots = SCATTER_SLOTS * units + 6
        scratch += (units - 1) * scatter_bufs(D // 32, D) + scatter_bufs(FF // 32, DT) + [vm((4, 16, D), F32), vm((6, 16, D), F32)]
        scratch += [pltpu.SemaphoreType.DMA((n,)) for n in (units, slots, slots)]
        extra = dict(collective_id=3, has_side_effects=True)
    return pl.pallas_call(
        functools.partial(kernel_c, linked),
        name="part_c",
        out_shape=out,
        in_specs=in_specs,
        out_specs=out_specs,
        scratch_shapes=scratch,
        compiler_params=pltpu.CompilerParams(vmem_limit_bytes=VMEM_LIMIT, **extra),
    )(*args)


AXES = ("dp", "fsdp")
MESH = pl.DeviceIdType.MESH
SMALL = ((0, 24, 0), (24, 24, 1), (48, 24, 4), (72, 24, 5), (96, 24, 6), (120, 24, 11), (144, 48, 2), (192, 96, 7))
SMALL_ORDER = (0, 1, 3, 4, 5, 7, 2, 6)
SMALL_LEN = 384


class Peers:
    def __init__(self):
        self.z, self.f = lax.axis_index("dp"), lax.axis_index("fsdp")
        self.c = self.f % 2
        self.yx = self.f // 2
        x, y = self.yx % 2, self.yx // 2
        self.partner = self.f + 1 - 2 * self.c
        self.fx, self.fy = self.f + 2 - 4 * x, self.f + 4 - 8 * y
        self.fd = self.fx + 4 - 8 * y
        self.qx, self.qy, self.qd = self.fx // 2, self.fy // 2, self.fd // 2
        self.dev = self.z * 8 + self.f
        self.other = 1 - self.c
        self.ups = [(self.z + d) % 4 for d in range(4)]

    def up(self, d):
        return self.ups[d]

    def at(self, name, d=0):
        if name == "z":
            return (self.up(d), self.f)
        return (self.z, {"x": self.fx, "y": self.fy, "p": self.partner}[name])

    def greet(self):
        barrier = pltpu.get_barrier_semaphore()
        for target in [self.at("p"), self.at("x"), self.at("y")] + [self.at("z", d) for d in (1, 2, 3)]:
            pl.semaphore_signal(barrier, inc=1, device_id=target, device_id_type=MESH)
        pl.semaphore_wait(barrier, 6)


class View:
    def __init__(self, ref, *index):
        self.ref, self.index = ref, index

    def get(self):
        return self.ref.at[self.index] if self.index else self.ref


class Links:
    def __init__(self, peers, send, recv):
        self.peers, self.send, self.recv = peers, send, recv
        self.slots, self.sent = {}, []

    def copy(self, key, src, dst, target):
        n = self.slots.setdefault(key, len(self.slots))
        return pltpu.make_async_remote_copy(
            src_ref=src.get(), dst_ref=dst.get(), send_sem=self.send.at[n], recv_sem=self.recv.at[n],
            device_id=target, device_id_type=MESH)

    def start(self, key, src, dst, name, d=0):
        args = (key, src, dst, self.peers.at(name, d))
        self.copy(*args).start()
        self.sent.append(args)

    def arrived(self, key, dst):
        self.copy(key, dst, dst, self.peers.at("p")).wait_recv()

    def finish(self):
        for args in self.sent:
            self.copy(*args).wait_send()
        self.sent = []


GATHER_SLOTS = 19


class Gather:
    def __init__(self, name, links, own, rows, full, sem):
        self.name, self.links, self.own, self.rows, self.full, self.sem = name, links, own, rows, full, sem
        p, self.deep = links.peers, len(full.shape) == 4
        place = (lambda f: f) if self.deep else (lambda f: pl.multiple_of(f * self.rows, 8))
        self.at = {n: place(f) for n, f in (("f", p.f), ("x", p.fx), ("y", p.fy), ("d", p.fd))}
        self.across = {n: place(f + 1 - 2 * p.c)
                       for n, f in (("f", p.f), ("x", p.fx), ("y", p.fy), ("d", p.fd))}

    def key(self, *k):
        return (self.name,) + k

    def piece(self, d, n):
        return View(self.full, self.links.peers.up((4 - d) % 4), self.window(self.at[n]))

    def column(self, at):
        return View(self.full, slice(None), self.window(at))

    def window(self, at):
        return at if self.deep else pl.ds(at, self.rows)

    def begin(self):
        here = self.piece(0, "f")
        for d in (1, 3, 2):
            self.links.start(self.key("z", d), self.own, here, "z", d)
        self.local_copy().start()

    def local_copy(self):
        return pltpu.make_async_copy(self.own.get(), self.piece(0, "f").get(), self.sem)

    def do(self, action):
        links, kind, d = self.links, action[0], int(action[1:] or 0)
        if kind == "F":
            piece = self.piece(d, "f")
            if d:
                links.arrived(self.key("z", d), piece)
            src = piece if d else self.own
            links.start(self.key("x", d), src, piece, "x")
            links.start(self.key("y", d), src, piece, "y")
            if d == 2:
                self.local_copy().wait()
                mine = self.column(self.at["f"])
                links.start(self.key("p", "f"), mine, mine, "p")
        elif kind == "S":
            px, py = self.piece(d, "x"), self.piece(d, "y")
            links.arrived(self.key("x", d), px)
            links.arrived(self.key("y", d), py)
            via, part = ("y", px) if d < 2 else ("x", py)
            links.start(self.key("d", d), part, part, via)
            if d == 2:
                for n in ("x", "y"):
                    part = self.column(self.at[n])
                    links.start(self.key("p", n), part, part, "p")
        elif kind == "T":
            for n in range(4):
                links.arrived(self.key("d", n), self.piece(n, "d"))
            part = self.column(self.at["d"])
            links.start(self.key("p", "d"), part, part, "p")
        else:
            for n in ("f", "x", "y", "d"):
                links.arrived(self.key("p", n), self.column(self.across[n]))


class Line(Gather):
    def piece(self, d, n):
        return View(self.full, self.links.peers.up((4 - d) % 4))

    def do(self, action):
        for d in (1, 2, 3):
            self.links.arrived(self.key("z", d), self.piece(d, "f"))
        self.local_copy().wait()


class Plane(Gather):
    def mine(self, d):
        return View(self.own.ref, self.links.peers.up((4 - d) % 4))

    def do(self, action):
        if action[0] != "F":
            return Gather.do(self, action)
        d = int(action[1:])
        for name in ("x", "y"):
            self.links.start(self.key(name, d), self.mine(d), self.piece(d, "f"), name)
        if d == 2:
            self.links.start(self.key("p", "f"), self.own, self.column(self.at["f"]), "p")


SCATTER_SLOTS = 10


class Scatter:
    def __init__(self, name, links, parts, keep, bufs, sem):
        self.name, self.links, self.parts, self.keep, self.sem = name, links, parts, keep, sem
        self.t, self.p, self.dx, self.dy, self.xr, self.yr, self.zr = bufs
        p, self.rows = links.peers, self.t.shape[2]
        self.here, self.there = (pl.multiple_of(c * self.rows, 8) for c in (p.c, p.other))

    def half(self, at):
        return View(self.parts[0], *self.parts[1:], slice(None), slice(None), pl.ds(at, self.rows))

    def do(self, action):
        {"B": self.begin, "F": self.first, "S": self.second, "T": self.third, "L": self.last}[action]()

    def key(self, *k):
        return (self.name,) + k

    def begin(self):
        p = self.links.peers
        self.links.start(self.key("p"), self.half(self.there), View(self.p), "p")
        self.local_copy().start()

    def local_copy(self):
        return pltpu.make_async_copy(self.half(self.here).get(), self.t, self.sem)

    def add(self, q, zs, ref, base=0):
        t = self.t

        @pl.loop(zs[0], zs[1])
        def _(i):
            t[i, q] = (t[i, q].astype(F32) + ref(i - base).astype(F32)).astype(BF16)

    def first(self):
        p, links, t = self.links.peers, self.links, self.t
        self.local_copy().wait()
        links.arrived(self.key("p"), View(self.p))
        self.add(p.qd, (0, 4), lambda i: self.p[i, p.qd])
        links.start(self.key("dx"), View(t, pl.ds(0, 2), p.qd), View(self.dx), "x")
        links.start(self.key("dy"), View(t, pl.ds(2, 2), p.qd), View(self.dy), "y")
        self.add(p.qx, (0, 4), lambda i: self.p[i, p.qx])
        links.start(self.key("x", 0), View(t, pl.ds(0, 2), p.qx), View(self.xr, pl.ds(0, 2)), "x")
        self.add(p.qy, (0, 4), lambda i: self.p[i, p.qy])
        links.start(self.key("y", 1), View(t, pl.ds(2, 2), p.qy), View(self.yr, pl.ds(2, 2)), "y")
        self.add(p.yx, (0, 4), lambda i: self.p[i, p.yx])

    def second(self):
        p, links, t = self.links.peers, self.links, self.t
        links.arrived(self.key("dy"), View(self.dy))
        self.add(p.qx, (2, 4), lambda i: self.dy[i], 2)
        links.start(self.key("x", 1), View(t, pl.ds(2, 2), p.qx), View(self.xr, pl.ds(2, 2)), "x")
        links.arrived(self.key("dx"), View(self.dx))
        self.add(p.qy, (0, 2), lambda i: self.dx[i])
        links.start(self.key("y", 0), View(t, pl.ds(0, 2), p.qy), View(self.yr, pl.ds(0, 2)), "y")

    def third(self):
        p, links, t = self.links.peers, self.links, self.t
        for n in range(2):
            links.arrived(self.key("x", n), View(self.xr, pl.ds(2 * n, 2)))
            links.arrived(self.key("y", n), View(self.yr, pl.ds(2 * n, 2)))

        @pl.loop(0, 4)
        def _(i):
            t[i, p.yx] = (t[i, p.yx].astype(F32) + self.xr[i].astype(F32) + self.yr[i].astype(F32)).astype(BF16)

        for d in (2, 1, 3):
            links.start(self.key("z", d), View(t, p.up(d), p.yx), View(self.zr, d - 1), "z", d)

    def last(self):
        p, links = self.links.peers, self.links
        for d in (1, 2, 3):
            links.arrived(self.key("z", d), View(self.zr, d - 1))
        total = self.t[p.z, p.yx].astype(F32)
        for n in range(3):
            total = total + self.zr[n].astype(F32)
        self.keep(total)


def scatter_bufs(rows, cols):
    return [pltpu.VMEM(lead + (rows, cols), BF16) for lead in ((4, 4), (4, 4), (2,), (2,), (4,), (4,), (3,))]


class SmallSum:
    def __init__(self, links, value, bufs):
        self.links, self.value, self.bufs = links, value, bufs

    def send(self, n, name):
        self.links.start(("s", n), View(self.value, n), View(self.bufs, n), name)

    def take(self, n):
        self.links.arrived(("s", n), View(self.bufs, n))
        self.value[n + 1] = self.value[n] + self.bufs[n]

    def spread(self):
        for d in (1, 2, 3):
            self.links.start(("s", 2 + d), View(self.value, 3), View(self.bufs, 2 + d), "z", d)

    def total(self):
        for d in (1, 2, 3):
            self.links.arrived(("s", 2 + d), View(self.bufs, 2 + d))
        return self.value[3] + self.bufs[3] + self.bufs[4] + self.bufs[5]


def small_places(dev):
    i = lax.broadcasted_iota(jnp.int32, (1, SMALL_LEN), 1)
    row, col = jnp.full((1, SMALL_LEN), 15, jnp.int32), jnp.full((1, SMALL_LEN), -1, jnp.int32)
    for start, n, base in SMALL:
        here = (i >= start) & (i < start + n)
        row = jnp.where(here, base + (dev * n) // D, row)
        col = jnp.where(here, (dev * n) % D + i - start, col)
    return row, col


def small_select(col):
    return (lax.broadcasted_iota(jnp.int32, (D, SMALL_LEN), 0) == col).astype(F32)


def kernel_prep(small, wqkv, wout, win, wdown, small_o, qkv_o, out_o, in_o, down_o):
    small_o[...] = jnp.broadcast_to(small[...], (8, SMALL_LEN)).astype(BF16)
    for c in range(3):
        for j in range(3):
            qkv_o[:, D * c + 256 * j : D * c + 256 * j + 256] = wqkv[:, D * j + 256 * c : D * j + 256 * c + 256].astype(BF16)
    out_o[...] = wout[...].astype(BF16)
    in_o[...] = win[...].astype(BF16)
    down_o[...] = wdown[...].astype(BF16)


def call_prep(small, weights):
    return pl.pallas_call(
        kernel_prep, name="prep",
        out_shape=[sds((8, SMALL_LEN), BF16)] + [sds(w.shape, BF16) for w in weights],
        in_specs=[VMEM] * 5, out_specs=[VMEM] * 5,
    )(small, *weights)


def build_table(gathered, staged, sem, vecs):
    copy = pltpu.make_async_copy(gathered, staged, sem)
    copy.start()
    copy.wait()
    rows = staged[...].reshape(256, SMALL_LEN).astype(F32).T
    r = lax.broadcasted_iota(jnp.int32, (256, D), 0)
    lane = lax.broadcasted_iota(jnp.int32, (1, D), 1)
    vecs[...] = jnp.zeros_like(vecs)
    for n in (24, 48, 96):
        part = [(start, base) for start, size, base in SMALL if size == n]
        values = rows[part[0][0] : part[-1][0] + n, :].astype(BF16)
        own = lax.broadcasted_iota(jnp.int32, (n, D), 0) == lax.rem(lane, n)
        first = (lane // n) * 8
        for line in range(n // 24):
            spread = mm(values, (r == first + 8 * line * (D // n)).astype(BF16))
            for m, (_, base) in enumerate(part):
                picked = jnp.where(own, spread[n * m : n * m + n, :], 0.0)
                vecs[base + line : base + line + 1, :] = jnp.sum(picked, axis=0, keepdims=True)


def gather_all(a):
    return lax.all_gather(a.astype(BF16), AXES, axis=0, tiled=True)


def scatter_sum(a):
    return lax.psum_scatter(a, AXES, scatter_dimension=0, tiled=True)


def split_small(row, small):
    parts, at = [], 0
    for s in small:
        parts.append(row[at : at + s.shape[0]])
        at += s.shape[0]
    return parts


def gather_plain(small, weights):
    every = lax.all_gather(jnp.concatenate([s.astype(BF16) for s in small]), AXES, axis=0, tiled=False)
    vecs, at = [], 0
    for s in small:
        vecs.append(every[:, at : at + s.shape[0]].reshape(-1, D))
        at += s.shape[0]
    vecs = jnp.concatenate(vecs + [jnp.zeros((4, D), BF16)], axis=0).astype(F32)
    return vecs, [gather_all(w) for w in weights]


def scatter_plain(sums_b, sums_c, grads, small):
    sb, sc = jnp.sum(sums_b, axis=1), jnp.sum(sums_c, axis=1)
    vectors = (sc[0], sc[1], sc[2:4].reshape(-1), sb[1], sb[2], sb[3], sb[4:8].reshape(-1), sb[8])
    devices = D // small[0].shape[0]
    packed = jnp.concatenate([g.reshape(devices, -1) for g in vectors], axis=1)
    return scatter_sum(packed).reshape(-1), [scatter_sum(g.astype(F32)) for g in grads]


def local(
    own_links,
    hidden_in, time_embed, seg_ids, pre_gain, pre_shift, qkv_weight, qv_bias, out_weight, out_bias,
    mid_gain, mid_shift, in_weight, in_bias, down_weight, down_bias, grad_out,
):
    sid = seg_ids.reshape(GROUPS, SHORT)[:, 0]
    small = (pre_gain, pre_shift, qv_bias, out_bias, mid_gain, mid_shift, in_bias, down_bias)
    weights = (qkv_weight, out_weight, in_weight, down_weight)
    if own_links:
        ordered = tuple(small[n] for n in SMALL_ORDER)
        row = jnp.concatenate(ordered + (jnp.zeros((SMALL_LEN - 288,), F32),)).reshape(1, SMALL_LEN)
        own = call_prep(row, weights)
        vecs, made, wq, (wout, win), wdown = call_a_links(sid, hidden_in, time_embed, own)
    else:
        vecs, (wqkv, wout, win, wdown) = gather_plain(small, weights)
        wq = list(wqkv.reshape(D, 3, 3, 256).transpose(2, 0, 1, 3).reshape(3, D, D))
        wdown = wdown.reshape(4, 8, FF // 32, D)
        made = call_a(sid, hidden_in, time_embed, vecs, wq)
    x, a1t, q0, q1, k0, k1, v, kt, o, ot, lse = made
    block_out, gx1, gb, go0, go1, dots, gdown, gin, sums_b, *more = call_b(own_links, sid, x, o, grad_out, vecs, wout, win, wdown)
    args_c = (sid, x, a1t, q0, q1, k0, k1, v, kt, ot, lse, gx1, gb, go0, go1, dots, vecs, *wq)
    if own_links:
        input_grad, time_grad, _, _, _, gin, gout, gqkv, mine, gdown = call_c(True, *args_c, gin, sums_b, gdown, more[0])
        parts = split_small(mine.reshape(-1), ordered)
        parts = [parts[SMALL_ORDER.index(n)] for n in range(8)]
    else:
        input_grad, time_grad, gqkv, gout, sums_c = call_c(False, *args_c)
        gdown = gdown.reshape(D // DT, FF, DT).transpose(1, 0, 2).reshape(FF, D)
        gin = gin.reshape(4, D, D).transpose(1, 0, 2).reshape(D, FF)
        gqkv = gqkv.reshape(3, D, 3, D // 3).transpose(1, 2, 0, 3).reshape(D, 3 * D)
        mine, (gdown, gin, gout, gqkv) = scatter_plain(sums_b, sums_c, (gdown, gin, gout.reshape(D, D), gqkv), small)
        parts = split_small(mine, small)
    gpg, gps, gqvb, gob, gmg, gms, gib, gdb = parts
    return (block_out, input_grad, time_grad, gpg, gps, gqkv, gqvb, gout, gob, gmg, gms, gin, gib, gdown, gdb)


def solution(mesh):
    rows, flat = P(AXES, None), P(AXES)
    own_links = dict(mesh.shape) == {"dp": 4, "fsdp": 8}
    return jax.shard_map(
        functools.partial(local, own_links),
        mesh=mesh,
        in_specs=(rows, rows, flat, flat, flat, rows, flat, rows, flat, flat, flat, rows, flat, rows, flat, rows),
        out_specs=(rows, rows, rows, flat, flat, rows, flat, rows, flat, flat, flat, rows, flat, rows, flat),
        check_vma=False,
    )
```

```python
import functools

import jax
import jax.numpy as jnp
from jax import lax
from jax.experimental import pallas as pl
from jax.experimental.pallas import tpu as pltpu
from jax.sharding import PartitionSpec as P

D = 768
HEADS = 12
HEAD_DIM = 64
FF = 3072
BLOCK = 1024
SHORT = 64
GROUPS = BLOCK // SHORT
PAIRS = HEADS // 2
TB = 256
NEG = -1e30
F32 = jnp.float32
BF16 = jnp.bfloat16
VMEM_LIMIT = 62 * 1024 * 1024
ANY = pl.BlockSpec(memory_space=pl.ANY)
VMEM = pl.BlockSpec(memory_space=pltpu.VMEM)
SMEM = pl.BlockSpec(memory_space=pltpu.SMEM)
ERFC_SCALE = 0.44
ERFC_POLY = (
    0.24822097621403005,
    0.2488708795734658,
    0.21731516533725015,
    0.21580763970434977,
    -0.020173037922183695,
    0.2966799647080617,
    -0.2779439059726245,
    0.07122249905985603,
)


def rows_at(i, size):
    return pl.ds(pl.multiple_of(i * size, size), size)


def mm(a, b):
    return lax.dot_general(a, b, (((1,), (0,)), ((), ())), preferred_element_type=F32)


def mm_t(a, b):
    return lax.dot_general(a, b, (((1,), (1,)), ((), ())), preferred_element_type=F32)


def normalize(v):
    center = v - jnp.mean(v, axis=-1, keepdims=True)
    spread = jnp.mean(center * center, axis=-1, keepdims=True)
    scale = lax.rsqrt(spread + 1e-05)
    return center * scale, scale


def norm_back(grad, gain, n, scale):
    g = grad * gain
    return scale * (
        g - jnp.mean(g, axis=-1, keepdims=True) - n * jnp.mean(g * n, axis=-1, keepdims=True)
    )


def fold8(v):
    return jnp.sum(v.reshape(v.shape[0] // 8, 8, v.shape[1]), axis=0)


def gelu_parts(u):
    v = jnp.abs(u)
    t = 1.0 / (1.0 + (ERFC_SCALE * 0.7071067811865476) * v)
    poly = t * (0.5 * ERFC_POLY[-1]) + 0.5 * ERFC_POLY[-2]
    for c in ERFC_POLY[-3::-1]:
        poly = poly * t + 0.5 * c
    e = jnp.exp2((u * u) * -0.7213475204444817)
    tail = poly * t * e
    inner = tail - v * e * 0.3989422804014327
    return jnp.maximum(u, 0.0) - v * tail, jnp.where(u >= 0, 1.0 - inner, inner)


class Mover:
    def __init__(self, sems):
        self.sems, self.next = sems, 0

    def start(self, src, dst):
        copy = pltpu.make_async_copy(src, dst, self.sems.at[self.next])
        self.next += 1
        copy.start()
        return copy


def run_hooks(step, hooks):
    for n, actions in hooks.items():
        if not actions:
            continue

        @pl.when(step == n)
        def _():
            for action in actions:
                action()


def stage_norm1(sid, time, vecs, x, a1, a1t, hooks):
    gain, shift = vecs[0:1, :], vecs[1:2, :]

    @pl.loop(0, BLOCK // 128)
    def _(i):
        parts = []
        for half in range(2):
            s = sid[2 * i + half]
            live = (s >= 0).astype(F32)
            row = time[pl.ds(jnp.maximum(s, 0), 1), :]
            parts.append((x[rows_at(2 * i + half, SHORT), :] + row) * live)
        block = jnp.concatenate(parts, axis=0)
        at = rows_at(i, 128)
        x[at, :] = block
        n, _ = normalize(block)
        a = n * gain + shift
        a1[at, :] = a.astype(BF16)
        a1t[:, at] = a.T.astype(BF16)
        run_hooks(i, hooks)


def mask_rows(sid, i, groups):
    lane = lax.rem(lax.broadcasted_iota(jnp.int32, (SHORT, 128), 1), 64)
    mq, mk = [], []
    for g in range(groups):
        s = sid[groups * i + g]
        own = jnp.where(s >= 0, s, 16)
        mk.append((lane == own).astype(F32))
        bad = ((lane < 16) & (lane != s)) | (lane == 16)
        mq.append(jnp.where(bad, NEG, 0.0))
    return jnp.concatenate(mq, axis=0), jnp.concatenate(mk, axis=0)


def low_lanes(shape):
    return lax.broadcasted_iota(jnp.int32, shape, 1) < 64


def low_rows(shape):
    return lax.broadcasted_iota(jnp.int32, shape, 0) < 64


def stage_qkv(c, sid, vecs, a1, w, q0, q1, k0, k1, kt, v, vt0, vt1, hooks):
    lo = 256 * c

    @pl.loop(0, BLOCK // TB)
    def _(i):
        at = rows_at(i, TB)
        mq, mk = mask_rows(sid, i, TB // SHORT)
        acc = mm(a1[at, :], w)
        q = (acc[:, :256] + vecs[2:3, lo : lo + 256]).astype(BF16).astype(F32) * (HEAD_DIM**-0.5)
        k = acc[:, 256:512]
        value = acc[:, 512:] + vecs[3:4, lo : lo + 256]
        kt[lo : lo + 256, at] = k.T.astype(BF16)
        v[at, lo : lo + 256] = value.astype(BF16)
        value_t = value.T
        low, low_t = low_lanes((TB, 128)), low_rows((128, TB))
        for p in range(2):
            here = slice(128 * p, 128 * p + 128)
            to = slice(lo + 128 * p, lo + 128 * p + 128)
            q0[at, to] = jnp.where(low, q[:, here], mq).astype(BF16)
            q1[at, to] = jnp.where(low, mq, q[:, here]).astype(BF16)
            k0[at, to] = jnp.where(low, k[:, here], mk).astype(BF16)
            k1[at, to] = jnp.where(low, mk, k[:, here]).astype(BF16)
            vt0[to, at] = jnp.where(low_t, value_t[here, :], 1.0).astype(BF16)
            vt1[to, at] = jnp.where(low_t, 1.0, value_t[here, :]).astype(BF16)
        run_hooks(i, hooks)


QB = 256


STEPS = PAIRS * (BLOCK // QB)


def step_place(step):
    return rows_at(step // (BLOCK // QB), 128), rows_at(lax.rem(step, BLOCK // QB), QB)


def attention_scores(step, q0, q1, k0, k1, s_ref, m_ref):
    lanes, at = step_place(step)
    for h, (q, k) in enumerate(((q0, k0), (q1, k1))):
        scores = mm_t(k[:, lanes], q[at, lanes])
        s_ref[h] = scores
        m_ref[h : h + 1, :] = jnp.max(scores, axis=0, keepdims=True)


def attention_apply(step, s_ref, m_ref, vt0, vt1, o, ot, lse):
    lanes, at = step_place(step)
    outs = []
    for h, (vt, total_row) in enumerate(((vt0, 64), (vt1, 0))):
        top = m_ref[h : h + 1, :]
        e = jnp.exp(s_ref[h] - top).astype(BF16)
        res = mm(vt[lanes, :], e)
        total = res[total_row : total_row + 1, :]
        outs.append(res * (1.0 / total))
        lse[pl.ds(2 * (step // (BLOCK // QB)) + h, 1), at] = top + jnp.log(total)
    both = jnp.where(low_rows((128, QB)), outs[0], outs[1])
    ot[lanes, at] = both.astype(BF16)
    o[at, lanes] = both.T.astype(BF16)


def paired_steps(first, count, end, slots, ahead, apply, hooks):
    parity = [{n: a for n, a in hooks.items() if n % 2 == k} for k in range(2)]

    @pl.loop(0, count // 2)
    def _(i):
        for k in range(2):
            step = first + 2 * i + k
            ahead(jnp.minimum(step + 1, end - 1), slots[1 - k])
            apply(step, slots[k])
            run_hooks(step, parity[k])


SCHEDULE_A = {
    ("pre", 0): ("s.F0", "q.F0", "k.F0", "s.F1", "s.F3", "s.F2", "s.S0", "q.F1", "s.S1", "q.F3", "s.S3", "s.S2", "q.F2", "q.S0", "q.S1", "k.F1", "k.F3", "q.S3", "s.T", "q.S2", "k.F2", "k.S0", "v.F0", "s.L",),
    ("pre", 1): ("v.F1",),
    ("norm", 1): ("v.F3", "k.S1",),
    ("norm", 3): ("k.S3", "v.F2", "o.F0",),
    ("norm", 4): ("q.T",),
    ("norm", 5): ("o.F1",),
    ("norm", 6): ("k.S2",),
    ("q", -1): ("v.S0", "o.F3", "v.S1", "o.F2", "q.L",),
    ("q", 0): ("v.S3",),
    ("q", 2): ("v.S2", "i.F0",),
    ("q", 3): ("o.S0",),
    ("att", 0): ("k.T", "o.S1", "i.F1",),
    ("att", 2): ("o.S3",),
    ("att", 4): ("k.L", "v.T", "o.S2",),
    ("att", 6): ("i.F3",),
    ("k", 0): ("v.L",),
    ("k", 2): ("i.F2", "i.S0",),
    ("att", 9): ("o.T", "i.S1",),
    ("att", 13): ("o.L", "i.S3",),
    ("v", 0): ("i.S2",),
    ("att", 17): ("d.Z",),
    ("att", 21): ("i.T",),
    ("end", 0): ("i.L",),
}
SCHEDULE_B = {
    ("pre", 0): ("d.F0", "d.F1", "d.F3", "d.F2",),
    ("p1", 1): ("d.S0",),
    ("p1", 2): ("d.S1",),
    ("p1", 3): ("d.S3",),
    ("p1", 4): ("d.S2",),
    ("p1", 7): ("d.T",),
    ("gd", 1): ("d.L", "x.B",),
    ("gd", 2): ("y.B",),
    ("p2", 0): ("x.F", "y.F",),
    ("p2", 2): ("x.S",),
    ("p2", 4): ("y.S",),
    ("p2", 5): ("x.T",),
    ("p2", 6): ("y.T",),
    ("gi", 1): ("x.L",),
    ("end", 0): ("y.L",),
}
SCHEDULE_C = {
    ("pre", 0): ("z.B", "0.B", "1.B", "2.B", "3.B",),
    ("att", 0): ("z.F",),
    ("att", 1): ("o.B", "0.F",),
    ("att", 2): ("1.F", "2.F",),
    ("att", 3): ("z.S", "3.F", "o.F",),
    ("att", 5): ("0.S",),
    ("att", 7): ("1.S",),
    ("att", 8): ("2.S",),
    ("att", 9): ("a.B",),
    ("att", 11): ("z.T",),
    ("att", 12): ("a.F", "3.S",),
    ("att", 14): ("o.S",),
    ("gw", 1): ("0.T",),
    ("att", 16): ("z.L", "1.T",),
    ("att", 17): ("b.B", "2.T",),
    ("att", 18): ("a.S",),
    ("att", 20): ("b.F", "0.L", "3.T",),
    ("att", 21): ("o.T",),
    ("att", 22): ("a.T", "1.L",),
    ("att", 23): ("b.S",),
    ("gw", 2): ("2.L",),
    ("gw", 3): ("c.B",),
    ("ln", 0): ("3.L",),
    ("ln", 1): ("b.T", "c.F", "o.L",),
    ("ln", 3): ("a.L",),
    ("end", 0): ("c.S", "b.L", "c.T", "c.L",),
}


class Schedule:
    def __init__(self, table):
        self.table, self.units = table, {}

    def actions(self, seg, step):
        found = self.table.get((seg, step), ()) if self.units else ()
        return [functools.partial(self.units[a[0]].do, a[2:]) for a in found]

    def hooks(self, seg, first=0, last=24):
        return {n: self.actions(seg, n) for n in range(first, last) if self.actions(seg, n)}

    def run(self, seg, step, part=slice(None)):
        for action in self.actions(seg, step)[part]:
            action()


def kernel_a(linked, sid, hidden, time, *refs):
    if linked:
        own, refs = refs[:5], refs[5:]
        vecs, refs = refs[0], refs[1:]
    else:
        (vecs, *wq), refs = refs[:4], refs[4:]
    (x_h, a1t_h, q0_h, q1_h, k0_h, k1_h, v_h, kt_h, o_h, ot_h, lse), refs = refs[:11], refs[11:]
    if linked:
        full, refs = refs[:7], refs[7:]
        wq = full[1:4]
    (x, a1, a1t, q0, q1, k0, k1, v, kt, vt0, vt1, o, ot, w, s0, m0, s1, m1, sems), refs = refs[:19], refs[19:]
    mv = Mover(sems)
    cx = mv.start(hidden, x)
    plan = Schedule(SCHEDULE_A)
    if linked:
        staged, local_sems, send, recv = refs
        peers = Peers()
        links = Links(peers, send, recv)
        peers.greet()
        small, qkv, out, inn, down = own
        pieces = [View(small)] + [View(qkv, slice(None), pl.ds(D * n, D)) for n in range(3)] + [View(out), View(inn), View(down)]
        rows = (small.shape[0],) + 5 * (D // 32,) + (FF // 32,)
        for n, name in enumerate("sqkvoid"):
            kind = Line if name == "d" else Gather
            plan.units[name] = kind(n, links, pieces[n], rows[n], full[n], local_sems.at[n])
            plan.units[name].begin()
    run, hooks = plan.run, plan.hooks
    run("pre", 0)
    if linked:
        build_table(full[0], staged, local_sems.at[7], vecs)
    run("pre", 1)
    cx.wait()
    stage_norm1(sid, time, vecs, x, a1, a1t, hooks("norm"))
    outs = [mv.start(x, x_h), mv.start(a1t, a1t_h)]

    def weight(name, j):
        run(name, -1)
        copy = mv.start(wq[j], w.at[j])
        copy.wait()
        return w[j].reshape(D, D)

    slots = ((s0, m0), (s1, m1))

    def ahead(step, slot):
        attention_scores(step, q0, q1, k0, k1, *slot)

    def apply(step, slot):
        attention_apply(step, *slot, vt0, vt1, o, ot, lse)

    steps = STEPS // 3
    for c, name in enumerate("qkv"):
        stage_qkv(c, sid, vecs, a1, weight(name, c), q0, q1, k0, k1, kt, v, vt0, vt1, hooks(name))
        if c == 2:
            outs += [mv.start(a, b) for a, b in ((q0, q0_h), (q1, q1_h), (k0, k0_h), (k1, k1_h), (kt, kt_h), (v, v_h))]
        ahead(steps * c, slots[0])
        paired_steps(steps * c, steps, steps * (c + 1), slots, ahead, apply, plan.hooks("att", steps * c, steps * (c + 1)))
    outs += [mv.start(o, o_h), mv.start(ot, ot_h)]
    run("end", 0)
    for copy in outs:
        copy.wait()
    if linked:
        links.finish()


def sds(shape, dtype):
    return jax.ShapeDtypeStruct(shape, dtype)


TOK = (BLOCK, D)
TOKT = (D, BLOCK)


def vm(shape, dtype):
    return pltpu.VMEM(shape, dtype)


OUT_A = [sds(TOK, F32), sds(TOKT, BF16)] + [sds(TOK, BF16)] * 5 + [sds(TOKT, BF16), sds(TOK, BF16), sds(TOKT, BF16), sds((16, BLOCK), F32)]
SCRATCH_A = [vm(TOK, F32), vm(TOK, BF16), vm(TOKT, BF16)] + [vm(TOK, BF16)] * 5 + [vm(TOKT, BF16)] * 3 + [
    vm(TOK, BF16), vm(TOKT, BF16), vm((3, 4, D // 4, D), BF16)] + 2 * [vm((2, BLOCK, QB), F32), vm((8, QB), F32)] + [pltpu.SemaphoreType.DMA((16,))]


def call_a(sid, hidden, time, vecs, wq):
    return pl.pallas_call(
        functools.partial(kernel_a, False),
        name="part_a",
        out_shape=OUT_A,
        in_specs=[SMEM, ANY, VMEM, VMEM, ANY, ANY, ANY],
        out_specs=[ANY] * 10 + [VMEM],
        scratch_shapes=SCRATCH_A,
        compiler_params=pltpu.CompilerParams(vmem_limit_bytes=VMEM_LIMIT),
    )(sid, hidden, time, vecs, *[a.reshape(4, D // 4, D) for a in wq])


def call_a_links(sid, hidden, time, own):
    small, qkv, out, inn, down = own
    sizes = [small.shape] + [(D // 32, D)] * 4 + [inn.shape]
    slots = GATHER_SLOTS * 7
    res = pl.pallas_call(
        functools.partial(kernel_a, True),
        name="part_a",
        out_shape=[sds((16, D), F32)] + OUT_A + [sds((4, 8 * r, c), BF16) for r, c in sizes] + [sds((4, FF // 32, D), BF16)],
        in_specs=[SMEM, ANY, VMEM] + [VMEM] * 5,
        out_specs=[VMEM] + [ANY] * 10 + [VMEM] + [ANY] * 7,
        scratch_shapes=SCRATCH_A + [vm((4, 64, SMALL_LEN), BF16)] + [pltpu.SemaphoreType.DMA((n,)) for n in (8, slots, slots)],
        compiler_params=pltpu.CompilerParams(vmem_limit_bytes=VMEM_LIMIT, collective_id=1, has_side_effects=True),
    )(sid, hidden, time, *own)
    full = [a.reshape(-1, a.shape[-1]) for a in res[13:18]]
    return res[0], res[1:12], full[:3], full[3:], res[18]


def kernel_b(linked, sid, x_h, o_h, gout_h, vecs, wout_h, win_h, wdown_h,
             out_h, gx1_h, gb_h, go0_h, go1_h, dots, gdown_h, gin_h, sums, *refs):
    if linked:
        (gdown_o, down_f), refs = refs[:2], refs[2:]
    (x, o, gy, wout, win, wdown, gm, a2t, ht, h, gu, gb, go0, go1, stage_d, stage, *u_refs, sems), refs = refs[:19], refs[19:]
    plan = Schedule(SCHEDULE_B)
    if linked:
        bufs, (local_sems, send, recv) = refs[:14], refs[14:]
        peers = Peers()
        links = Links(peers, send, recv)
        peers.greet()
        plan.units["d"] = Plane(3, links, View(wdown_h), FF // 32, down_f, local_sems.at[3])
        for n, name in enumerate("xy"):
            keep = functools.partial(store_lanes, gdown_o, ((0, DT * n, DT),))
            plan.units[name] = Scatter(n, links, (gdown_h, n), keep, bufs[7 * n : 7 * n + 7], local_sems.at[n])
        plan.run("pre", 0)
    mv = Mover(sems)
    cx, co, cg = mv.start(x_h, x), mv.start(o_h, o), mv.start(gout_h, gy)
    cwo = mv.start(wout_h, wout)
    cwi = [mv.start(win_h.at[:, pl.ds(D * j, D)], win.at[j]) for j in range(4)]
    p1_hooks = [{n: plan.actions("p1", n) for n in range(k, 8, 2)} for k in range(2)]
    sums[...] = jnp.zeros_like(sums)
    for c in [cx, co, cg, cwo] + cwi:
        c.wait()
    lane = lax.broadcasted_iota(jnp.int32, (16, D), 1) // HEAD_DIM
    heads = (lane == lax.broadcasted_iota(jnp.int32, (16, D), 0)).astype(BF16)
    blocks = BLOCK // TB
    outs = []
    so = mv.sems

    def out_copies(i):
        at = rows_at(i, TB)
        return [pltpu.make_async_copy(x.at[at, :], out_h.at[at, :], so.at[24]),
                pltpu.make_async_copy(gy.at[at, :], gx1_h.at[at, :], so.at[25])]

    def live_rows(i):
        return jnp.concatenate(
            [jnp.full((SHORT, 1), (sid[(TB // SHORT) * i + g] >= 0).astype(F32), F32) for g in range(TB // SHORT)], axis=0)

    @pl.loop(0, blocks)
    def _(i):
        at = rows_at(i, TB)
        x1 = x[at, :] + mm(o[at, :], wout[...]) + vecs[4:5, :]
        x[at, :] = x1
        n2, _ = normalize(x1)
        a2f = n2 * vecs[5:6, :] + vecs[6:7, :]
        a2 = a2f.astype(BF16)
        a2t[:, at] = a2f.T.astype(BF16)
        gyb = gy[at, :] * live_rows(i)
        gy[at, :] = gyb
        gm[at, :] = gyb.astype(BF16)
        u_refs[0][...] = mm(a2, win[0]) + vecs[7:8, :]
        for j in range(4):
            if j < 3:
                u_refs[1 - j % 2][...] = mm(a2, win[j + 1]) + vecs[8 + j : 9 + j, :]
            hf, slope = gelu_parts(u_refs[j % 2][...])
            ht[D * j : D * j + D, at] = hf.T.astype(BF16)
            h[at, D * j : D * j + D] = hf.astype(BF16)
            gu[at, D * j : D * j + D] = slope.astype(BF16)
            if j % 2:
                run_hooks(2 * i + j // 2, p1_hooks[j // 2])

    pending = None
    for t in range(D // DT):
        if pending is not None:
            pending.wait()

        @pl.loop(0, FF // D)
        def _(r):
            part = mm(ht[rows_at(r, D), :], gm[:, DT * t : DT * t + DT]).astype(BF16)
            stage_d[r] = part.reshape(4, 192, DT)

        plan.run("gd", t)
        pending = pltpu.make_async_copy(stage_d, gdown_h.at[t], so.at[26])
        pending.start()
    pending.wait()
    plan.run("wd", 0)
    if linked:
        cwd = [mv.start(wdown_h, wdown.at[:, peers.f])]
        for n in range(1, 8):
            f = (peers.f + n) % 8
            cwd.append(mv.start(down_f.at[:, f], wdown.at[:, f]))
    else:
        cwd = [mv.start(wdown_h, wdown)]
    plan.run("wd", 1)
    for c in cwd:
        c.wait()
    first_hooks, second_hooks = ({n: plan.actions("p2", n) for n in range(k, 2 * blocks, 2)} for k in range(2))

    @pl.loop(0, blocks)
    def _(i):
        at = rows_at(i, TB)
        n2, r2 = normalize(x[at, :])
        gmb = gm[at, :]
        acc = x[at, :] + vecs[11:12, :]
        ga2 = jnp.zeros((TB, D), F32)
        for j in range(4):
            acc = acc + mm(h[at, D * j : D * j + D], wdown[j].reshape(D, D))
            guf = mm_t(gmb, wdown[j].reshape(D, D)) * gu[at, D * j : D * j + D].astype(F32)
            gub = guf.astype(BF16)
            gu[at, D * j : D * j + D] = gub
            sums[4 + j] += fold8(gub.astype(F32))
            ga2 = ga2 + mm_t(gub, win[j])
        x[at, :] = acc * live_rows(i)
        run_hooks(2 * i, first_hooks)
        gyb = gy[at, :]
        sums[8] += fold8(gmb.astype(F32))
        sums[2] += fold8(ga2 * n2)
        sums[3] += fold8(ga2)
        gx1 = gyb + norm_back(ga2, vecs[5:6, :], n2, r2)
        gy[at, :] = gx1
        for c in out_copies(i):
            c.start()
        gbb = gx1.astype(BF16)
        gb[at, :] = gbb
        sums[1] += fold8(gbb.astype(F32))
        go = mm_t(gbb, wout[...]).astype(BF16).astype(F32)
        prod = go * o[at, :].astype(F32)
        hi = prod.astype(BF16)
        lo = (prod - hi.astype(F32)).astype(BF16)
        dots[:, at] = mm_t(heads, hi) + mm_t(heads, lo)
        low = lax.rem(lax.broadcasted_iota(jnp.int32, (TB, D), 1), 128) < 64
        go0[at, :] = jnp.where(low, go, 0.0).astype(BF16)
        go1[at, :] = jnp.where(low, 0.0, go).astype(BF16)
        run_hooks(2 * i + 1, second_hooks)

    outs += [mv.start(gb, gb_h), mv.start(go0, go0_h), mv.start(go1, go1_h)]
    copies = []
    for j in range(4):
        if j > 1:
            copies[j - 2].wait()

        part = mm(a2t[...], gu[:, D * j : D * j + D]).astype(BF16)
        stage[j % 2] = part.reshape(4, 4, 48, D)
        plan.run("gi", j)
        copies.append(pltpu.make_async_copy(stage.at[j % 2], gin_h.at[j], so.at[27 + j % 2]))
        copies[j].start()
    plan.run("end", 0)
    for c in copies[2:] + outs:
        c.wait()
    for i in range(blocks):
        for c in out_copies(i):
            c.wait()
    if linked:
        links.finish()


DT = 256


def store_lanes(out, places, total):
    for source, target, width in places:
        out[:, target : target + width] = total[:, source : source + width]


def call_b(linked, sid, x, o, gout, vecs, wout, win, wdown):
    out = [sds(TOK, F32), sds(TOK, F32)] + [sds(TOK, BF16)] * 3 + [
        sds((16, BLOCK), F32), sds((D // DT, 4, 4, 192, DT), BF16), sds((4, 4, 4, 48, D), BF16), sds((9, 8, D), F32)]
    out_specs = [ANY] * 5 + [VMEM, ANY, ANY, VMEM]
    scratch = [vm(TOK, F32), vm(TOK, BF16), vm(TOK, F32), vm((D, D), BF16), vm((4, D, D), BF16), vm((4, 8, FF // 32, D), BF16),
               vm(TOK, BF16), vm(TOKT, BF16), vm((FF, BLOCK), BF16), vm((BLOCK, FF), BF16), vm((BLOCK, FF), BF16),
               vm(TOK, BF16), vm(TOK, BF16), vm(TOK, BF16), vm((4, 4, 192, DT), BF16), vm((2, 4, 4, 48, D), BF16), vm((TB, D), F32), vm((TB, D), F32), pltpu.SemaphoreType.DMA((29,))]
    extra = {}
    if linked:
        out += [sds((FF // 32, 2 * DT), F32), sds((4, 8, FF // 32, D), BF16)]
        out_specs += [VMEM, ANY]
        slots = 2 * SCATTER_SLOTS + GATHER_SLOTS
        scratch += 2 * scatter_bufs(FF // 32, DT) + [pltpu.SemaphoreType.DMA((n,)) for n in (4, slots, slots)]
        extra = dict(collective_id=2, has_side_effects=True)
    return pl.pallas_call(
        functools.partial(kernel_b, linked),
        name="part_b",
        out_shape=out,
        in_specs=[SMEM, ANY, ANY, ANY, VMEM, ANY, ANY, ANY],
        out_specs=out_specs,
        scratch_shapes=scratch,
        compiler_params=pltpu.CompilerParams(vmem_limit_bytes=VMEM_LIMIT, **extra),
    )(sid, x, o, gout, vecs, wout, win, wdown)


def attention_back_scores(step, q0, q1, k0, k1, v, go0, go1, lse, dots, p_ref, g_ref):
    lanes, at = step_place(step)
    row = 2 * (step // (BLOCK // QB))
    vv = v[:, lanes]
    for h, (q, k, go) in enumerate(((q0, k0, go0), (q1, k1, go1))):
        scores = mm_t(k[:, lanes], q[at, lanes])
        p = jnp.exp(scores - lse[pl.ds(row + h, 1), at])
        gp = mm_t(vv, go[at, lanes])
        g_ref[h] = (p * (gp - dots[pl.ds(row + h, 1), at])).astype(BF16)
        p_ref[h] = p.astype(BF16)


def attention_back_apply(step, p_ref, g_ref, q0, q1, kt, go0, go1, gk_acc, gv_acc, gqkv):
    lanes, at = step_place(step)
    part = lax.rem(step, BLOCK // QB)
    gk_parts, gq_parts, gv_parts = [], [], []
    for h, (q, go) in enumerate(((q0, go0), (q1, go1))):
        gv_parts.append(mm(p_ref[h], go[at, lanes]))
        gk_parts.append(mm(g_ref[h], q[at, lanes]))
        gq_parts.append(mm(kt[lanes, :], g_ref[h]))
    gk = jnp.where(low_lanes((BLOCK, 128)), gk_parts[0], gk_parts[1])
    gv = gv_parts[0] + gv_parts[1]
    gq = jnp.where(low_rows((128, QB)), gq_parts[0], gq_parts[1]) * (HEAD_DIM**-0.5)
    gqkv[0, at, lanes] = gq.T.astype(BF16)
    first = part == 0
    gk_acc[...] = jnp.where(first, gk, gk_acc[...] + gk)
    gv_acc[...] = jnp.where(first, gv, gv_acc[...] + gv)

    @pl.when(part == BLOCK // QB - 1)
    def _():
        gqkv[1, :, lanes] = gk_acc[...].astype(BF16)
        gqkv[2, :, lanes] = gv_acc[...].astype(BF16)


UNITS_C = "0123oabcz"


def kernel_c(linked, sid, x_h, a1t_h, q0_h, q1_h, k0_h, k1_h, v_h, kt_h, ot_h, lse, gx1_h, gb_h, go0_h, go1_h, dots, vecs, w0_h, w1_h, w2_h, *refs):
    if linked:
        (gin_h, sums_b, gdown_h, down_part), refs = refs[:4], refs[4:]
    (ig_h, tg, gqkv_h, gwo_h, sums), refs = refs[:5], refs[5:]
    if linked:
        (gin_o, gout_o, gqkv_o, small_o, gdown_o), refs = refs[:5], refs[5:]
    (x, a1t, q0, q1, k0, k1, v, kt, ot, gx1, gb, go0, go1, w, gqkv, gk_acc, gv_acc, gw, gwo, tsum, p0, g0, p1, g1, sems), refs = refs[:25], refs[25:]
    plan = Schedule(SCHEDULE_C)
    if linked:
        bufs, (value, small_b, local_sems, send, recv) = refs[:63], refs[63:]
        peers = Peers()
        links = Links(peers, send, recv)
        peers.greet()
        third = D // 3
        for n, name in enumerate(UNITS_C):
            if n < 4:
                parts, keep = (gin_h, n), functools.partial(store_lanes, gin_o, ((0, D * n, D),))
            elif n == 4:
                parts, keep = (gwo_h,), functools.partial(store_lanes, gout_o, ((0, 0, D),))
            elif n == 8:
                parts, keep = (gdown_h, 2), functools.partial(store_lanes, gdown_o, ((0, 2 * DT, DT),))
            else:
                places = tuple((third * m, D * m + third * (n - 5), third) for m in range(3))
                parts, keep = (gqkv_h, n - 5), functools.partial(store_lanes, gqkv_o, places)
            plan.units[name] = Scatter(n, links, parts, keep, bufs[7 * n : 7 * n + 7], local_sems.at[n])
        plan.run("pre", 0)
        gdown_o[:, : 2 * DT] = down_part[...]
    mv = Mover(sems)
    early = [mv.start(s, d) for s, d in ((ot_h, ot), (gb_h, gb), (q0_h, q0), (q1_h, q1), (k0_h, k0), (k1_h, k1), (v_h, v), (kt_h, kt), (go0_h, go0), (go1_h, go1))]
    for c in early[:2]:
        c.wait()
    sums[...] = jnp.zeros_like(sums)

    @pl.loop(0, 2)
    def _(r):
        gwo[pl.ds(2 * r, 2)] = mm(ot[rows_at(r, 384), :], gb[...]).astype(BF16).reshape(2, 4, 48, D)

    gwo_copy = mv.start(gwo, gwo_h)
    for c in early[2:]:
        c.wait()
    late = [mv.start(a1t_h, a1t), mv.start(x_h, x), mv.start(gx1_h, gx1)]
    late += [mv.start(part.at[:, pl.ds(256 * j, 256)], w.at[j, :, pl.ds(256 * n, 256)]) for n, part in enumerate((w0_h, w1_h, w2_h)) for j in range(3)]
    gwo_copy.wait()
    plan.run("gwo", 0)
    steps = 2 * (BLOCK // QB)
    slots = ((p0, g0), (p1, g1))

    def ahead(step, slot):
        attention_back_scores(step, q0, q1, k0, k1, v, go0, go1, lse, dots, *slot)

    def apply(step, slot):
        attention_back_apply(step, *slot, q0, q1, kt, go0, go1, gk_acc, gv_acc, gqkv)

    ahead(0, slots[0])
    step_hooks, chunk_hooks = plan.hooks("att"), plan.hooks("gw", 0, 3)

    @pl.loop(0, 3)
    def _(chunk):
        paired_steps(steps * chunk, steps, STEPS, slots, ahead, apply, step_hooks)
        pl.when(chunk == 0)(late[0].wait)
        for j in range(3):
            for r in range(2):
                part = mm(a1t[384 * r : 384 * r + 384, :], gqkv[j, :, rows_at(chunk, 256)]).astype(BF16)
                gw[chunk, 2 * r : 2 * r + 2, :, :, 256 * j : 256 * j + 256] = part.reshape(2, 4, 48, 256)
        copy = pltpu.make_async_copy(gw.at[chunk], gqkv_h.at[chunk], sems.at[31])
        copy.start()
        run_hooks(chunk, chunk_hooks)
        copy.wait()

    for c in late[1:]:
        c.wait()
    plan.run("gw", 3)
    gain = vecs[0:1, :]
    ln_hooks = plan.hooks("ln")

    @pl.loop(0, BLOCK // TB)
    def _(i):
        at = rows_at(i, TB)
        ga1 = mm_t(gqkv[0, at, :], w[0]) + mm_t(gqkv[1, at, :], w[1]) + mm_t(gqkv[2, at, :], w[2])
        sums[2] += fold8(gqkv[0, at, :].astype(F32))
        sums[3] += fold8(gqkv[2, at, :].astype(F32))
        n1, r1 = normalize(x[at, :])
        sums[0] += fold8(ga1 * n1)
        sums[1] += fold8(ga1)
        total = gx1[at, :] + norm_back(ga1, gain, n1, r1)
        for g in range(TB // SHORT):
            s = sid[(TB // SHORT) * i + g]
            live = (s >= 0).astype(F32)
            part = total[SHORT * g : SHORT * g + SHORT, :] * live
            x[rows_at((TB // SHORT) * i + g, SHORT), :] = part
            tsum[pl.ds((TB // SHORT) * i + g, 1), :] = jnp.sum(part, axis=0, keepdims=True)
        run_hooks(i, ln_hooks)

    ig_copy = mv.start(x, ig_h)
    if linked:
        pick = lambda ref, n: jnp.sum(ref[n], axis=0, keepdims=True)
        rows = [pick(sums, n) for n in range(4)] + [pick(sums_b, n) for n in range(1, 9)] + [jnp.zeros((4, D), F32)]
        value[0] = jnp.concatenate(rows, axis=0)
        small = SmallSum(links, value, small_b)
        small.send(0, "p")
    row = lax.broadcasted_iota(jnp.int32, (GROUPS, D), 0)
    acc = jnp.zeros((GROUPS, D), F32)
    for g in range(GROUPS):
        acc = acc + jnp.where(row == sid[g], tsum[g : g + 1, :], 0.0)
    tg[...] = acc
    if linked:
        small.take(0)
        small.send(1, "x")
        small.take(1)
        small.send(2, "y")
        plan.run("end", 0, slice(0, -1))
        small.take(2)
        small.spread()
        row, col = small_places(peers.dev)
        select = small_select(col).astype(BF16)
        plan.run("end", 0, slice(-1, None))
        left, picked = small.total(), 0.0
        for _ in range(3):
            part = left.astype(BF16)
            picked = picked + mm(part, select)
            left = left - part.astype(F32)
        at_row = lax.broadcasted_iota(jnp.int32, (16, SMALL_LEN), 0) == row
        small_o[...] = jnp.sum(jnp.where(at_row, picked, 0.0), axis=0, keepdims=True)
        links.finish()
    ig_copy.wait()


def call_c(linked, *args):
    out = [sds(TOK, F32), sds((GROUPS, D), F32), sds((3, 4, 4, 48, D), BF16), sds((4, 4, 48, D), BF16), sds((4, 8, D), F32)]
    in_specs = [SMEM] + [ANY] * 9 + [VMEM] + [ANY] * 4 + [VMEM, VMEM, ANY, ANY, ANY]
    out_specs = [ANY, VMEM, ANY, ANY, VMEM]
    scratch = [vm(TOK, F32), vm(TOKT, BF16)] + [vm(TOK, BF16)] * 5 + [vm(TOKT, BF16)] * 2 + [vm(TOK, F32)] + [vm(TOK, BF16)] * 3
    scratch += [vm((3, D, D), BF16), vm((3, BLOCK, D), BF16), vm((BLOCK, 128), F32), vm((BLOCK, 128), F32), vm((3, 4, 4, 48, D), BF16), vm((4, 4, 48, D), BF16),
                vm((GROUPS, D), F32)] + 4 * [vm((2, BLOCK, QB), BF16)] + [pltpu.SemaphoreType.DMA((32,))]
    extra = {}
    if linked:
        in_specs += [ANY, VMEM, ANY, VMEM]
        out += [sds((D // 32, n * D), F32) for n in (4, 1, 3)] + [sds((1, SMALL_LEN), F32), sds((FF // 32, D), F32)]
        out_specs += [VMEM] * 5
        units = len(UNITS_C)
        slots = SCATTER_SLOTS * units + 6
        scratch += (units - 1) * scatter_bufs(D // 32, D) + scatter_bufs(FF // 32, DT) + [vm((4, 16, D), F32), vm((6, 16, D), F32)]
        scratch += [pltpu.SemaphoreType.DMA((n,)) for n in (units, slots, slots)]
        extra = dict(collective_id=3, has_side_effects=True)
    return pl.pallas_call(
        functools.partial(kernel_c, linked),
        name="part_c",
        out_shape=out,
        in_specs=in_specs,
        out_specs=out_specs,
        scratch_shapes=scratch,
        compiler_params=pltpu.CompilerParams(vmem_limit_bytes=VMEM_LIMIT, **extra),
    )(*args)


AXES = ("dp", "fsdp")
MESH = pl.DeviceIdType.MESH
SMALL = ((0, 24, 0), (24, 24, 1), (48, 24, 4), (72, 24, 5), (96, 24, 6), (120, 24, 11), (144, 48, 2), (192, 96, 7))
SMALL_ORDER = (0, 1, 3, 4, 5, 7, 2, 6)
SMALL_LEN = 384


class Peers:
    def __init__(self):
        self.z, self.f = lax.axis_index("dp"), lax.axis_index("fsdp")
        self.c = self.f % 2
        self.yx = self.f // 2
        x, y = self.yx % 2, self.yx // 2
        self.partner = self.f + 1 - 2 * self.c
        self.fx, self.fy = self.f + 2 - 4 * x, self.f + 4 - 8 * y
        self.fd = self.fx + 4 - 8 * y
        self.qx, self.qy, self.qd = self.fx // 2, self.fy // 2, self.fd // 2
        self.dev = self.z * 8 + self.f
        self.other = 1 - self.c
        self.ups = [(self.z + d) % 4 for d in range(4)]

    def up(self, d):
        return self.ups[d]

    def at(self, name, d=0):
        if name == "z":
            return (self.up(d), self.f)
        return (self.z, {"x": self.fx, "y": self.fy, "p": self.partner}[name])

    def greet(self):
        barrier = pltpu.get_barrier_semaphore()
        for target in [self.at("p"), self.at("x"), self.at("y")] + [self.at("z", d) for d in (1, 2, 3)]:
            pl.semaphore_signal(barrier, inc=1, device_id=target, device_id_type=MESH)
        pl.semaphore_wait(barrier, 6)


class View:
    def __init__(self, ref, *index):
        self.ref, self.index = ref, index

    def get(self):
        return self.ref.at[self.index] if self.index else self.ref


class Links:
    def __init__(self, peers, send, recv):
        self.peers, self.send, self.recv = peers, send, recv
        self.slots, self.sent = {}, []

    def copy(self, key, src, dst, target):
        n = self.slots.setdefault(key, len(self.slots))
        return pltpu.make_async_remote_copy(
            src_ref=src.get(), dst_ref=dst.get(), send_sem=self.send.at[n], recv_sem=self.recv.at[n],
            device_id=target, device_id_type=MESH)

    def start(self, key, src, dst, name, d=0):
        args = (key, src, dst, self.peers.at(name, d))
        self.copy(*args).start()
        self.sent.append(args)

    def arrived(self, key, dst):
        self.copy(key, dst, dst, self.peers.at("p")).wait_recv()

    def finish(self):
        for args in self.sent:
            self.copy(*args).wait_send()
        self.sent = []


GATHER_SLOTS = 19


class Gather:
    def __init__(self, name, links, own, rows, full, sem):
        self.name, self.links, self.own, self.rows, self.full, self.sem = name, links, own, rows, full, sem
        p, self.deep = links.peers, len(full.shape) == 4
        place = (lambda f: f) if self.deep else (lambda f: pl.multiple_of(f * self.rows, 8))
        self.at = {n: place(f) for n, f in (("f", p.f), ("x", p.fx), ("y", p.fy), ("d", p.fd))}
        self.across = {n: place(f + 1 - 2 * p.c)
                       for n, f in (("f", p.f), ("x", p.fx), ("y", p.fy), ("d", p.fd))}

    def key(self, *k):
        return (self.name,) + k

    def piece(self, d, n):
        return View(self.full, self.links.peers.up((4 - d) % 4), self.window(self.at[n]))

    def column(self, at):
        return View(self.full, slice(None), self.window(at))

    def window(self, at):
        return at if self.deep else pl.ds(at, self.rows)

    def begin(self):
        here = self.piece(0, "f")
        for d in (1, 3, 2):
            self.links.start(self.key("z", d), self.own, here, "z", d)
        self.local_copy().start()

    def local_copy(self):
        return pltpu.make_async_copy(self.own.get(), self.piece(0, "f").get(), self.sem)

    def do(self, action):
        links, kind, d = self.links, action[0], int(action[1:] or 0)
        if kind == "F":
            piece = self.piece(d, "f")
            if d:
                links.arrived(self.key("z", d), piece)
            src = piece if d else self.own
            links.start(self.key("x", d), src, piece, "x")
            links.start(self.key("y", d), src, piece, "y")
            if d == 2:
                self.local_copy().wait()
                mine = self.column(self.at["f"])
                links.start(self.key("p", "f"), mine, mine, "p")
        elif kind == "S":
            px, py = self.piece(d, "x"), self.piece(d, "y")
            links.arrived(self.key("x", d), px)
            links.arrived(self.key("y", d), py)
            via, part = ("y", px) if d < 2 else ("x", py)
            links.start(self.key("d", d), part, part, via)
            if d == 2:
                for n in ("x", "y"):
                    part = self.column(self.at[n])
                    links.start(self.key("p", n), part, part, "p")
        elif kind == "T":
            for n in range(4):
                links.arrived(self.key("d", n), self.piece(n, "d"))
            part = self.column(self.at["d"])
            links.start(self.key("p", "d"), part, part, "p")
        else:
            for n in ("f", "x", "y", "d"):
                links.arrived(self.key("p", n), self.column(self.across[n]))


class Line(Gather):
    def piece(self, d, n):
        return View(self.full, self.links.peers.up((4 - d) % 4))

    def do(self, action):
        for d in (1, 2, 3):
            self.links.arrived(self.key("z", d), self.piece(d, "f"))
        self.local_copy().wait()


class Plane(Gather):
    def mine(self, d):
        return View(self.own.ref, self.links.peers.up((4 - d) % 4))

    def do(self, action):
        if action[0] != "F":
            return Gather.do(self, action)
        d = int(action[1:])
        for name in ("x", "y"):
            self.links.start(self.key(name, d), self.mine(d), self.piece(d, "f"), name)
        if d == 2:
            self.links.start(self.key("p", "f"), self.own, self.column(self.at["f"]), "p")


SCATTER_SLOTS = 10


class Scatter:
    def __init__(self, name, links, parts, keep, bufs, sem):
        self.name, self.links, self.parts, self.keep, self.sem = name, links, parts, keep, sem
        self.t, self.p, self.dx, self.dy, self.xr, self.yr, self.zr = bufs
        p, self.rows = links.peers, self.t.shape[2]
        self.here, self.there = (pl.multiple_of(c * self.rows, 8) for c in (p.c, p.other))

    def half(self, at):
        return View(self.parts[0], *self.parts[1:], slice(None), slice(None), pl.ds(at, self.rows))

    def do(self, action):
        {"B": self.begin, "F": self.first, "S": self.second, "T": self.third, "L": self.last}[action]()

    def key(self, *k):
        return (self.name,) + k

    def begin(self):
        p = self.links.peers
        self.links.start(self.key("p"), self.half(self.there), View(self.p), "p")
        self.local_copy().start()

    def local_copy(self):
        return pltpu.make_async_copy(self.half(self.here).get(), self.t, self.sem)

    def add(self, q, zs, ref, base=0):
        t = self.t

        @pl.loop(zs[0], zs[1])
        def _(i):
            t[i, q] = (t[i, q].astype(F32) + ref(i - base).astype(F32)).astype(BF16)

    def first(self):
        p, links, t = self.links.peers, self.links, self.t
        self.local_copy().wait()
        links.arrived(self.key("p"), View(self.p))
        self.add(p.qd, (0, 4), lambda i: self.p[i, p.qd])
        links.start(self.key("dx"), View(t, pl.ds(0, 2), p.qd), View(self.dx), "x")
        links.start(self.key("dy"), View(t, pl.ds(2, 2), p.qd), View(self.dy), "y")
        self.add(p.qx, (0, 4), lambda i: self.p[i, p.qx])
        links.start(self.key("x", 0), View(t, pl.ds(0, 2), p.qx), View(self.xr, pl.ds(0, 2)), "x")
        self.add(p.qy, (0, 4), lambda i: self.p[i, p.qy])
        links.start(self.key("y", 1), View(t, pl.ds(2, 2), p.qy), View(self.yr, pl.ds(2, 2)), "y")
        self.add(p.yx, (0, 4), lambda i: self.p[i, p.yx])

    def second(self):
        p, links, t = self.links.peers, self.links, self.t
        links.arrived(self.key("dy"), View(self.dy))
        self.add(p.qx, (2, 4), lambda i: self.dy[i], 2)
        links.start(self.key("x", 1), View(t, pl.ds(2, 2), p.qx), View(self.xr, pl.ds(2, 2)), "x")
        links.arrived(self.key("dx"), View(self.dx))
        self.add(p.qy, (0, 2), lambda i: self.dx[i])
        links.start(self.key("y", 0), View(t, pl.ds(0, 2), p.qy), View(self.yr, pl.ds(0, 2)), "y")

    def third(self):
        p, links, t = self.links.peers, self.links, self.t
        for n in range(2):
            links.arrived(self.key("x", n), View(self.xr, pl.ds(2 * n, 2)))
            links.arrived(self.key("y", n), View(self.yr, pl.ds(2 * n, 2)))

        @pl.loop(0, 4)
        def _(i):
            t[i, p.yx] = (t[i, p.yx].astype(F32) + self.xr[i].astype(F32) + self.yr[i].astype(F32)).astype(BF16)

        for d in (2, 1, 3):
            links.start(self.key("z", d), View(t, p.up(d), p.yx), View(self.zr, d - 1), "z", d)

    def last(self):
        p, links = self.links.peers, self.links
        for d in (1, 2, 3):
            links.arrived(self.key("z", d), View(self.zr, d - 1))
        total = self.t[p.z, p.yx].astype(F32)
        for n in range(3):
            total = total + self.zr[n].astype(F32)
        self.keep(total)


def scatter_bufs(rows, cols):
    return [pltpu.VMEM(lead + (rows, cols), BF16) for lead in ((4, 4), (4, 4), (2,), (2,), (4,), (4,), (3,))]


class SmallSum:
    def __init__(self, links, value, bufs):
        self.links, self.value, self.bufs = links, value, bufs

    def send(self, n, name):
        self.links.start(("s", n), View(self.value, n), View(self.bufs, n), name)

    def take(self, n):
        self.links.arrived(("s", n), View(self.bufs, n))
        self.value[n + 1] = self.value[n] + self.bufs[n]

    def spread(self):
        for d in (1, 2, 3):
            self.links.start(("s", 2 + d), View(self.value, 3), View(self.bufs, 2 + d), "z", d)

    def total(self):
        for d in (1, 2, 3):
            self.links.arrived(("s", 2 + d), View(self.bufs, 2 + d))
        return self.value[3] + self.bufs[3] + self.bufs[4] + self.bufs[5]


def small_places(dev):
    i = lax.broadcasted_iota(jnp.int32, (1, SMALL_LEN), 1)
    row, col = jnp.full((1, SMALL_LEN), 15, jnp.int32), jnp.full((1, SMALL_LEN), -1, jnp.int32)
    for start, n, base in SMALL:
        here = (i >= start) & (i < start + n)
        row = jnp.where(here, base + (dev * n) // D, row)
        col = jnp.where(here, (dev * n) % D + i - start, col)
    return row, col


def small_select(col):
    return (lax.broadcasted_iota(jnp.int32, (D, SMALL_LEN), 0) == col).astype(F32)


def kernel_prep(small, wqkv, wout, win, wdown, small_o, qkv_o, out_o, in_o, down_o):
    small_o[...] = jnp.broadcast_to(small[...], (8, SMALL_LEN)).astype(BF16)
    for c in range(3):
        for j in range(3):
            qkv_o[:, D * c + 256 * j : D * c + 256 * j + 256] = wqkv[:, D * j + 256 * c : D * j + 256 * c + 256].astype(BF16)
    out_o[...] = wout[...].astype(BF16)
    in_o[...] = win[...].astype(BF16)
    down_o[...] = wdown[...].astype(BF16)


def call_prep(small, weights):
    return pl.pallas_call(
        kernel_prep, name="prep",
        out_shape=[sds((8, SMALL_LEN), BF16)] + [sds(w.shape, BF16) for w in weights],
        in_specs=[VMEM] * 5, out_specs=[VMEM] * 5,
    )(small, *weights)


def build_table(gathered, staged, sem, vecs):
    copy = pltpu.make_async_copy(gathered, staged, sem)
    copy.start()
    copy.wait()
    rows = staged[...].reshape(256, SMALL_LEN).astype(F32).T
    r = lax.broadcasted_iota(jnp.int32, (256, D), 0)
    lane = lax.broadcasted_iota(jnp.int32, (1, D), 1)
    vecs[...] = jnp.zeros_like(vecs)
    for n in (24, 48, 96):
        part = [(start, base) for start, size, base in SMALL if size == n]
        values = rows[part[0][0] : part[-1][0] + n, :].astype(BF16)
        own = lax.broadcasted_iota(jnp.int32, (n, D), 0) == lax.rem(lane, n)
        first = (lane // n) * 8
        for line in range(n // 24):
            spread = mm(values, (r == first + 8 * line * (D // n)).astype(BF16))
            for m, (_, base) in enumerate(part):
                picked = jnp.where(own, spread[n * m : n * m + n, :], 0.0)
                vecs[base + line : base + line + 1, :] = jnp.sum(picked, axis=0, keepdims=True)


def gather_all(a):
    return lax.all_gather(a.astype(BF16), AXES, axis=0, tiled=True)


def scatter_sum(a):
    return lax.psum_scatter(a, AXES, scatter_dimension=0, tiled=True)


def split_small(row, small):
    parts, at = [], 0
    for s in small:
        parts.append(row[at : at + s.shape[0]])
        at += s.shape[0]
    return parts


def gather_plain(small, weights):
    every = lax.all_gather(jnp.concatenate([s.astype(BF16) for s in small]), AXES, axis=0, tiled=False)
    vecs, at = [], 0
    for s in small:
        vecs.append(every[:, at : at + s.shape[0]].reshape(-1, D))
        at += s.shape[0]
    vecs = jnp.concatenate(vecs + [jnp.zeros((4, D), BF16)], axis=0).astype(F32)
    return vecs, [gather_all(w) for w in weights]


def scatter_plain(sums_b, sums_c, grads, small):
    sb, sc = jnp.sum(sums_b, axis=1), jnp.sum(sums_c, axis=1)
    vectors = (sc[0], sc[1], sc[2:4].reshape(-1), sb[1], sb[2], sb[3], sb[4:8].reshape(-1), sb[8])
    devices = D // small[0].shape[0]
    packed = jnp.concatenate([g.reshape(devices, -1) for g in vectors], axis=1)
    return scatter_sum(packed).reshape(-1), [scatter_sum(g.astype(F32)) for g in grads]


def local(
    own_links,
    hidden_in, time_embed, seg_ids, pre_gain, pre_shift, qkv_weight, qv_bias, out_weight, out_bias,
    mid_gain, mid_shift, in_weight, in_bias, down_weight, down_bias, grad_out,
):
    sid = seg_ids.reshape(GROUPS, SHORT)[:, 0]
    small = (pre_gain, pre_shift, qv_bias, out_bias, mid_gain, mid_shift, in_bias, down_bias)
    weights = (qkv_weight, out_weight, in_weight, down_weight)
    if own_links:
        ordered = tuple(small[n] for n in SMALL_ORDER)
        row = jnp.concatenate(ordered + (jnp.zeros((SMALL_LEN - 288,), F32),)).reshape(1, SMALL_LEN)
        own = call_prep(row, weights)
        vecs, made, wq, (wout, win), wdown = call_a_links(sid, hidden_in, time_embed, own)
    else:
        vecs, (wqkv, wout, win, wdown) = gather_plain(small, weights)
        wq = list(wqkv.reshape(D, 3, 3, 256).transpose(2, 0, 1, 3).reshape(3, D, D))
        wdown = wdown.reshape(4, 8, FF // 32, D)
        made = call_a(sid, hidden_in, time_embed, vecs, wq)
    x, a1t, q0, q1, k0, k1, v, kt, o, ot, lse = made
    block_out, gx1, gb, go0, go1, dots, gdown, gin, sums_b, *more = call_b(own_links, sid, x, o, grad_out, vecs, wout, win, wdown)
    args_c = (sid, x, a1t, q0, q1, k0, k1, v, kt, ot, lse, gx1, gb, go0, go1, dots, vecs, *wq)
    if own_links:
        input_grad, time_grad, _, _, _, gin, gout, gqkv, mine, gdown = call_c(True, *args_c, gin, sums_b, gdown, more[0])
        parts = split_small(mine.reshape(-1), ordered)
        parts = [parts[SMALL_ORDER.index(n)] for n in range(8)]
    else:
        input_grad, time_grad, gqkv, gout, sums_c = call_c(False, *args_c)
        gdown = gdown.reshape(D // DT, FF, DT).transpose(1, 0, 2).reshape(FF, D)
        gin = gin.reshape(4, D, D).transpose(1, 0, 2).reshape(D, FF)
        gqkv = gqkv.reshape(3, D, 3, D // 3).transpose(1, 2, 0, 3).reshape(D, 3 * D)
        mine, (gdown, gin, gout, gqkv) = scatter_plain(sums_b, sums_c, (gdown, gin, gout.reshape(D, D), gqkv), small)
        parts = split_small(mine, small)
    gpg, gps, gqvb, gob, gmg, gms, gib, gdb = parts
    return (block_out, input_grad, time_grad, gpg, gps, gqkv, gqvb, gout, gob, gmg, gms, gin, gib, gdown, gdb)


def solution(mesh):
    rows, flat = P(AXES, None), P(AXES)
    own_links = dict(mesh.shape) == {"dp": 4, "fsdp": 8}
    return jax.shard_map(
        functools.partial(local, own_links),
        mesh=mesh,
        in_specs=(rows, rows, flat, flat, flat, rows, flat, rows, flat, flat, flat, rows, flat, rows, flat, rows),
        out_specs=(rows, rows, rows, flat, flat, rows, flat, rows, flat, flat, flat, rows, flat, rows, flat),
        check_vma=False,
    )
```
